32 devices in a mesh: panel: 2 (over core), lat: 4 (over y, x), lon: 4 (over z).
Axes of the slice: x: 2, y: 2, z: 4, core: 2. Of those that a mesh axis runs over, the one named last changes fastest.
Arguments:
- mass_per_volume: float32 [2, 16, 128, 1536], P('panel', None, 'lat', 'lon'), may hold values from 0.5 to 2
- flow_speed: float32 [2, 3, 16, 128, 1536], P('panel', None, None, 'lat', 'lon'), may hold values from -3 to 3
- heat_measure: float32 [2, 16, 128, 1536], P('panel', None, 'lat', 'lon'), may hold values from 0.5 to 2
- fields_at_outset: float32 [2, 5, 16, 128, 1536], P('panel', None, None, 'lat', 'lon'), may hold values from -6 to 6
- opposite_block: int32 [2, 4, 4, 1664], P('panel', 'lat', 'lon'), may hold values from 0 to 3, as said below
- donor_lower_corner: int32 [2, 4, 4, 1664], P('panel', 'lat', 'lon'), may hold values from 0 to 11902, as said below
- blend_factors: float32 [2, 4, 4, 4, 1664], P('panel', 'lat', 'lon'), may hold values from 0 to 1, as said below
- frame_turning: float32 [2, 4, 4, 2, 1664], P('panel', 'lat', 'lon'), may hold values from -1 to 1, as said below
Outputs:
- section_rate: float32 [2, 5, 16, 128, 1536], P('panel', None, None, 'lat', 'lon')
- new_state: float32 [2, 5, 16, 128, 1536], P('panel', None, None, 'lat', 'lon')
The draws below stay inside these ranges and needn't reach their ends.
Inputs may be any that keep to these rules, and one draw needn't show every extreme that they name: `opposite_block`: within each side of a block's slots (768, 768, 64, 64 slots), the slots fall into 4 runs of equal length in order, and the runs name different partners. `donor_lower_corner`: the source corners i, i + 1 and j, j + 1 lie inside the partner block. `blend_factors`: Nonnegative, summing to one over the four corners. `frame_turning`: cosine and sine of one angle.
All inputs are finite; a program needn't handle non-finite values.
Results may differ from the reference program's by a relative error of at most 0.0003.
Values sent between devices are 32-bit elements; how exact they have to be, the bound alone decides.
No kernel may reach another device: no remote copies, remote signals or barrier semaphores. Data moves between devices by JAX's collectives and lax.ppermute only.
A program may use at most 128 MiB of HBM per device.

```python
import math
import jax
import jax.numpy as jnp
from jax import lax

CLAT = 32
CLON = 384
DEPTH_STRATA = 16
LAT_BLOCKS = 4
LON_BLOCKS = 4
MESH_HEIGHT = 128
MESH_WIDTH = 1536
SLOTS = 1664


def draw_opposite_block(key, part):
    shifts = jax.random.randint(key, (2, LAT_BLOCKS, LON_BLOCKS, 4), 0, LAT_BLOCKS)
    index = jnp.arange(SLOTS, dtype=jnp.int32)
    lat_len = 2 * CLON
    lon_len = 2 * CLAT
    side = jnp.where(index < lat_len, 0, jnp.where(index < 2 * lat_len, 1, jnp.where(index < 2 * lat_len + lon_len, 2, 3)))
    starts = jnp.array([0, lat_len, 2 * lat_len, 2 * lat_len + lon_len], jnp.int32)[side]
    run_len = jnp.where(side < 2, lat_len // LAT_BLOCKS, lon_len // LAT_BLOCKS)
    run_index = (index - starts) // run_len
    picked = jnp.take(shifts, side, axis=3)
    return ((run_index + picked) % LAT_BLOCKS).astype(jnp.int32)


def draw_donor_lower_corner(key, part):
    key_rows, key_cols = jax.random.split(jax.random.fold_in(key, 7))
    shape = (2, LAT_BLOCKS, LON_BLOCKS, SLOTS)
    rows_in = jax.random.randint(key_rows, shape, 0, CLAT - 1)
    cols_in = jax.random.randint(key_cols, shape, 0, CLON - 1)
    cells = rows_in * CLON + cols_in
    cells = cells.at[:, :, :, 0].set(0)
    cells = cells.at[:, :, :, SLOTS - 1].set(CLAT * CLON - CLON - 2)
    return cells.astype(jnp.int32)


def draw_blend_factors(key, part):
    key_lat, key_lon = jax.random.split(jax.random.fold_in(key, 11))
    shape = (2, LAT_BLOCKS, LON_BLOCKS, SLOTS)
    frac_lat = jax.random.uniform(key_lat, shape, jnp.float32)
    frac_lon = jax.random.uniform(key_lon, shape, jnp.float32)
    stacked = jnp.stack([(1.0 - frac_lat) * (1.0 - frac_lon), frac_lat * (1.0 - frac_lon), (1.0 - frac_lat) * frac_lon, frac_lat * frac_lon], axis=3)
    return stacked.astype(jnp.float32)


def draw_frame_turning(key, part):
    shape = (2, LAT_BLOCKS, LON_BLOCKS, SLOTS)
    angle = jax.random.uniform(jax.random.fold_in(key, 13), shape, jnp.float32, -math.pi, math.pi)
    return jnp.stack([jnp.cos(angle), jnp.sin(angle)], axis=3).astype(jnp.float32)


def steps_of(rng, shape, cuts, low, top_value):
    def one(position, shards_of):
        draws = jax.random.uniform(jax.random.fold_in(jax.random.fold_in(rng, 6), position), (shards_of,), jnp.float32, low / len(cuts), top_value / len(cuts))
        return jnp.repeat(jnp.exp(draws), shape[position] // shards_of).reshape((-1,) + (1,) * (len(shape) - position - 1))

    gain = one(*cuts[0])
    for cut in cuts[1:]:
        gain = gain * one(*cut)
    return gain


def centred(rng, shape, spread, reach, shards=(), kind=jnp.bfloat16):
    factor_of = steps_of(rng, shape, shards, -0.22, 0.18) if shards else 1.0
    values = jax.random.normal(rng, shape, jnp.float32) * spread * factor_of
    return jnp.minimum(jnp.maximum(values, -reach), reach).astype(kind)


def setup_inputs(seed: int = 0) -> dict:
    arg_keys = jax.random.split(jax.random.key(seed), 9)
    return {
        "mass_per_volume": jnp.clip(jnp.exp(math.log(2.0) - 1.3862944 * jax.random.uniform(arg_keys[0], (2, DEPTH_STRATA, MESH_HEIGHT, MESH_WIDTH), jnp.float32) ** steps_of(arg_keys[0], (2, DEPTH_STRATA, MESH_HEIGHT, MESH_WIDTH), ((0, 2), (2, 4), (3, 4)), -0.2, 0.2)), 0.5, 2.0),
        "flow_speed": centred(arg_keys[1], (2, 3, DEPTH_STRATA, MESH_HEIGHT, MESH_WIDTH), 0.5, 3.0, ((0, 2), (3, 4), (4, 4)), jnp.float32),
        "heat_measure": jnp.clip(jnp.exp(math.log(2.0) - 1.3862944 * jax.random.uniform(arg_keys[2], (2, DEPTH_STRATA, MESH_HEIGHT, MESH_WIDTH), jnp.float32) ** steps_of(arg_keys[2], (2, DEPTH_STRATA, MESH_HEIGHT, MESH_WIDTH), ((0, 2), (2, 4), (3, 4)), -0.2, 0.2)), 0.5, 2.0),
        "fields_at_outset": centred(arg_keys[3], (2, 5, DEPTH_STRATA, MESH_HEIGHT, MESH_WIDTH), 1.0, 6.0, ((0, 2), (3, 4), (4, 4)), jnp.float32),
        "opposite_block": draw_opposite_block(jax.random.fold_in(arg_keys[8], 71), 0),
        "donor_lower_corner": draw_donor_lower_corner(jax.random.fold_in(arg_keys[8], 71), 0),
        "blend_factors": draw_blend_factors(jax.random.fold_in(arg_keys[8], 71), 0),
        "frame_turning": draw_frame_turning(jax.random.fold_in(arg_keys[8], 71), 0),
    }


OMEGA = 0.5
GRAVITY = 1.0
VISCOSITY = 0.2
DIFFUSIVITY = 0.2
GAMMA = 1.4
TIME_STEP = 0.05


def tendency(padded, below, above, radius, theta, longitude, yang_flag, step_lat, step_lon):
    height = padded.shape[2] - 4
    width = padded.shape[3] - 4
    center = padded[:, :, 2:height + 2, 2:width + 2]
    north_far = padded[:, :, 0:height, 2:width + 2]
    north_near = padded[:, :, 1:height + 1, 2:width + 2]
    south_near = padded[:, :, 3:height + 3, 2:width + 2]
    south_far = padded[:, :, 4:height + 4, 2:width + 2]
    west_far = padded[:, :, 2:height + 2, 0:width]
    west_near = padded[:, :, 2:height + 2, 1:width + 1]
    east_near = padded[:, :, 2:height + 2, 3:width + 3]
    east_far = padded[:, :, 2:height + 2, 4:width + 4]
    grad_lat = (north_far - 8.0 * north_near + 8.0 * south_near - south_far) / (12.0 * step_lat)
    curv_lat = (16.0 * (north_near + south_near) - (north_far + south_far) - 30.0 * center) / (12.0 * step_lat * step_lat)
    grad_lon = (west_far - 8.0 * west_near + 8.0 * east_near - east_far) / (12.0 * step_lon)
    curv_lon = (16.0 * (west_near + east_near) - (west_far + east_far) - 30.0 * center) / (12.0 * step_lon * step_lon)
    grad_rad = 0.5 * (above - below)
    curv_rad = above - 2.0 * center + below
    sin_lat = jnp.sin(theta)
    cos_lat = jnp.cos(theta)
    cot_lat = cos_lat / sin_lat
    inv_radius = 1.0 / radius
    inv_arc = inv_radius / sin_lat
    slope_lat = inv_radius * grad_lat
    slope_lon = inv_arc * grad_lon
    mass_per_volume = center[0]
    wind_rad = center[1]
    wind_lat = center[2]
    wind_lon = center[3]
    thermal = center[4]
    advect = wind_rad * grad_rad + wind_lat * slope_lat + wind_lon * slope_lon
    laplace = curv_rad + 2.0 * inv_radius * grad_rad + inv_radius * inv_radius * (curv_lat + cot_lat * grad_lat) + inv_arc * inv_arc * curv_lon
    diverge = grad_rad[1] + 2.0 * inv_radius * wind_rad + slope_lat[2] + cot_lat * inv_radius * wind_lat + slope_lon[3]
    inv_density = 1.0 / mass_per_volume
    press_rad = (thermal * grad_rad[0] + mass_per_volume * grad_rad[4]) * inv_density
    press_lat = (thermal * slope_lat[0] + mass_per_volume * slope_lat[4]) * inv_density
    press_lon = (thermal * slope_lon[0] + mass_per_volume * slope_lon[4]) * inv_density
    sin_lon = jnp.sin(longitude)
    cos_lon = jnp.cos(longitude)
    yin_flag = 1.0 - yang_flag
    spin_rad = OMEGA * (yin_flag * cos_lat + yang_flag * sin_lat * sin_lon)
    spin_lat = OMEGA * (yang_flag * cos_lat * sin_lon - yin_flag * sin_lat)
    spin_lon = OMEGA * yang_flag * cos_lon
    coriolis_rad = -2.0 * (spin_lat * wind_lon - spin_lon * wind_lat)
    coriolis_lat = -2.0 * (spin_lon * wind_rad - spin_rad * wind_lon)
    coriolis_lon = -2.0 * (spin_rad * wind_lat - spin_lat * wind_rad)
    rate_density = -advect[0] - mass_per_volume * diverge
    rate_rad = -advect[1] + inv_radius * (wind_lat * wind_lat + wind_lon * wind_lon) - press_rad - GRAVITY + coriolis_rad + VISCOSITY * laplace[1]
    rate_lat = -advect[2] + inv_radius * (cot_lat * wind_lon * wind_lon - wind_rad * wind_lat) - press_lat + coriolis_lat + VISCOSITY * laplace[2]
    rate_lon = -advect[3] - inv_radius * (wind_rad * wind_lon + cot_lat * wind_lat * wind_lon) - press_lon + coriolis_lon + VISCOSITY * laplace[3]
    rate_heat = -advect[4] - (GAMMA - 1.0) * thermal * diverge + DIFFUSIVITY * laplace[4]
    return jnp.stack([rate_density, rate_rad, rate_lat, rate_lon, rate_heat])


def reference(mass_per_volume, flow_speed, heat_measure, fields_at_outset, opposite_block, donor_lower_corner, blend_factors, frame_turning):
    integrator_substep = jnp.concatenate([mass_per_volume[:, None], flow_speed, heat_measure[:, None]], axis=1)
    step_lat = (math.pi / 2.0) / MESH_HEIGHT
    step_lon = (1.5 * math.pi) / MESH_WIDTH
    lat_len = 2 * CLON
    lon_len = 2 * CLAT
    blocks = jnp.arange(LON_BLOCKS, dtype=jnp.int32)[None, :, None]
    padded = jnp.pad(integrator_substep, ((0, 0), (0, 0), (0, 0), (2, 2), (2, 2)))
    corner_shift = [0, MESH_WIDTH, 1, MESH_WIDTH + 1]
    for panel in range(2):
        source = integrator_substep[1 - panel].reshape(5 * DEPTH_STRATA, MESH_HEIGHT * MESH_WIDTH)
        rows_src = opposite_block[panel] * CLAT + donor_lower_corner[panel] // CLON
        cols_src = blocks * CLON + donor_lower_corner[panel] % CLON
        anchor = (rows_src * MESH_WIDTH + cols_src).astype(jnp.int32)
        ghost = jnp.zeros((5 * DEPTH_STRATA,) + anchor.shape, jnp.float32)
        for corner in range(4):
            took = jnp.take(source, (anchor + corner_shift[corner]).reshape(-1), axis=1).reshape((5 * DEPTH_STRATA,) + anchor.shape)
            ghost = ghost + blend_factors[panel][:, :, corner, :] * took
        ghost = ghost.reshape(5, DEPTH_STRATA, LAT_BLOCKS, LON_BLOCKS, SLOTS)
        cosine = frame_turning[panel][:, :, 0, :]
        sine = frame_turning[panel][:, :, 1, :]
        turned_lat = cosine * ghost[2] + sine * ghost[3]
        turned_lon = cosine * ghost[3] - sine * ghost[2]
        ghost = jnp.stack([ghost[0], ghost[1], turned_lat, turned_lon, ghost[4]])
        north = ghost[:, :, 0, :, 0:lat_len].reshape(5, DEPTH_STRATA, LON_BLOCKS, 2, CLON).transpose(0, 1, 3, 2, 4).reshape(5, DEPTH_STRATA, 2, MESH_WIDTH)
        south = ghost[:, :, LAT_BLOCKS - 1, :, lat_len:2 * lat_len].reshape(5, DEPTH_STRATA, LON_BLOCKS, 2, CLON).transpose(0, 1, 3, 2, 4).reshape(5, DEPTH_STRATA, 2, MESH_WIDTH)
        west = ghost[:, :, :, 0, 2 * lat_len:2 * lat_len + lon_len].reshape(5, DEPTH_STRATA, LAT_BLOCKS, 2, CLAT).transpose(0, 1, 3, 2, 4).reshape(5, DEPTH_STRATA, 2, MESH_HEIGHT).transpose(0, 1, 3, 2)
        east = ghost[:, :, :, LON_BLOCKS - 1, 2 * lat_len + lon_len:].reshape(5, DEPTH_STRATA, LAT_BLOCKS, 2, CLAT).transpose(0, 1, 3, 2, 4).reshape(5, DEPTH_STRATA, 2, MESH_HEIGHT).transpose(0, 1, 3, 2)
        padded = padded.at[panel, :, :, 0:2, 2:MESH_WIDTH + 2].set(north)
        padded = padded.at[panel, :, :, MESH_HEIGHT + 2:MESH_HEIGHT + 4, 2:MESH_WIDTH + 2].set(south)
        padded = padded.at[panel, :, :, 2:MESH_HEIGHT + 2, 0:2].set(west)
        padded = padded.at[panel, :, :, 2:MESH_HEIGHT + 2, MESH_WIDTH + 2:MESH_WIDTH + 4].set(east)
    theta = (math.pi / 4.0 + (jnp.arange(MESH_HEIGHT, dtype=jnp.int32).astype(jnp.float32) + 0.5) * step_lat).reshape(MESH_HEIGHT, 1)
    longitude = -0.75 * math.pi + (jnp.arange(MESH_WIDTH, dtype=jnp.int32).astype(jnp.float32) + 0.5) * step_lon
    base_radius = 1.0 / step_lat

    def one_level(level):
        lower = jnp.maximum(level - 1, 0).astype(jnp.int32)
        upper = jnp.minimum(level + 1, DEPTH_STRATA - 1).astype(jnp.int32)
        center = lax.dynamic_slice_in_dim(padded, level, 1, axis=2)
        below = lax.dynamic_slice_in_dim(padded, lower, 1, axis=2)[:, :, :, 2:MESH_HEIGHT + 2, 2:MESH_WIDTH + 2]
        above = lax.dynamic_slice_in_dim(padded, upper, 1, axis=2)[:, :, :, 2:MESH_HEIGHT + 2, 2:MESH_WIDTH + 2]
        radius = (base_radius + level.astype(jnp.float32)).reshape(1, 1, 1)
        rates = [tendency(center[panel], below[panel], above[panel], radius, theta, longitude, float(panel), step_lat, step_lon) for panel in range(2)]
        return jnp.stack(rates)

    levels_out = lax.map(one_level, jnp.arange(DEPTH_STRATA, dtype=jnp.int32))
    section_rate = jnp.moveaxis(levels_out[:, :, :, 0], 0, 2)
    new_state = 0.75 * fields_at_outset + 0.25 * (integrator_substep + TIME_STEP * section_rate)
    return section_rate, new_state
```

```python
import functools
import math

import jax
import jax.numpy as jnp
from jax import lax
from jax.experimental import pallas as pl
from jax.experimental.pallas import tpu as pltpu
from jax.sharding import PartitionSpec as P

OMEGA = 0.5
GRAVITY = 1.0
VISCOSITY = 0.2
DIFFUSIVITY = 0.2
GAMMA = 1.4
TIME_STEP = 0.05
LANES = 128
SUB = 8
ANY = pl.BlockSpec(memory_space=pl.ANY)
VMEM = pl.BlockSpec(memory_space=pltpu.VMEM)
SMEM = pl.BlockSpec(memory_space=pltpu.SMEM)


def pair_partner(i, count, odd):
    if not odd:
        return i ^ 1
    return (i + 1) % count if i % 2 else (i - 1) % count


def swap_pairs(value, axis, odd):
    count = lax.axis_size(axis)
    return lax.ppermute(value, axis, [(i, pair_partner(i, count, odd)) for i in range(count)])


def swap_panels(value, distance):
    n_lat = lax.axis_size("lat")
    pairs = [
        (p * n_lat + a, (1 - p) * n_lat + (a ^ distance)) for p in range(2) for a in range(n_lat)
    ]
    return lax.ppermute(value, ("panel", "lat"), pairs)


def window_of(run, cols):
    tiles = cols // LANES
    for width in range(1, tiles + 1):
        if all(
            start - min(start // LANES, tiles - width) * LANES + run <= width * LANES
            for start in range(0, cols, run)
        ):
            return width
    return tiles


def edge_rows_kernel(rho, flow, heat, even_out, odd_out, tops, bottoms, sems):
    levels = rho.shape[1]
    rows = rho.shape[2]
    copies = []
    for side, buf, start in ((0, tops, 0), (1, bottoms, rows - SUB)):
        span = pl.ds(start, SUB)
        copies.append(pltpu.make_async_copy(rho.at[0, :, span], buf.at[0], sems.at[side, 0]))
        copies.append(
            pltpu.make_async_copy(flow.at[0, :, :, span], buf.at[pl.ds(1, 3)], sems.at[side, 1])
        )
        copies.append(pltpu.make_async_copy(heat.at[0, :, span], buf.at[4], sems.at[side, 2]))
    for copy in copies:
        copy.start()
    for copy in copies:
        copy.wait()
    even = lax.rem(lax.axis_index("lat"), 2) == 0
    for row in range(2):
        for field in range(5):
            for tile in range(even_out.shape[2]):
                lanes = slice(tile * LANES, (tile + 1) * LANES)
                top = tops[field, :, row, lanes]
                bottom = bottoms[field, :, SUB - 2 + row, lanes]
                even_out[row, field, tile] = jnp.where(even, bottom, top)
                odd_out[row, field, tile] = jnp.where(even, top, bottom)


def edge_rows(rho, flow, heat):
    levels, rows, cols = rho.shape[1:]
    shape = jax.ShapeDtypeStruct((2, 5, cols // LANES, levels, LANES), jnp.float32)
    return pl.pallas_call(
        edge_rows_kernel,
        out_shape=(shape, shape),
        in_specs=[ANY] * 3,
        out_specs=(VMEM, VMEM),
        scratch_shapes=[
            pltpu.VMEM((5, levels, SUB, cols), jnp.float32),
            pltpu.VMEM((5, levels, SUB, cols), jnp.float32),
            pltpu.SemaphoreType.DMA((2, 3)),
        ],
        name="edge_rows",
    )(rho, flow, heat)


def cell_major_kernel(rho, flow, heat, cells, even_out, odd_out):
    levels = rho.shape[1]
    cols = rho.shape[3]
    field_rows = 5 * levels
    for row in range(SUB):
        for start in range(0, cols, LANES):
            span = slice(start, start + LANES)
            stack = jnp.concatenate(
                [rho[0, :, row, span]]
                + [flow[0, part, :, row, span] for part in range(3)]
                + [heat[0, :, row, span]],
                axis=0,
            )
            at = row * cols + start
            cells[at : at + LANES, 0:field_rows] = stack.T
    even = lax.rem(lax.axis_index("lon"), 2) == 0
    for row in range(SUB):
        for layer in range(2):
            west = cells[row * cols + layer : row * cols + layer + 1, :]
            at = row * cols + cols - 2 + layer
            east = cells[at : at + 1, :]
            even_out[layer, row : row + 1, :] = jnp.where(even, east, west)
            odd_out[layer, row : row + 1, :] = jnp.where(even, west, east)


def cell_major(rho, flow, heat):
    levels, rows, cols = rho.shape[1:]
    column = jax.ShapeDtypeStruct((2, rows, LANES), jnp.float32)
    column_spec = pl.BlockSpec((2, SUB, LANES), lambda i: (0, i, 0))
    return pl.pallas_call(
        cell_major_kernel,
        grid=(rows // SUB,),
        out_shape=(jax.ShapeDtypeStruct((rows * cols, LANES), jnp.float32), column, column),
        in_specs=[
            pl.BlockSpec((1, levels, SUB, cols), lambda i: (0, 0, i, 0)),
            pl.BlockSpec((1, 3, levels, SUB, cols), lambda i: (0, 0, 0, i, 0)),
            pl.BlockSpec((1, levels, SUB, cols), lambda i: (0, 0, i, 0)),
        ],
        out_specs=(
            pl.BlockSpec((SUB * cols, LANES), lambda i: (i, 0)),
            column_spec,
            column_spec,
        ),
        name="cell_major",
    )(rho, flow, heat)


def donate_kernel(n_lat, n_lon, rows, cols, field_rows, *refs):
    requests = refs[:n_lat]
    cells = refs[n_lat]
    replies = refs[n_lat + 1 : 2 * n_lat + 1]
    gathered = refs[2 * n_lat + 1]
    lat_len, lon_len = 2 * cols, 2 * rows
    run_lat, run_lon = lat_len // n_lat, lon_len // n_lat
    tiles = cols // LANES
    width = window_of(run_lat, cols)
    lat_here = lax.axis_index("lat")
    lon_here = lax.axis_index("lon")

    def find_run(request, start, run):
        found = jnp.int32(0)
        for r in range(1, n_lat):
            match = request[0, start + r * run].astype(jnp.int32) == lat_here
            found = jnp.where(match, jnp.int32(r), found)
        return found

    def blend(request, slot):
        cell = request[1, slot].astype(jnp.int32)
        total = request[2, slot] * cells[pl.ds(cell, 1), :]
        total += request[3, slot] * cells[pl.ds(cell + cols, 1), :]
        total += request[4, slot] * cells[pl.ds(cell + 1, 1), :]
        total += request[5, slot] * cells[pl.ds(cell + cols + 1, 1), :]
        return total

    for distance in range(n_lat):
        request, reply = requests[distance], replies[distance]
        asker = jnp.bitwise_xor(lat_here, distance)

        @pl.when((asker == 0) | (asker == n_lat - 1))
        def _():
            run = find_run(request, 0, run_lat)
            start = lax.rem(run * run_lat, cols)
            base = jnp.minimum(lax.div(start, LANES), tiles - width)
            offset = start - base * LANES

            def step(t, carry):
                gathered[pl.ds(offset + t, 1), :] = blend(request, run * run_lat + t)
                return carry

            lax.fori_loop(0, run_lat, step, 0, unroll=8)
            for tile in range(width):
                block = gathered[tile * LANES : (tile + 1) * LANES, :]
                reply[0:field_rows, tile * LANES : (tile + 1) * LANES] = block.T[0:field_rows]

        @pl.when((lon_here == 0) | (lon_here == n_lon - 1))
        def _():
            run = find_run(request, lat_len, run_lon)

            def step(t, carry):
                gathered[pl.ds(t, 1), :] = blend(request, lat_len + run * run_lon + t)
                return carry

            lax.fori_loop(0, run_lon, step, 0, unroll=8)
            reply[field_rows : field_rows + run_lon, 0:LANES] = gathered[0:run_lon, :]


def donate(requests, cells, rows, cols, field_rows):
    n_lat, n_lon = lax.axis_size("lat"), lax.axis_size("lon")
    width = window_of(2 * cols // n_lat, cols)
    reply = jax.ShapeDtypeStruct(
        (field_rows + 2 * rows // n_lat, max(width, 1) * LANES), jnp.float32
    )
    return pl.pallas_call(
        functools.partial(donate_kernel, n_lat, n_lon, rows, cols, field_rows),
        out_shape=(reply,) * n_lat,
        in_specs=[SMEM] * n_lat + [VMEM],
        out_specs=(VMEM,) * n_lat,
        scratch_shapes=[pltpu.VMEM((width * LANES, LANES), jnp.float32)],
        name="donate",
    )(*requests, cells)


def stencil_kernel(geometry, groups, chunk, aliased, *refs):
    n_panel, n_lat, n_lon, levels, rows, cols = geometry
    tiles = cols // LANES
    field_rows = 5 * levels
    (partners, turn_lat, turn_lon) = refs[:3]
    replies = refs[3 : 3 + n_lat]
    at = 3 + n_lat
    lat_even, lat_odd, lon_even, lon_odd = refs[at : at + 4]
    rho, flow, heat, outset = refs[at + 4 : at + 8]
    at += 8 + (2 if aliased else 0)
    rate_out, state_out = refs[at : at + 2]
    (
        block,
        start_box,
        rate_box,
        state_box,
        reply_box,
        halo,
        side,
        mixed,
        row_box,
        spin_box,
        in_sems,
        start_sems,
        out_sems,
        edge_sems,
    ) = refs[at + 2 :]
    lat_here = lax.axis_index("lat")
    lon_here = lax.axis_index("lon")
    panel_here = lax.axis_index("panel")
    lat_len, lon_len = 2 * cols, 2 * rows
    run_lat, run_lon = lat_len // n_lat, lon_len // n_lat
    width = window_of(run_lat, cols)
    step_lat = math.pi / 2.0 / (rows * n_lat)
    step_lon = 1.5 * math.pi / (cols * n_lon)
    chunks = levels // chunk

    def load_copies(c):
        span = pl.ds(c * chunk, chunk)
        out = []
        for t in range(tiles):
            lanes = pl.ds(t * LANES, LANES)
            body = pl.ds(SUB, rows)
            out.append(
                pltpu.make_async_copy(
                    rho.at[0, span, :, lanes], block.at[0, t, span, body], in_sems.at[c, t, 0]
                )
            )
            out.append(
                pltpu.make_async_copy(
                    flow.at[0, :, span, :, lanes],
                    block.at[pl.ds(1, 3), t, span, body],
                    in_sems.at[c, t, 1],
                )
            )
            out.append(
                pltpu.make_async_copy(
                    heat.at[0, span, :, lanes], block.at[4, t, span, body], in_sems.at[c, t, 2]
                )
            )
        return out

    def start_copies(c):
        span = pl.ds(c * chunk, chunk)
        return [
            pltpu.make_async_copy(
                outset.at[0, :, span, pl.ds(first, count)],
                start_box.at[:, span, pl.ds(first, count)],
                start_sems.at[c, g],
            )
            for g, (first, count) in enumerate(groups)
        ]

    def out_copies(c):
        span = pl.ds(c * chunk, chunk)
        out = []
        for g, (first, count) in enumerate(groups):
            part = pl.ds(first, count)
            out.append(
                pltpu.make_async_copy(
                    rate_box.at[:, span, part], rate_out.at[0, :, span, part], out_sems.at[c, g, 0]
                )
            )
            out.append(
                pltpu.make_async_copy(
                    state_box.at[:, span, part],
                    state_out.at[0, :, span, part],
                    out_sems.at[c, g, 1],
                )
            )
        return out

    for copy in load_copies(0):
        copy.start()
    reply_copies = [
        pltpu.make_async_copy(replies[d], reply_box.at[d], edge_sems.at[d]) for d in range(n_lat)
    ]
    for copy in reply_copies:
        copy.start()
    lat_is_even = lax.rem(lat_here, 2) == 0
    lon_is_even = lax.rem(lon_here, 2) == 0

    def halo_copies(which):
        even_at = jnp.where(which == 0, 1, 0)
        return (
            pltpu.make_async_copy(lat_even, halo.at[even_at], edge_sems.at[n_lat]),
            pltpu.make_async_copy(lat_odd, halo.at[1 - even_at], edge_sems.at[n_lat + 1]),
            pltpu.make_async_copy(lon_even, side.at[0], edge_sems.at[n_lat + 2]),
            pltpu.make_async_copy(lon_odd, side.at[1], edge_sems.at[n_lat + 3]),
        )

    edge_copies = halo_copies(lax.rem(lat_here, 2))
    for copy in edge_copies:
        copy.start()
    for copy in start_copies(0):
        copy.start()
    for c in range(1, chunks):
        for copy in load_copies(c) + start_copies(c):
            copy.start()

    @pl.when(True)
    def _():
        sub = lax.broadcasted_iota(jnp.int32, (rows, LANES), 0)
        row_global = (lat_here * rows + sub).astype(jnp.float32)
        theta = math.pi / 4.0 + (row_global + 0.5) * step_lat
        sin_lat, cos_lat = jnp.sin(theta), jnp.cos(theta)
        row_box[0] = 1.0 / sin_lat
        row_box[1] = cos_lat / sin_lat
        yang = panel_here.astype(jnp.float32)
        yin = 1.0 - yang
        for t in range(tiles):
            lane = lax.broadcasted_iota(jnp.int32, (SUB, LANES), 1) + t * LANES
            col_global = (lon_here * cols + lane).astype(jnp.float32)
            longitude = -0.75 * math.pi + (col_global + 0.5) * step_lon
            sin_lon = jnp.sin(longitude)[0:1]
            cos_lon = jnp.cos(longitude)[0:1]
            spin_box[0, t] = 2.0 * OMEGA * (yin * cos_lat + yang * sin_lat * sin_lon)
            spin_box[1, t] = 2.0 * OMEGA * (yang * cos_lat * sin_lon - yin * sin_lat)
            spin_box[2, t] = jnp.broadcast_to(2.0 * OMEGA * yang * cos_lon, (rows, LANES))

    for copy in reply_copies:
        copy.wait()
    for copy in edge_copies:
        copy.wait()

    lane8 = lax.broadcasted_iota(jnp.int32, (SUB, LANES), 1)
    sub8 = lax.broadcasted_iota(jnp.int32, (SUB, LANES), 0)

    for which, slot0 in ((0, 0), (1, lat_len)):

        @pl.when(lat_here == (0 if which == 0 else n_lat - 1))
        def _(which=which, slot0=slot0):
            sources = [
                jnp.bitwise_xor(partners[0, slot0 + r * run_lat], lat_here) for r in range(n_lat)
            ]
            for layer in range(2):
                for t in range(tiles):
                    lane = lax.broadcasted_iota(jnp.int32, (field_rows, LANES), 1) + t * LANES
                    value = None
                    for r in range(n_lat):
                        first = r * run_lat - layer * cols
                        if first < 0 or first >= cols:
                            continue
                        if first >= (t + 1) * LANES or first + run_lat <= t * LANES:
                            continue
                        base = min(first // LANES, tiles - width)
                        here = (t - base) * LANES
                        piece = reply_box[sources[r], 0:field_rows, here : here + LANES]
                        value = piece if value is None else jnp.where(lane >= first, piece, value)
                    spot = slot0 + layer * cols + t * LANES
                    cosine = turn_lat[0:1, spot : spot + LANES]
                    sine = turn_lat[1:2, spot : spot + LANES]
                    parts = [value[f * levels : (f + 1) * levels] for f in range(5)]
                    parts[2], parts[3] = (
                        cosine * parts[2] + sine * parts[3],
                        cosine * parts[3] - sine * parts[2],
                    )
                    for f in range(5):
                        halo[which, layer, f, t] = parts[f]

    for which, slot0 in ((0, 2 * lat_len), (1, 2 * lat_len + lon_len)):
        mine = jnp.where(lon_is_even, 1, 0) if which == 0 else jnp.where(lon_is_even, 0, 1)

        @pl.when(lon_here != (0 if which == 0 else n_lon - 1))
        def _(which=which, mine=mine):
            side[2 + which] = side[mine]

        @pl.when(lon_here == (0 if which == 0 else n_lon - 1))
        def _(which=which, slot0=slot0):
            lane = lax.broadcasted_iota(jnp.int32, (run_lon, LANES), 1)
            is_lat = (lane >= 2 * levels) & (lane < 3 * levels)
            is_lon = (lane >= 3 * levels) & (lane < 4 * levels)
            for r in range(n_lat):
                source = jnp.bitwise_xor(partners[0, slot0 + r * run_lon], lat_here)
                layer, first = r * run_lon // rows, r * run_lon % rows
                value = reply_box[source, field_rows : field_rows + run_lon, 0:LANES]
                slots = slice(which * lon_len + r * run_lon, which * lon_len + (r + 1) * run_lon)
                cosine = jnp.broadcast_to(turn_lon[slots, 0:1], (run_lon, LANES))
                sine = jnp.broadcast_to(turn_lon[slots, 1:2], (run_lon, LANES))
                later = pltpu.roll(value, LANES - levels, 1)
                earlier = pltpu.roll(value, levels, 1)
                value = jnp.where(
                    is_lat,
                    cosine * value + sine * later,
                    jnp.where(is_lon, cosine * value - sine * earlier, value),
                )
                side[2 + which, layer, first : first + run_lon] = value

    lane_all = lax.broadcasted_iota(jnp.int32, (rows, LANES), 1)
    columns = [side[3, 0], side[3, 1], side[2, 0], side[2, 1]]
    columns = [columns[0]] + [pltpu.roll(columns[j], j, 1) for j in range(1, 4)]
    for q in range(4):
        pick = jnp.bitwise_and(lane_all - q, 3)
        value = columns[0]
        for j in range(1, 4):
            value = jnp.where(pick == j, columns[j], value)
        mixed[q] = value

    for copy in load_copies(0):
        copy.wait()

    by_lat = 1.0 / (12.0 * step_lat)
    by_lon = 1.0 / (12.0 * step_lon)

    def one_level(k):
        below = jnp.maximum(k - 1, 0)
        above = jnp.minimum(k + 1, levels - 1)
        quarter = jnp.bitwise_and(k, 3)
        radius = jnp.broadcast_to(
            1.0 / step_lat + k.astype(jnp.float32), (SUB, LANES)
        )
        inv_radius = 1.0 / radius
        lat_scale = inv_radius * by_lat
        for first, count in groups:
            for top in range(first, first + count, SUB):
                one_strip(k, below, above, quarter, inv_radius, lat_scale, top)

    def one_strip(k, below, above, quarter, inv_radius, lat_scale, top):
        strip = slice(top, top + SUB)
        inv_sin, cot = row_box[0, strip], row_box[1, strip]
        inv_arc = inv_radius * inv_sin
        lon_scale = inv_arc * by_lon
        cot_r = cot * inv_radius
        two_r = 2.0 * inv_radius
        curve_lat = (VISCOSITY / (12.0 * step_lat * step_lat)) * inv_radius * inv_radius
        curve_lon = (VISCOSITY / (12.0 * step_lon * step_lon)) * inv_arc * inv_arc
        slope_extra = (VISCOSITY * by_lat) * inv_radius * cot_r
        radial_extra = VISCOSITY * inv_radius
        center_weight = 2.0 * VISCOSITY + 30.0 * (curve_lat + curve_lon)
        north, south = top == 0, top == rows - SUB

        def derive(f, full):
            here = [block[f, t, k, SUB + top : 2 * SUB + top] for t in range(tiles)]
            shift = LANES - 2 - f * levels - k
            ghost = pltpu.roll(mixed[quarter, strip], shift, 1)
            ghost_w, ghost_e = pltpu.roll(ghost, LANES - 1, 1), pltpu.roll(ghost, 1, 1)
            w1s = [pltpu.roll(x, 1, 1) for x in here]
            w2s = [pltpu.roll(x, 2, 1) for x in here]
            e1s = [pltpu.roll(x, LANES - 1, 1) for x in here]
            e2s = [pltpu.roll(x, LANES - 2, 1) for x in here]
            out = []
            for t in range(tiles):
                at = SUB + top
                n1, n2 = block[f, t, k, at - 1 : at + 7], block[f, t, k, at - 2 : at + 6]
                s1, s2 = block[f, t, k, at + 1 : at + 9], block[f, t, k, at + 2 : at + 10]
                if north:
                    g2 = jnp.broadcast_to(halo[0, 0, f, t, pl.ds(k, 1), :], (SUB, LANES))
                    g1 = jnp.broadcast_to(halo[0, 1, f, t, pl.ds(k, 1), :], (SUB, LANES))
                    n1 = jnp.where(sub8 == 0, g1, n1)
                    n2 = jnp.where(sub8 == 0, g2, jnp.where(sub8 == 1, g1, n2))
                if south:
                    g1 = jnp.broadcast_to(halo[1, 0, f, t, pl.ds(k, 1), :], (SUB, LANES))
                    g2 = jnp.broadcast_to(halo[1, 1, f, t, pl.ds(k, 1), :], (SUB, LANES))
                    s1 = jnp.where(sub8 == SUB - 1, g1, s1)
                    s2 = jnp.where(sub8 == SUB - 1, g2, jnp.where(sub8 == SUB - 2, g1, s2))
                w1 = jnp.where(lane8 == 0, w1s[t - 1] if t else ghost_w, w1s[t])
                w2 = jnp.where(lane8 < 2, w2s[t - 1] if t else ghost, w2s[t])
                last = t == tiles - 1
                e1 = jnp.where(lane8 == LANES - 1, ghost_e if last else e1s[t + 1], e1s[t])
                e2 = jnp.where(lane8 >= LANES - 2, ghost if last else e2s[t + 1], e2s[t])
                low = block[f, t, below, SUB + top : 2 * SUB + top]
                high = block[f, t, above, SUB + top : 2 * SUB + top]
                rad = high - low
                lat = 8.0 * (s1 - n1) - (s2 - n2)
                lon = 8.0 * (e1 - w1) - (e2 - w2)
                bend = None
                if full:
                    bend = (
                        VISCOSITY * (high + low)
                        + curve_lat * (16.0 * (s1 + n1) - (s2 + n2))
                        + curve_lon * (16.0 * (e1 + w1) - (e2 + w2))
                        - center_weight * here[t]
                    )
                out.append((rad, lat, lon, bend))
            return here, out

        wind_rad = [block[1, t, k, SUB + top : 2 * SUB + top] for t in range(tiles)]
        wind_lat = [block[2, t, k, SUB + top : 2 * SUB + top] for t in range(tiles)]
        wind_lon = [block[3, t, k, SUB + top : 2 * SUB + top] for t in range(tiles)]
        go_rad = [0.5 * x for x in wind_rad]
        go_lat = [lat_scale * x for x in wind_lat]
        go_lon = [lon_scale * x for x in wind_lon]

        def put(f, t, center, rate):
            lanes = slice(t * LANES, (t + 1) * LANES)
            rate_box[f, k, strip, lanes] = rate
            state_box[f, k, strip, lanes] = (
                0.75 * start_box[f, k, strip, lanes] + 0.25 * center
            ) + (0.25 * TIME_STEP) * rate

        rho_here, rho_d = derive(0, False)
        heat_here, heat_d = derive(4, True)
        ratio = [heat_here[t] / rho_here[t] for t in range(tiles)]
        press, rho_rate, heat_rate = [], [], []
        for t in range(tiles):
            (a, b, c, _), (d, e, g, bend) = rho_d[t], heat_d[t]
            press.append(
                (
                    0.5 * (ratio[t] * a + d),
                    lat_scale * (ratio[t] * b + e),
                    lon_scale * (ratio[t] * c + g),
                )
            )
            rho_rate.append(go_rad[t] * a + go_lat[t] * b + go_lon[t] * c)
            heat_rate.append(
                bend
                + (radial_extra - go_rad[t]) * d
                + (slope_extra - go_lat[t]) * e
                - go_lon[t] * g
            )
        diverge = [two_r * wind_rad[t] + cot_r * wind_lat[t] for t in range(tiles)]
        for f in (1, 2, 3):
            here, d_all = derive(f, True)
            for t in range(tiles):
                d, e, g, bend = d_all[t]
                spin_rad, spin_lat = spin_box[0, t, strip], spin_box[1, t, strip]
                spin_lon = spin_box[2, t, strip]
                rate = (
                    bend
                    + (radial_extra - go_rad[t]) * d
                    + (slope_extra - go_lat[t]) * e
                    - go_lon[t] * g
                    - press[t][f - 1]
                )
                if f == 1:
                    diverge[t] += 0.5 * d
                    rate += inv_radius * (wind_lat[t] * wind_lat[t] + wind_lon[t] * wind_lon[t])
                    rate += spin_lon * wind_lat[t] - spin_lat * wind_lon[t] - GRAVITY
                elif f == 2:
                    diverge[t] += lat_scale * e
                    rate += cot_r * (wind_lon[t] * wind_lon[t])
                    rate -= inv_radius * (wind_rad[t] * wind_lat[t])
                    rate += spin_rad * wind_lon[t] - spin_lon * wind_rad[t]
                else:
                    diverge[t] += lon_scale * g
                    rate -= (inv_radius * wind_rad[t] + cot_r * wind_lat[t]) * wind_lon[t]
                    rate += spin_lat * wind_rad[t] - spin_rad * wind_lat[t]
                put(f, t, here[t], rate)
        for t in range(tiles):
            put(0, t, rho_here[t], -rho_rate[t] - rho_here[t] * diverge[t])
            put(
                4,
                t,
                heat_here[t],
                heat_rate[t] - (GAMMA - 1.0) * (heat_here[t] * diverge[t]),
            )

    for c in range(chunks):
        if c + 1 < chunks:
            for copy in load_copies(c + 1):
                copy.wait()
        for copy in start_copies(c):
            copy.wait()

        @pl.loop(c * chunk, (c + 1) * chunk)
        def _(k):
            one_level(k)

        for copy in out_copies(c):
            copy.start()
    for c in range(chunks):
        for copy in out_copies(c):
            copy.wait()


def stencil(
    groups, partners, turn_lat, turn_lon, replies, halos, sides, rho, flow, heat, outset, prior=None
):
    levels, rows, cols = rho.shape[1:]
    n_panel, n_lat, n_lon = (lax.axis_size(x) for x in ("panel", "lat", "lon"))
    tiles = cols // LANES
    chunk = 4
    chunks = levels // chunk
    out = jax.ShapeDtypeStruct(outset.shape, jnp.float32)
    prior = tuple(prior or ())
    box = pltpu.VMEM((5, levels, rows, cols), jnp.float32)
    share = sum(count for _, count in groups) / rows
    n_in = 3 + n_lat + 8
    return pl.pallas_call(
        functools.partial(
            stencil_kernel, (n_panel, n_lat, n_lon, levels, rows, cols), groups, chunk, bool(prior)
        ),
        out_shape=(out, out),
        in_specs=[SMEM, VMEM, VMEM] + [ANY] * (n_in - 3 + len(prior)),
        out_specs=(ANY, ANY),
        input_output_aliases={n_in: 0, n_in + 1: 1} if prior else {},
        scratch_shapes=[
            pltpu.VMEM((5, tiles, levels, rows + 2 * SUB, LANES), jnp.float32),
            box,
            box,
            box,
            pltpu.VMEM((n_lat,) + replies[0].shape, jnp.float32),
            pltpu.VMEM((2, 2, 5, tiles, levels, LANES), jnp.float32),
            pltpu.VMEM((4, 2, rows, LANES), jnp.float32),
            pltpu.VMEM((4, rows, LANES), jnp.float32),
            pltpu.VMEM((2, rows, LANES), jnp.float32),
            pltpu.VMEM((3, tiles, rows, LANES), jnp.float32),
            pltpu.SemaphoreType.DMA((chunks, tiles, 3)),
            pltpu.SemaphoreType.DMA((chunks, len(groups))),
            pltpu.SemaphoreType.DMA((chunks, len(groups), 2)),
            pltpu.SemaphoreType.DMA((n_lat + 4,)),
        ],
        compiler_params=pltpu.CompilerParams(vmem_limit_bytes=40 * 1024 * 1024),
        cost_estimate=pl.CostEstimate(
            flops=int(250 * share * levels * rows * cols),
            bytes_accessed=int(16 * share * levels * rows * cols * 5),
            transcendentals=0,
        ),
        name="stencil",
    )(
        partners,
        turn_lat,
        turn_lon,
        *replies,
        *halos,
        *sides,
        rho,
        flow,
        heat,
        outset,
        *prior,
    )


def shards(rho, flow, heat, outset, opposite_block, donor_lower_corner, blend, turning):
    levels, rows, cols = rho.shape[1:]
    n_lat, n_lon = lax.axis_size("lat"), lax.axis_size("lon")
    lat_here, lon_here = lax.axis_index("lat"), lax.axis_index("lon")
    slots = opposite_block.shape[-1]
    lat_len, lon_len = 2 * cols, 2 * rows
    partners = opposite_block.reshape(1, slots)
    meta = jnp.concatenate(
        [
            partners.astype(jnp.float32),
            donor_lower_corner.reshape(1, slots).astype(jnp.float32),
            blend.reshape(4, slots),
        ],
        axis=0,
    )
    request = jnp.concatenate(
        [
            jnp.where(lat_here == 0, meta[:, 0:lat_len], meta[:, lat_len : 2 * lat_len]),
            jnp.where(
                lon_here == 0,
                meta[:, 2 * lat_len : 2 * lat_len + lon_len],
                meta[:, 2 * lat_len + lon_len :],
            ),
        ],
        axis=1,
    )
    requests = [swap_panels(request, d) for d in range(n_lat)]
    even_rows, odd_rows = edge_rows(rho, flow, heat)
    halos = (swap_pairs(even_rows, "lat", False), swap_pairs(odd_rows, "lat", True))
    cells, even_cols, odd_cols = cell_major(rho, flow, heat)
    sides = (swap_pairs(even_cols, "lon", False), swap_pairs(odd_cols, "lon", True))
    replies = donate(requests, cells, rows, cols, 5 * levels)
    replies = [swap_panels(reply, d) for d, reply in enumerate(replies)]
    turn = turning.reshape(2, slots)
    turn_lon = turn[:, 2 * lat_len :].T
    return stencil(
        ((0, rows),), partners, turn, turn_lon, replies, halos, sides, rho, flow, heat, outset
    )


def solution(mesh):
    in_specs = (
        P("panel", None, "lat", "lon"),
        P("panel", None, None, "lat", "lon"),
        P("panel", None, "lat", "lon"),
        P("panel", None, None, "lat", "lon"),
        P("panel", "lat", "lon", None),
        P("panel", "lat", "lon", None),
        P("panel", "lat", "lon", None, None),
        P("panel", "lat", "lon", None, None),
    )
    out_specs = (P("panel", None, None, "lat", "lon"), P("panel", None, None, "lat", "lon"))
    return jax.shard_map(shards, mesh=mesh, in_specs=in_specs, out_specs=out_specs, check_vma=False)
```

```python
import functools
import math

import jax
import jax.numpy as jnp
from jax import lax
from jax.experimental import pallas as pl
from jax.experimental.pallas import tpu as pltpu
from jax.sharding import PartitionSpec as P

OMEGA = 0.5
GRAVITY = 1.0
VISCOSITY = 0.2
DIFFUSIVITY = 0.2
GAMMA = 1.4
TIME_STEP = 0.05
LANES = 128
SUB = 8
MIB = 1024 * 1024
ANY = pl.BlockSpec(memory_space=pl.ANY)
HBM = pl.BlockSpec(memory_space=pltpu.HBM)
VMEM = pl.BlockSpec(memory_space=pltpu.VMEM)
SMEM = pl.BlockSpec(memory_space=pltpu.SMEM)


def in_hbm(value):
    return pltpu.with_memory_space_constraint(value, pltpu.HBM)


def pair_partner(i, count, odd):
    if not odd:
        return i ^ 1
    return (i + 1) % count if i % 2 else (i - 1) % count


def swap_pairs(value, axis, odd):
    count = lax.axis_size(axis)
    return lax.ppermute(value, axis, [(i, pair_partner(i, count, odd)) for i in range(count)])


def swap_panels(value, distance):
    n_lat = lax.axis_size("lat")
    pairs = [
        (p * n_lat + a, (1 - p) * n_lat + (a ^ distance)) for p in range(2) for a in range(n_lat)
    ]
    return lax.ppermute(value, ("panel", "lat"), pairs)


def window_of(run, cols):
    tiles = cols // LANES
    for width in range(1, tiles + 1):
        if all(
            start - min(start // LANES, tiles - width) * LANES + run <= width * LANES
            for start in range(0, cols, run)
        ):
            return width
    return tiles


def ask_kernel(partners, corners, blend, request, partners_box, corners_box, blend_box, sems):
    lat_len = corners.shape[-1] - request.shape[-1]
    copies = [
        pltpu.make_async_copy(partners, partners_box, sems.at[0]),
        pltpu.make_async_copy(corners, corners_box, sems.at[1]),
        pltpu.make_async_copy(blend, blend_box, sems.at[2]),
    ]
    for copy in copies:
        copy.start()
    for copy in copies:
        copy.wait()
    north = lax.axis_index("lat") == 0
    for row, source in ((0, partners_box), (1, corners_box)):
        values = source[0, 0].astype(jnp.float32)
        request[row : row + 1, 0:lat_len] = jnp.where(
            north, values[:, 0:lat_len], values[:, lat_len : 2 * lat_len]
        )
        request[row : row + 1, lat_len:] = values[:, 2 * lat_len :]
    weights = blend_box[0, 0, 0]
    request[2:6, 0:lat_len] = jnp.where(
        north, weights[:, 0:lat_len], weights[:, lat_len : 2 * lat_len]
    )
    request[2:6, lat_len:] = weights[:, 2 * lat_len :]


def ask(partners, corners, blend, rows, cols):
    return pl.pallas_call(
        ask_kernel,
        out_shape=jax.ShapeDtypeStruct((SUB, 2 * cols + 4 * rows), jnp.float32),
        in_specs=[HBM] * 3,
        out_specs=VMEM,
        scratch_shapes=[
            pltpu.VMEM(partners.shape, jnp.int32),
            pltpu.VMEM(corners.shape, jnp.int32),
            pltpu.VMEM(blend.shape, jnp.float32),
            pltpu.SemaphoreType.DMA((3,)),
        ],
        compiler_params=pltpu.CompilerParams(vmem_limit_bytes=MIB),
        name="ask",
    )(*(in_hbm(x) for x in (partners, corners, blend)))


def prepare_kernel(
    n_lat,
    n_lon,
    rows,
    rho,
    flow,
    heat,
    cells,
    block,
    even_rows,
    odd_rows,
    even_cols,
    odd_cols,
    row_box,
    spin_box,
):
    levels = rho.shape[1]
    cols = rho.shape[3]
    tiles = cols // LANES
    step = pl.program_id(0)

    def field_tile(field, row, tile):
        lanes = slice(tile * LANES, (tile + 1) * LANES)
        if field == 0:
            return rho[0, :, row, lanes]
        if field == 4:
            return heat[0, :, row, lanes]
        return flow[0, field - 1, :, row, lanes]

    for tile in range(tiles):
        lanes = slice(tile * LANES, (tile + 1) * LANES)
        block[0, tile] = rho[0, :, :, lanes]
        for part in range(3):
            block[1 + part, tile] = flow[0, part, :, :, lanes]
        block[4, tile] = heat[0, :, :, lanes]

    step_lat = math.pi / 2.0 / (rows * n_lat)
    step_lon = 1.5 * math.pi / (cols * n_lon)
    sub = lax.broadcasted_iota(jnp.int32, (SUB, LANES), 0)
    row_global = (lax.axis_index("lat") * rows + step * SUB + sub).astype(jnp.float32)
    theta = math.pi / 4.0 + (row_global + 0.5) * step_lat
    sin_lat, cos_lat = jnp.sin(theta), jnp.cos(theta)
    row_box[0] = 1.0 / sin_lat
    row_box[1] = cos_lat / sin_lat
    yang = lax.axis_index("panel").astype(jnp.float32)
    yin = 1.0 - yang
    for tile in range(tiles):
        lane = lax.broadcasted_iota(jnp.int32, (SUB, LANES), 1) + tile * LANES
        col_global = (lax.axis_index("lon") * cols + lane).astype(jnp.float32)
        longitude = -0.75 * math.pi + (col_global + 0.5) * step_lon
        sin_lon, cos_lon = jnp.sin(longitude), jnp.cos(longitude)
        spin_box[0, tile] = 2.0 * OMEGA * (yin * cos_lat + yang * sin_lat * sin_lon)
        spin_box[1, tile] = 2.0 * OMEGA * (yang * cos_lat * sin_lon - yin * sin_lat)
        spin_box[2, tile] = 2.0 * OMEGA * yang * cos_lon

    lat_even = lax.rem(lax.axis_index("lat"), 2) == 0
    for first, at, to_even in (
        (0, 0, jnp.logical_not(lat_even)),
        (SUB - 2, pl.num_programs(0) - 1, lat_even),
    ):
        for keep, out in ((to_even, even_rows), (jnp.logical_not(to_even), odd_rows)):

            @pl.when((step == at) & keep)
            def _(first=first, out=out):
                for layer in range(2):
                    for field in range(5):
                        for tile in range(tiles):
                            out[layer, field, tile] = field_tile(field, first + layer, tile)

    for row in range(SUB):
        for tile in range(tiles):
            stack = jnp.concatenate([field_tile(f, row, tile) for f in range(5)], axis=0)
            at = row * cols + tile * LANES
            cells[at : at + LANES, 0 : 5 * levels] = stack.T
    lon_even = lax.rem(lax.axis_index("lon"), 2) == 0
    for row in range(SUB):
        for layer in range(2):
            at = row * cols + layer
            west = cells[at : at + 1, :]
            at = row * cols + cols - 2 + layer
            east = cells[at : at + 1, :]
            even_cols[layer, row : row + 1, :] = jnp.where(lon_even, east, west)
            odd_cols[layer, row : row + 1, :] = jnp.where(lon_even, west, east)


def prepare(rho, flow, heat):
    levels, rows, cols = rho.shape[1:]
    column = jax.ShapeDtypeStruct((2, rows, LANES), jnp.float32)
    column_spec = pl.BlockSpec((2, SUB, LANES), lambda i: (0, i, 0))
    tiles = cols // LANES
    edge = jax.ShapeDtypeStruct((2, 5, tiles, levels, LANES), jnp.float32)
    edge_spec = pl.BlockSpec(edge.shape, lambda i: (0, 0, 0, 0, 0))
    return pl.pallas_call(
        functools.partial(
            prepare_kernel, lax.axis_size("lat"), lax.axis_size("lon"), rows
        ),
        grid=(rows // SUB,),
        out_shape=(
            jax.ShapeDtypeStruct((rows * cols, LANES), jnp.float32),
            jax.ShapeDtypeStruct((5, tiles, levels, rows + 2 * SUB, LANES), jnp.float32),
            edge,
            edge,
            column,
            column,
            jax.ShapeDtypeStruct((2, rows, LANES), jnp.float32),
            jax.ShapeDtypeStruct((3, tiles, rows, LANES), jnp.float32),
        ),
        in_specs=[
            pl.BlockSpec((1, levels, SUB, cols), lambda i: (0, 0, i, 0)),
            pl.BlockSpec((1, 3, levels, SUB, cols), lambda i: (0, 0, 0, i, 0)),
            pl.BlockSpec((1, levels, SUB, cols), lambda i: (0, 0, i, 0)),
        ],
        out_specs=(
            pl.BlockSpec((SUB * cols, LANES), lambda i: (i, 0)),
            pl.BlockSpec((5, tiles, levels, SUB, LANES), lambda i: (0, 0, 0, i + 1, 0)),
            edge_spec,
            edge_spec,
            column_spec,
            column_spec,
            pl.BlockSpec((2, SUB, LANES), lambda i: (0, i, 0)),
            pl.BlockSpec((3, tiles, SUB, LANES), lambda i: (0, 0, i, 0)),
        ),
        compiler_params=pltpu.CompilerParams(vmem_limit_bytes=12 * MIB),
        name="prepare",
    )(*(in_hbm(x) for x in (rho, flow, heat)))


def donate_kernel(n_lat, n_lon, rows, cols, field_rows, *refs):
    weights = refs[:n_lat]
    cells = refs[n_lat]
    replies = refs[n_lat + 1 : 2 * n_lat + 1]
    corners, turned, gathered, whole_box, requests, sems = refs[2 * n_lat + 1 :]
    copies = []
    for distance in range(n_lat):
        whole_box[distance] = weights[distance][...].astype(jnp.int32)
        copies.append(
            pltpu.make_async_copy(
                whole_box.at[distance], requests.at[distance], sems.at[distance]
            )
        )
        copies[-1].start()
    for copy in copies:
        copy.wait()
    lat_len, lon_len = 2 * cols, 2 * rows
    run_lat, run_lon = lat_len // n_lat, lon_len // n_lat
    tiles = cols // LANES
    width = window_of(run_lat, cols)
    lat_here = lax.axis_index("lat")
    lon_here = lax.axis_index("lon")

    def find_run(request, start, run):
        found = jnp.int32(0)
        for r in range(1, n_lat):
            match = requests[request, 0, start + r * run] == lat_here
            found = jnp.where(match, jnp.int32(r), found)
        return found

    def gather(request, first, count):
        def step(i, carry):
            for u in range(SUB):
                t = i * SUB + u
                cell = requests[request, 1, first + t]
                for j, shift in enumerate((0, cols, 1, cols + 1)):
                    corners[j, pl.ds(t, 1), :] = cells[pl.ds(cell + shift, 1), :]
            return carry

        lax.fori_loop(0, count // SUB, step, 0)

    def blend(first, count):
        rows_here = pl.ds(pl.multiple_of(first, SUB), count)
        total = None
        for j in range(4):
            weight = jnp.broadcast_to(turned[rows_here, 2 + j : 3 + j], (count, LANES))
            part = weight * corners[j, 0:count, :]
            total = part if total is None else total + part
        return total

    for distance in range(n_lat):
        request, reply = distance, replies[distance]
        asker = jnp.bitwise_xor(lat_here, distance)

        @pl.when((asker == 0) | (asker == n_lat - 1))
        def _(distance=distance, request=request, reply=reply):
            for at in range(0, lat_len, LANES):
                turned[at : at + LANES, 0:SUB] = weights[distance][:, at : at + LANES].T
            run = find_run(request, 0, run_lat)
            start = lax.rem(run * run_lat, cols)
            base = jnp.minimum(lax.div(start, LANES), tiles - width)
            offset = pl.multiple_of(start - base * LANES, SUB)
            gather(request, run * run_lat, run_lat)
            gathered[pl.ds(offset, run_lat), :] = blend(run * run_lat, run_lat)
            for tile in range(width):
                block = gathered[tile * LANES : (tile + 1) * LANES, :]
                reply[0:field_rows, tile * LANES : (tile + 1) * LANES] = block.T[0:field_rows]

        @pl.when((lon_here == 0) | (lon_here == n_lon - 1))
        def _(distance=distance, request=request, reply=reply):
            for at in range(lat_len, lat_len + 2 * lon_len, LANES):
                turned[at : at + LANES, 0:SUB] = weights[distance][:, at : at + LANES].T
            first = lat_len + jnp.where(lon_here == 0, 0, lon_len)
            run = find_run(request, first, run_lon)
            gather(request, first + run * run_lon, run_lon)
            reply[field_rows : field_rows + run_lon, 0:LANES] = blend(
                first + run * run_lon, run_lon
            )


def donate(requests, cells, rows, cols, field_rows):
    n_lat, n_lon = lax.axis_size("lat"), lax.axis_size("lon")
    run_lat = 2 * cols // n_lat
    width = window_of(run_lat, cols)
    reply = jax.ShapeDtypeStruct((field_rows + 2 * rows // n_lat, width * LANES), jnp.float32)
    return pl.pallas_call(
        functools.partial(donate_kernel, n_lat, n_lon, rows, cols, field_rows),
        out_shape=(reply,) * n_lat,
        in_specs=[VMEM] * (n_lat + 1),
        out_specs=(VMEM,) * n_lat,
        scratch_shapes=[
            pltpu.VMEM((4, max(run_lat, 2 * rows // n_lat), LANES), jnp.float32),
            pltpu.VMEM((requests[0].shape[1], LANES), jnp.float32),
            pltpu.VMEM((width * LANES, LANES), jnp.float32),
            pltpu.VMEM((n_lat,) + requests[0].shape, jnp.int32),
            pltpu.SMEM((n_lat,) + requests[0].shape, jnp.int32),
            pltpu.SemaphoreType.DMA((n_lat,)),
        ],
        compiler_params=pltpu.CompilerParams(vmem_limit_bytes=9 * MIB),
        name="donate",
    )(*requests, cells)


def stencil_kernel(geometry, chunk, *refs):
    n_lat, n_lon, levels, rows, cols = geometry
    tiles = cols // LANES
    field_rows = 5 * levels
    partners, turning = refs[:2]
    reply_box = refs[2 : 2 + n_lat]
    (
        lon_even,
        lon_odd,
        lat_even,
        lat_odd,
        block,
        row_box,
        spin_box,
        outset,
        rate_out,
        state_out,
        rate_box,
        state_box,
        replies,
        halo,
        side,
        mixed,
        out_sems,
    ) = refs[2 + n_lat :]
    lat_here = lax.axis_index("lat")
    lon_here = lax.axis_index("lon")
    lat_len, lon_len = 2 * cols, 2 * rows
    run_lat, run_lon = lat_len // n_lat, lon_len // n_lat
    width = window_of(run_lat, cols)
    step_lat = math.pi / 2.0 / (rows * n_lat)
    step_lon = 1.5 * math.pi / (cols * n_lon)
    chunks = levels // chunk
    groups = ((0, rows),)

    def out_copies(c):
        span = pl.ds(c * chunk, chunk)
        return (
            pltpu.make_async_copy(
                rate_box.at[:, span], rate_out.at[0, :, span], out_sems.at[c, 0]
            ),
            pltpu.make_async_copy(
                state_box.at[:, span], state_out.at[0, :, span], out_sems.at[c, 1]
            ),
        )

    lat_is_even = lax.rem(lat_here, 2) == 0
    lon_is_even = lax.rem(lon_here, 2) == 0
    for even, north, south in ((True, lat_odd, lat_even), (False, lat_even, lat_odd)):

        @pl.when(lat_is_even == even)
        def _(north=north, south=south):
            halo[0] = north[...]
            halo[1] = south[...]

    for even, west, east in ((True, lon_odd, lon_even), (False, lon_even, lon_odd)):

        @pl.when(lon_is_even == even)
        def _(west=west, east=east):
            side[0] = west[...]
            side[1] = east[...]

    @pl.when((lat_here == 0) | (lat_here == n_lat - 1) | (lon_here == 0) | (lon_here == n_lon - 1))
    def _():
        for d in range(n_lat):
            replies[d] = reply_box[d][...]

    lane8 = lax.broadcasted_iota(jnp.int32, (SUB, LANES), 1)
    sub8 = lax.broadcasted_iota(jnp.int32, (SUB, LANES), 0)

    for which, slot0 in ((0, 0), (1, lat_len)):

        @pl.when(lat_here == (0 if which == 0 else n_lat - 1))
        def _(which=which, slot0=slot0):
            sources = [
                jnp.bitwise_xor(partners[0, 0, 0, slot0 + r * run_lat], lat_here) for r in range(n_lat)
            ]
            for layer in range(2):
                for t in range(tiles):
                    lane = lax.broadcasted_iota(jnp.int32, (field_rows, LANES), 1) + t * LANES
                    value = None
                    for r in range(n_lat):
                        first = r * run_lat - layer * cols
                        if first < 0 or first >= cols:
                            continue
                        if first >= (t + 1) * LANES or first + run_lat <= t * LANES:
                            continue
                        base = min(first // LANES, tiles - width)
                        here = (t - base) * LANES
                        piece = replies[sources[r], 0:field_rows, here : here + LANES]
                        value = piece if value is None else jnp.where(lane >= first, piece, value)
                    spot = slot0 + layer * cols + t * LANES
                    cosine = turning[0, 0, 0, 0:1, spot : spot + LANES]
                    sine = turning[0, 0, 0, 1:2, spot : spot + LANES]
                    parts = [value[f * levels : (f + 1) * levels] for f in range(5)]
                    parts[2], parts[3] = (
                        cosine * parts[2] + sine * parts[3],
                        cosine * parts[3] - sine * parts[2],
                    )
                    for f in range(5):
                        halo[which, layer, f, t] = parts[f]

    turn_lon = jnp.concatenate(
        [turning[0, 0, 0, :, 2 * lat_len :], jnp.zeros((SUB - 2, 2 * lon_len), jnp.float32)], axis=0
    ).T

    for which, slot0 in ((0, 2 * lat_len), (1, 2 * lat_len + lon_len)):
        @pl.when(lon_here == (0 if which == 0 else n_lon - 1))
        def _(which=which, slot0=slot0):
            lane = lax.broadcasted_iota(jnp.int32, (run_lon, LANES), 1)
            is_lat = (lane >= 2 * levels) & (lane < 3 * levels)
            is_lon = (lane >= 3 * levels) & (lane < 4 * levels)
            for r in range(n_lat):
                source = jnp.bitwise_xor(partners[0, 0, 0, slot0 + r * run_lon], lat_here)
                layer, first = r * run_lon // rows, r * run_lon % rows
                value = replies[source, field_rows : field_rows + run_lon, 0:LANES]
                slots = slice(which * lon_len + r * run_lon, which * lon_len + (r + 1) * run_lon)
                cosine = jnp.broadcast_to(turn_lon[slots, 0:1], (run_lon, LANES))
                sine = jnp.broadcast_to(turn_lon[slots, 1:2], (run_lon, LANES))
                later = pltpu.roll(value, LANES - levels, 1)
                earlier = pltpu.roll(value, levels, 1)
                value = jnp.where(
                    is_lat,
                    cosine * value + sine * later,
                    jnp.where(is_lon, cosine * value - sine * earlier, value),
                )
                side[which, layer, first : first + run_lon] = value

    lane_all = lax.broadcasted_iota(jnp.int32, (rows, LANES), 1)
    columns = [side[1, 0], side[1, 1], side[0, 0], side[0, 1]]
    columns = [columns[0]] + [pltpu.roll(columns[j], j, 1) for j in range(1, 4)]
    for q in range(4):
        pick = jnp.bitwise_and(lane_all - q, 3)
        value = columns[0]
        for j in range(1, 4):
            value = jnp.where(pick == j, columns[j], value)
        for first, count in groups:
            span = slice(first, first + count)
            for row in range(q, field_rows, 4):
                mixed[row // levels, row % levels, span] = pltpu.roll(
                    value[span], LANES - 2 - row, 1
                )

    by_lat = 1.0 / (12.0 * step_lat)
    by_lon = 1.0 / (12.0 * step_lon)

    def one_level(k):
        below = jnp.maximum(k - 1, 0)
        above = jnp.minimum(k + 1, levels - 1)
        radius = jnp.broadcast_to(
            1.0 / step_lat + k.astype(jnp.float32), (SUB, LANES)
        )
        inv_radius = 1.0 / radius
        lat_scale = inv_radius * by_lat
        for first, count in groups:
            for top in range(first, first + count, SUB):
                one_strip(k, below, above, inv_radius, lat_scale, top)

    def one_strip(k, below, above, inv_radius, lat_scale, top):
        strip = slice(top, top + SUB)
        inv_sin, cot = row_box[0, strip], row_box[1, strip]
        inv_arc = inv_radius * inv_sin
        lon_scale = inv_arc * by_lon
        cot_r = cot * inv_radius
        two_r = 2.0 * inv_radius
        curve_lat = (VISCOSITY / (12.0 * step_lat * step_lat)) * inv_radius * inv_radius
        curve_lon = (VISCOSITY / (12.0 * step_lon * step_lon)) * inv_arc * inv_arc
        slope_extra = (VISCOSITY * by_lat) * inv_radius * cot_r
        radial_extra = VISCOSITY * inv_radius
        center_weight = 2.0 * VISCOSITY + 30.0 * (curve_lat + curve_lon)
        north, south = top == 0, top == rows - SUB

        def derive(f, full):
            here = [block[f, t, k, SUB + top : 2 * SUB + top] for t in range(tiles)]
            ghost = mixed[f, k, strip]
            ghost_w, ghost_e = pltpu.roll(ghost, LANES - 1, 1), pltpu.roll(ghost, 1, 1)
            w1s = [pltpu.roll(x, 1, 1) for x in here]
            w2s = [pltpu.roll(x, 2, 1) for x in here]
            e1s = [pltpu.roll(x, LANES - 1, 1) for x in here]
            e2s = [pltpu.roll(x, LANES - 2, 1) for x in here]
            out = []
            for t in range(tiles):
                at = SUB + top
                n1, n2 = block[f, t, k, at - 1 : at + 7], block[f, t, k, at - 2 : at + 6]
                s1, s2 = block[f, t, k, at + 1 : at + 9], block[f, t, k, at + 2 : at + 10]
                if north:
                    g2 = jnp.broadcast_to(halo[0, 0, f, t, pl.ds(k, 1), :], (SUB, LANES))
                    g1 = jnp.broadcast_to(halo[0, 1, f, t, pl.ds(k, 1), :], (SUB, LANES))
                    n1 = jnp.where(sub8 == 0, g1, n1)
                    n2 = jnp.where(sub8 == 0, g2, jnp.where(sub8 == 1, g1, n2))
                if south:
                    g1 = jnp.broadcast_to(halo[1, 0, f, t, pl.ds(k, 1), :], (SUB, LANES))
                    g2 = jnp.broadcast_to(halo[1, 1, f, t, pl.ds(k, 1), :], (SUB, LANES))
                    s1 = jnp.where(sub8 == SUB - 1, g1, s1)
                    s2 = jnp.where(sub8 == SUB - 1, g2, jnp.where(sub8 == SUB - 2, g1, s2))
                w1 = jnp.where(lane8 == 0, w1s[t - 1] if t else ghost_w, w1s[t])
                w2 = jnp.where(lane8 < 2, w2s[t - 1] if t else ghost, w2s[t])
                last = t == tiles - 1
                e1 = jnp.where(lane8 == LANES - 1, ghost_e if last else e1s[t + 1], e1s[t])
                e2 = jnp.where(lane8 >= LANES - 2, ghost if last else e2s[t + 1], e2s[t])
                low = block[f, t, below, SUB + top : 2 * SUB + top]
                high = block[f, t, above, SUB + top : 2 * SUB + top]
                rad = high - low
                lat = 8.0 * (s1 - n1) - (s2 - n2)
                lon = 8.0 * (e1 - w1) - (e2 - w2)
                bend = None
                if full:
                    bend = (
                        VISCOSITY * (high + low)
                        + curve_lat * (16.0 * (s1 + n1) - (s2 + n2))
                        + curve_lon * (16.0 * (e1 + w1) - (e2 + w2))
                        - center_weight * here[t]
                    )
                out.append((rad, lat, lon, bend))
            return here, out

        wind_rad = [block[1, t, k, SUB + top : 2 * SUB + top] for t in range(tiles)]
        wind_lat = [block[2, t, k, SUB + top : 2 * SUB + top] for t in range(tiles)]
        wind_lon = [block[3, t, k, SUB + top : 2 * SUB + top] for t in range(tiles)]
        go_rad = [0.5 * x for x in wind_rad]
        go_lat = [lat_scale * x for x in wind_lat]
        go_lon = [lon_scale * x for x in wind_lon]

        def put(f, t, center, rate):
            lanes = slice(t * LANES, (t + 1) * LANES)
            rate_box[f, k, strip, lanes] = rate
            state_box[f, k, strip, lanes] = (
                0.75 * outset[0, f, k, strip, lanes] + 0.25 * center
            ) + (0.25 * TIME_STEP) * rate

        rho_here, rho_d = derive(0, False)
        heat_here, heat_d = derive(4, True)
        ratio = [heat_here[t] / rho_here[t] for t in range(tiles)]
        press, rho_rate, heat_rate = [], [], []
        for t in range(tiles):
            (a, b, c, _), (d, e, g, bend) = rho_d[t], heat_d[t]
            press.append(
                (
                    0.5 * (ratio[t] * a + d),
                    lat_scale * (ratio[t] * b + e),
                    lon_scale * (ratio[t] * c + g),
                )
            )
            rho_rate.append(go_rad[t] * a + go_lat[t] * b + go_lon[t] * c)
            heat_rate.append(
                bend
                + (radial_extra - go_rad[t]) * d
                + (slope_extra - go_lat[t]) * e
                - go_lon[t] * g
            )
        diverge = [two_r * wind_rad[t] + cot_r * wind_lat[t] for t in range(tiles)]
        for f in (1, 2, 3):
            here, d_all = derive(f, True)
            for t in range(tiles):
                d, e, g, bend = d_all[t]
                spin_rad, spin_lat = spin_box[0, t, strip], spin_box[1, t, strip]
                spin_lon = spin_box[2, t, strip]
                rate = (
                    bend
                    + (radial_extra - go_rad[t]) * d
                    + (slope_extra - go_lat[t]) * e
                    - go_lon[t] * g
                    - press[t][f - 1]
                )
                if f == 1:
                    diverge[t] += 0.5 * d
                    rate += inv_radius * (wind_lat[t] * wind_lat[t] + wind_lon[t] * wind_lon[t])
                    rate += spin_lon * wind_lat[t] - spin_lat * wind_lon[t] - GRAVITY
                elif f == 2:
                    diverge[t] += lat_scale * e
                    rate += cot_r * (wind_lon[t] * wind_lon[t])
                    rate -= inv_radius * (wind_rad[t] * wind_lat[t])
                    rate += spin_rad * wind_lon[t] - spin_lon * wind_rad[t]
                else:
                    diverge[t] += lon_scale * g
                    rate -= (inv_radius * wind_rad[t] + cot_r * wind_lat[t]) * wind_lon[t]
                    rate += spin_lat * wind_rad[t] - spin_rad * wind_lat[t]
                put(f, t, here[t], rate)
        for t in range(tiles):
            put(0, t, rho_here[t], -rho_rate[t] - rho_here[t] * diverge[t])
            put(
                4,
                t,
                heat_here[t],
                heat_rate[t] - (GAMMA - 1.0) * (heat_here[t] * diverge[t]),
            )

    for c in range(chunks):
        @pl.loop(c * chunk, (c + 1) * chunk)
        def _(k):
            one_level(k)

        for copy in out_copies(c):
            copy.start()
    for c in range(chunks):
        for copy in out_copies(c):
            copy.wait()


def stencil(partners, turning, replies, sides, halos, block, row_box, spin_box, outset):
    levels, rows, cols = outset.shape[2:]
    n_lat, n_lon = lax.axis_size("lat"), lax.axis_size("lon")
    chunk = 4
    out = jax.ShapeDtypeStruct(outset.shape, jnp.float32)
    box = pltpu.VMEM(outset.shape[1:], jnp.float32)
    return pl.pallas_call(
        functools.partial(stencil_kernel, (n_lat, n_lon, levels, rows, cols), chunk),
        out_shape=(out, out),
        in_specs=[SMEM] + [VMEM] * (n_lat + 9),
        out_specs=(ANY, ANY),
        scratch_shapes=[
            box,
            box,
            pltpu.VMEM((n_lat,) + replies[0].shape, jnp.float32),
            pltpu.VMEM((2,) + halos[0].shape, jnp.float32),
            pltpu.VMEM((2, 2, rows, LANES), jnp.float32),
            pltpu.VMEM((5, levels, rows, LANES), jnp.float32),
            pltpu.SemaphoreType.DMA((levels // chunk, 2)),
        ],
        compiler_params=pltpu.CompilerParams(vmem_limit_bytes=25 * MIB),
        cost_estimate=pl.CostEstimate(
            flops=250 * levels * rows * cols,
            bytes_accessed=80 * levels * rows * cols,
            transcendentals=0,
        ),
        name="stencil",
    )(partners, turning, *replies, *sides, *halos, block, row_box, spin_box, outset)


def shards(rho, flow, heat, outset, opposite_block, donor_lower_corner, blend, turning):
    levels, rows, cols = rho.shape[1:]
    n_lat = lax.axis_size("lat")
    request = ask(opposite_block, donor_lower_corner, blend, rows, cols)
    requests = [swap_panels(request, d) for d in range(n_lat)]
    cells, block, even_rows, odd_rows, even_cols, odd_cols, row_box, spin_box = prepare(
        rho, flow, heat
    )
    *requests, even_rows, odd_rows, even_cols, odd_cols = lax.optimization_barrier(
        (*requests, even_rows, odd_rows, even_cols, odd_cols)
    )
    sides = (swap_pairs(even_cols, "lon", False), swap_pairs(odd_cols, "lon", True))
    halos = (swap_pairs(even_rows, "lat", False), swap_pairs(odd_rows, "lat", True))
    replies = donate(requests, cells, rows, cols, 5 * levels)
    replies = [swap_panels(reply, d) for d, reply in enumerate(replies)]
    return stencil(
        opposite_block, turning, replies, sides, halos, block, row_box, spin_box, outset
    )


def solution(mesh):
    in_specs = (
        P("panel", None, "lat", "lon"),
        P("panel", None, None, "lat", "lon"),
        P("panel", None, "lat", "lon"),
        P("panel", None, None, "lat", "lon"),
        P("panel", "lat", "lon", None),
        P("panel", "lat", "lon", None),
        P("panel", "lat", "lon", None, None),
        P("panel", "lat", "lon", None, None),
    )
    out_specs = (P("panel", None, None, "lat", "lon"), P("panel", None, None, "lat", "lon"))
    return jax.shard_map(shards, mesh=mesh, in_specs=in_specs, out_specs=out_specs, check_vma=False)
```

```python
import functools
import math

import jax
import jax.numpy as jnp
from jax import lax
from jax.experimental import pallas as pl
from jax.experimental.pallas import tpu as pltpu
from jax.sharding import PartitionSpec as P

OMEGA = 0.5
GRAVITY = 1.0
VISCOSITY = 0.2
DIFFUSIVITY = 0.2
GAMMA = 1.4
TIME_STEP = 0.05
LANES = 128
SUB = 8
MIB = 1024 * 1024
ANY = pl.BlockSpec(memory_space=pl.ANY)
HBM = pl.BlockSpec(memory_space=pltpu.HBM)
VMEM = pl.BlockSpec(memory_space=pltpu.VMEM)
SMEM = pl.BlockSpec(memory_space=pltpu.SMEM)


def in_hbm(value):
    return pltpu.with_memory_space_constraint(value, pltpu.HBM)


def pair_partner(i, count, odd):
    if not odd:
        return i ^ 1
    return (i + 1) % count if i % 2 else (i - 1) % count


def swap_pairs(value, axis, odd):
    count = lax.axis_size(axis)
    return lax.ppermute(value, axis, [(i, pair_partner(i, count, odd)) for i in range(count)])


def swap_panels(value, distance):
    n_lat = lax.axis_size("lat")
    pairs = [
        (p * n_lat + a, (1 - p) * n_lat + (a ^ distance)) for p in range(2) for a in range(n_lat)
    ]
    return lax.ppermute(value, ("panel", "lat"), pairs)


def window_of(run, cols):
    tiles = cols // LANES
    for width in range(1, tiles + 1):
        if all(
            start - min(start // LANES, tiles - width) * LANES + run <= width * LANES
            for start in range(0, cols, run)
        ):
            return width
    return tiles


def ask_kernel(partners, corners, blend, request, partners_box, corners_box, blend_box, sems):
    lat_len = corners.shape[-1] - request.shape[-1]
    copies = [
        pltpu.make_async_copy(partners, partners_box, sems.at[0]),
        pltpu.make_async_copy(corners, corners_box, sems.at[1]),
        pltpu.make_async_copy(blend, blend_box, sems.at[2]),
    ]
    for copy in copies:
        copy.start()
    for copy in copies:
        copy.wait()
    north = lax.axis_index("lat") == 0
    for row, source in ((0, partners_box), (1, corners_box)):
        values = source[0, 0].astype(jnp.float32)
        request[row : row + 1, 0:lat_len] = jnp.where(
            north, values[:, 0:lat_len], values[:, lat_len : 2 * lat_len]
        )
        request[row : row + 1, lat_len:] = values[:, 2 * lat_len :]
    weights = blend_box[0, 0, 0]
    request[2:6, 0:lat_len] = jnp.where(
        north, weights[:, 0:lat_len], weights[:, lat_len : 2 * lat_len]
    )
    request[2:6, lat_len:] = weights[:, 2 * lat_len :]


def ask(partners, corners, blend, rows, cols):
    return pl.pallas_call(
        ask_kernel,
        out_shape=jax.ShapeDtypeStruct((SUB, 2 * cols + 4 * rows), jnp.float32),
        in_specs=[HBM] * 3,
        out_specs=VMEM,
        scratch_shapes=[
            pltpu.VMEM(partners.shape, jnp.int32),
            pltpu.VMEM(corners.shape, jnp.int32),
            pltpu.VMEM(blend.shape, jnp.float32),
            pltpu.SemaphoreType.DMA((3,)),
        ],
        compiler_params=pltpu.CompilerParams(vmem_limit_bytes=MIB),
        name="ask",
    )(*(in_hbm(x) for x in (partners, corners, blend)))


def prepare_kernel(
    n_lat,
    n_lon,
    rho,
    flow,
    heat,
    cells,
    block,
    even_rows,
    odd_rows,
    even_cols,
    odd_cols,
    row_box,
    spin_box,
    staged,
    sems,
):
    levels, rows, cols = rho.shape[1:]
    tiles = cols // LANES
    strips = rows // SUB

    def load_copies(strip):
        here = pl.ds(strip * SUB, SUB)
        return (
            pltpu.make_async_copy(rho.at[0, :, here], staged.at[0, :, here], sems.at[strip, 0]),
            pltpu.make_async_copy(
                flow.at[0, :, :, here], staged.at[pl.ds(1, 3), :, here], sems.at[strip, 1]
            ),
            pltpu.make_async_copy(heat.at[0, :, here], staged.at[4, :, here], sems.at[strip, 2]),
        )

    for strip in range(strips):
        for copy in load_copies(strip):
            copy.start()

    zero = jnp.zeros((levels, SUB, LANES), jnp.float32)
    for field in range(5):
        for tile in range(tiles):
            block[field, tile, :, 0:SUB] = zero
            block[field, tile, :, rows + SUB :] = zero

    step_lat = math.pi / 2.0 / (rows * n_lat)
    step_lon = 1.5 * math.pi / (cols * n_lon)
    sub = lax.broadcasted_iota(jnp.int32, (rows, LANES), 0)
    row_global = (lax.axis_index("lat") * rows + sub).astype(jnp.float32)
    theta = math.pi / 4.0 + (row_global + 0.5) * step_lat
    sin_lat, cos_lat = jnp.sin(theta), jnp.cos(theta)
    row_box[0] = 1.0 / sin_lat
    row_box[1] = cos_lat / sin_lat
    yang = lax.axis_index("panel").astype(jnp.float32)
    yin = 1.0 - yang
    for tile in range(tiles):
        lane = lax.broadcasted_iota(jnp.int32, (SUB, LANES), 1) + tile * LANES
        col_global = (lax.axis_index("lon") * cols + lane).astype(jnp.float32)
        longitude = -0.75 * math.pi + (col_global + 0.5) * step_lon
        sin_lon, cos_lon = jnp.sin(longitude)[0:1], jnp.cos(longitude)[0:1]
        spin_box[0, tile] = 2.0 * OMEGA * (yin * cos_lat + yang * sin_lat * sin_lon)
        spin_box[1, tile] = 2.0 * OMEGA * (yang * cos_lat * sin_lon - yin * sin_lat)
        spin_box[2, tile] = jnp.broadcast_to(2.0 * OMEGA * yang * cos_lon, (rows, LANES))

    for strip in range(strips):
        for copy in load_copies(strip):
            copy.wait()

        here, there = strip * SUB, (strip + 1) * SUB
        for field in range(5):
            for tile in range(tiles):
                block[field, tile, :, there : there + SUB] = staged[
                    field, :, here:there, tile * LANES : (tile + 1) * LANES
                ]
        for row in range(here, there):
            for tile in range(tiles):
                stack = jnp.concatenate(
                    [
                        staged[f, :, row, tile * LANES : (tile + 1) * LANES] for f in range(5)
                    ],
                    axis=0,
                )
                at = row * cols + tile * LANES
                cells[at : at + LANES, 0 : 5 * levels] = stack.T

    lat_even = lax.rem(lax.axis_index("lat"), 2) == 0
    for first, to_even in ((0, jnp.logical_not(lat_even)), (rows - 2, lat_even)):
        for keep, out in ((to_even, even_rows), (jnp.logical_not(to_even), odd_rows)):

            @pl.when(keep)
            def _(first=first, out=out):
                for layer in range(2):
                    for field in range(5):
                        for tile in range(tiles):
                            out[layer, field, tile] = block[field, tile, :, SUB + first + layer, :]

    lon_even = lax.rem(lax.axis_index("lon"), 2) == 0
    for first, to_even in ((0, jnp.logical_not(lon_even)), (cols - 2, lon_even)):
        for keep, out in ((to_even, even_cols), (jnp.logical_not(to_even), odd_cols)):

            @pl.when(keep)
            def _(first=first, out=out):
                for layer in range(2):
                    for row in range(rows):
                        at = row * cols + first + layer
                        out[layer, row : row + 1, :] = cells[at : at + 1, :]


def prepare(rho, flow, heat):
    levels, rows, cols = rho.shape[1:]
    tiles = cols // LANES
    shapes = (
        (rows * cols, LANES),
        (5, tiles, levels, rows + 2 * SUB, LANES),
        (2, 5, tiles, levels, LANES),
        (2, 5, tiles, levels, LANES),
        (2, rows, LANES),
        (2, rows, LANES),
        (2, rows, LANES),
        (3, tiles, rows, LANES),
    )
    return pl.pallas_call(
        functools.partial(prepare_kernel, lax.axis_size("lat"), lax.axis_size("lon")),
        out_shape=tuple(jax.ShapeDtypeStruct(shape, jnp.float32) for shape in shapes),
        in_specs=[ANY] * 3,
        out_specs=(VMEM,) * len(shapes),
        scratch_shapes=[
            pltpu.VMEM((5, levels, rows, cols), jnp.float32),
            pltpu.SemaphoreType.DMA((rows // SUB, 3)),
        ],
        compiler_params=pltpu.CompilerParams(vmem_limit_bytes=16 * MIB),
        name="prepare",
    )(*(in_hbm(x) for x in (rho, flow, heat)))


def donate_kernel(n_lat, n_lon, rows, cols, field_rows, *refs):
    weights = refs[:n_lat]
    cells = refs[n_lat]
    replies = refs[n_lat + 1 : 2 * n_lat + 1]
    corners, turned, gathered, whole_box, requests, sems = refs[2 * n_lat + 1 :]
    slots = weights[0].shape[1]
    for distance in range(n_lat):
        for row in range(2):
            for tile in range(slots // LANES):
                lanes = slice(tile * LANES, (tile + 1) * LANES)
                whole_box[distance, row, tile : tile + 1] = weights[distance][
                    row : row + 1, lanes
                ].astype(jnp.int32)
    copy = pltpu.make_async_copy(whole_box, requests, sems.at[0])
    copy.start()
    for distance in range(n_lat):
        for at in range(0, slots, LANES):
            turned[distance, at : at + LANES, 0:SUB] = weights[distance][:, at : at + LANES].T
    copy.wait()
    lat_len, lon_len = 2 * cols, 2 * rows
    run_lat, run_lon = lat_len // n_lat, lon_len // n_lat
    tiles = cols // LANES
    width = window_of(run_lat, cols)
    lat_here = lax.axis_index("lat")
    lon_here = lax.axis_index("lon")

    def word(request, row, slot):
        return requests[request, row, lax.shift_right_logical(slot, 7), jnp.bitwise_and(slot, 127)]

    def find_run(request, start, run):
        start = jnp.int32(start)
        found = jnp.int32(0)
        for r in range(1, n_lat):
            match = word(request, 0, start + r * run) == lat_here
            found = jnp.where(match, jnp.int32(r), found)
        return found

    def gather(request, first, count):
        def step(i, carry):
            for u in range(SUB):
                t = i * SUB + u
                cell = word(request, 1, first + t)
                for j, shift in enumerate((0, cols, 1, cols + 1)):
                    corners[j, pl.ds(t, 1), :] = cells[pl.ds(cell + shift, 1), :]
            return carry

        lax.fori_loop(0, count // SUB, step, 0)

    def blend(distance, first, count):
        rows_here = pl.ds(pl.multiple_of(first, SUB), count)
        total = None
        for j in range(4):
            weight = jnp.broadcast_to(turned[distance, rows_here, 2 + j : 3 + j], (count, LANES))
            part = weight * corners[j, 0:count, :]
            total = part if total is None else total + part
        return total

    for distance in range(n_lat):
        request, reply = distance, replies[distance]
        asker = jnp.bitwise_xor(lat_here, distance)

        @pl.when((asker == 0) | (asker == n_lat - 1))
        def _(distance=distance, request=request, reply=reply):
            run = find_run(request, 0, run_lat)
            start = lax.rem(run * run_lat, cols)
            base = jnp.minimum(lax.div(start, LANES), tiles - width)
            offset = pl.multiple_of(start - base * LANES, SUB)
            gather(request, run * run_lat, run_lat)
            gathered[pl.ds(offset, run_lat), :] = blend(distance, run * run_lat, run_lat)
            for tile in range(width):
                block = gathered[tile * LANES : (tile + 1) * LANES, :]
                reply[0:field_rows, tile * LANES : (tile + 1) * LANES] = block.T[0:field_rows]

        @pl.when((lon_here == 0) | (lon_here == n_lon - 1))
        def _(distance=distance, request=request, reply=reply):
            first = lat_len + jnp.where(lon_here == 0, 0, lon_len)
            run = find_run(request, first, run_lon)
            gather(request, first + run * run_lon, run_lon)
            reply[field_rows : field_rows + run_lon, 0:LANES] = blend(
                distance, first + run * run_lon, run_lon
            )


def donate(requests, cells, rows, cols, field_rows):
    n_lat, n_lon = lax.axis_size("lat"), lax.axis_size("lon")
    run_lat = 2 * cols // n_lat
    width = window_of(run_lat, cols)
    slots = requests[0].shape[1]
    words = (pl.cdiv(slots, SUB * LANES) * SUB, LANES)
    reply = jax.ShapeDtypeStruct((field_rows + 2 * rows // n_lat, width * LANES), jnp.float32)
    return pl.pallas_call(
        functools.partial(donate_kernel, n_lat, n_lon, rows, cols, field_rows),
        out_shape=(reply,) * n_lat,
        in_specs=[VMEM] * (n_lat + 1),
        out_specs=(VMEM,) * n_lat,
        scratch_shapes=[
            pltpu.VMEM((4, max(run_lat, 2 * rows // n_lat), LANES), jnp.float32),
            pltpu.VMEM((n_lat, slots, LANES), jnp.float32),
            pltpu.VMEM((width * LANES, LANES), jnp.float32),
            pltpu.VMEM((n_lat, 2) + words, jnp.int32),
            pltpu.SMEM((n_lat, 2) + words, jnp.int32),
            pltpu.SemaphoreType.DMA((1,)),
        ],
        compiler_params=pltpu.CompilerParams(vmem_limit_bytes=9 * MIB),
        name="donate",
    )(*requests, cells)


def core_parts(rows, tiles):
    return (SUB, rows - 2 * SUB, LANES, (tiles - 2) * LANES)


def edge_parts(rows, tiles):
    cols = tiles * LANES
    return (
        (0, SUB, 0, cols),
        (rows - SUB, SUB, 0, cols),
        (SUB, rows - 2 * SUB, 0, LANES),
        (SUB, rows - 2 * SUB, cols - LANES, LANES),
    )


def part_copies(boxes, outs, part, span, sems):
    first, count, lane, lanes = part
    at = (span, pl.ds(first, count), pl.ds(lane, lanes))
    return [
        pltpu.make_async_copy(box.at[(slice(None),) + at], out.at[(0, slice(None)) + at], sems.at[n])
        for n, (box, out) in enumerate(zip(boxes, outs))
    ]


def stencil_kernel(
    geometry, chunk, block, row_box, spin_box, outset, rate_out, state_out, rate_box, state_box, sems
):
    n_lat, n_lon, levels, rows, cols = geometry
    tiles = cols // LANES
    step_lat = math.pi / 2.0 / (rows * n_lat)
    step_lon = 1.5 * math.pi / (cols * n_lon)
    chunks = levels // chunk
    by_lat = 1.0 / (12.0 * step_lat)
    by_lon = 1.0 / (12.0 * step_lon)
    lane8 = lax.broadcasted_iota(jnp.int32, (SUB, LANES), 1)

    def out_copies(c):
        return part_copies(
            (rate_box, state_box),
            (rate_out, state_out),
            core_parts(rows, tiles),
            pl.ds(c * chunk, chunk),
            sems.at[c],
        )

    def one_level(k):
        below = jnp.maximum(k - 1, 0)
        above = jnp.minimum(k + 1, levels - 1)
        radius = jnp.broadcast_to(1.0 / step_lat + k.astype(jnp.float32), (SUB, LANES))
        inv_radius = 1.0 / radius
        for top in range(0, rows, SUB):
            one_strip(k, below, above, inv_radius, inv_radius * by_lat, top)

    def one_strip(k, below, above, inv_radius, lat_scale, top):
        strip = slice(top, top + SUB)
        inv_sin, cot = row_box[0, strip], row_box[1, strip]
        inv_arc = inv_radius * inv_sin
        lon_scale = inv_arc * by_lon
        cot_r = cot * inv_radius
        two_r = 2.0 * inv_radius
        curve_lat = (VISCOSITY / (12.0 * step_lat * step_lat)) * inv_radius * inv_radius
        curve_lon = (VISCOSITY / (12.0 * step_lon * step_lon)) * inv_arc * inv_arc
        slope_extra = (VISCOSITY * by_lat) * inv_radius * cot_r
        radial_extra = VISCOSITY * inv_radius
        center_weight = 2.0 * VISCOSITY + 30.0 * (curve_lat + curve_lon)

        def derive(f, full):
            here = [block[f, t, k, SUB + top : 2 * SUB + top] for t in range(tiles)]
            w1s = [pltpu.roll(x, 1, 1) for x in here]
            w2s = [pltpu.roll(x, 2, 1) for x in here]
            e1s = [pltpu.roll(x, LANES - 1, 1) for x in here]
            e2s = [pltpu.roll(x, LANES - 2, 1) for x in here]
            out = []
            for t in range(tiles):
                at = SUB + top
                n1, n2 = block[f, t, k, at - 1 : at + 7], block[f, t, k, at - 2 : at + 6]
                s1, s2 = block[f, t, k, at + 1 : at + 9], block[f, t, k, at + 2 : at + 10]
                w1 = jnp.where(lane8 == 0, w1s[t - 1] if t else 0.0, w1s[t])
                w2 = jnp.where(lane8 < 2, w2s[t - 1] if t else 0.0, w2s[t])
                last = t == tiles - 1
                e1 = jnp.where(lane8 == LANES - 1, 0.0 if last else e1s[t + 1], e1s[t])
                e2 = jnp.where(lane8 >= LANES - 2, 0.0 if last else e2s[t + 1], e2s[t])
                low = block[f, t, below, SUB + top : 2 * SUB + top]
                high = block[f, t, above, SUB + top : 2 * SUB + top]
                rad = high - low
                lat = 8.0 * (s1 - n1) - (s2 - n2)
                lon = 8.0 * (e1 - w1) - (e2 - w2)
                bend = None
                if full:
                    bend = (
                        VISCOSITY * (high + low)
                        + curve_lat * (16.0 * (s1 + n1) - (s2 + n2))
                        + curve_lon * (16.0 * (e1 + w1) - (e2 + w2))
                        - center_weight * here[t]
                    )
                out.append((rad, lat, lon, bend))
            return here, out

        wind_rad = [block[1, t, k, SUB + top : 2 * SUB + top] for t in range(tiles)]
        wind_lat = [block[2, t, k, SUB + top : 2 * SUB + top] for t in range(tiles)]
        wind_lon = [block[3, t, k, SUB + top : 2 * SUB + top] for t in range(tiles)]
        go_rad = [0.5 * x for x in wind_rad]
        go_lat = [lat_scale * x for x in wind_lat]
        go_lon = [lon_scale * x for x in wind_lon]

        def put(f, t, center, rate):
            lanes = slice(t * LANES, (t + 1) * LANES)
            rate_box[f, k, strip, lanes] = rate
            state_box[f, k, strip, lanes] = (
                0.75 * outset[0, f, k, strip, lanes] + 0.25 * center
            ) + (0.25 * TIME_STEP) * rate

        rho_here, rho_d = derive(0, False)
        heat_here, heat_d = derive(4, True)
        ratio = [heat_here[t] / rho_here[t] for t in range(tiles)]
        press, rho_rate, heat_rate = [], [], []
        for t in range(tiles):
            (a, b, c, _), (d, e, g, bend) = rho_d[t], heat_d[t]
            press.append(
                (
                    0.5 * (ratio[t] * a + d),
                    lat_scale * (ratio[t] * b + e),
                    lon_scale * (ratio[t] * c + g),
                )
            )
            rho_rate.append(go_rad[t] * a + go_lat[t] * b + go_lon[t] * c)
            heat_rate.append(
                bend
                + (radial_extra - go_rad[t]) * d
                + (slope_extra - go_lat[t]) * e
                - go_lon[t] * g
            )
        diverge = [two_r * wind_rad[t] + cot_r * wind_lat[t] for t in range(tiles)]
        for f in (1, 2, 3):
            here, d_all = derive(f, True)
            for t in range(tiles):
                d, e, g, bend = d_all[t]
                spin_rad, spin_lat = spin_box[0, t, strip], spin_box[1, t, strip]
                spin_lon = spin_box[2, t, strip]
                rate = (
                    bend
                    + (radial_extra - go_rad[t]) * d
                    + (slope_extra - go_lat[t]) * e
                    - go_lon[t] * g
                    - press[t][f - 1]
                )
                if f == 1:
                    diverge[t] += 0.5 * d
                    rate += inv_radius * (wind_lat[t] * wind_lat[t] + wind_lon[t] * wind_lon[t])
                    rate += spin_lon * wind_lat[t] - spin_lat * wind_lon[t] - GRAVITY
                elif f == 2:
                    diverge[t] += lat_scale * e
                    rate += cot_r * (wind_lon[t] * wind_lon[t])
                    rate -= inv_radius * (wind_rad[t] * wind_lat[t])
                    rate += spin_rad * wind_lon[t] - spin_lon * wind_rad[t]
                else:
                    diverge[t] += lon_scale * g
                    rate -= (inv_radius * wind_rad[t] + cot_r * wind_lat[t]) * wind_lon[t]
                    rate += spin_lat * wind_rad[t] - spin_rad * wind_lat[t]
                put(f, t, here[t], rate)
        for t in range(tiles):
            put(0, t, rho_here[t], -rho_rate[t] - rho_here[t] * diverge[t])
            put(
                4,
                t,
                heat_here[t],
                heat_rate[t] - (GAMMA - 1.0) * (heat_here[t] * diverge[t]),
            )

    for c in range(chunks):

        @pl.loop(c * chunk, (c + 1) * chunk)
        def _(k):
            one_level(k)

        for copy in out_copies(c):
            copy.start()
    for c in range(chunks):
        for copy in out_copies(c):
            copy.wait()


def stencil(block, row_box, spin_box, outset):
    levels, rows, cols = outset.shape[2:]
    n_lat, n_lon = lax.axis_size("lat"), lax.axis_size("lon")
    chunk = 4
    out = jax.ShapeDtypeStruct(outset.shape, jnp.float32)
    box = jax.ShapeDtypeStruct(outset.shape[1:], jnp.float32)
    return pl.pallas_call(
        functools.partial(stencil_kernel, (n_lat, n_lon, levels, rows, cols), chunk),
        out_shape=(out, out, box, box),
        in_specs=[VMEM] * 4,
        out_specs=(ANY, ANY, VMEM, VMEM),
        scratch_shapes=[pltpu.SemaphoreType.DMA((levels // chunk, 2))],
        compiler_params=pltpu.CompilerParams(vmem_limit_bytes=20 * MIB),
        cost_estimate=pl.CostEstimate(
            flops=250 * levels * rows * cols,
            bytes_accessed=80 * levels * rows * cols,
            transcendentals=0,
        ),
        name="stencil",
    )(block, row_box, spin_box, outset)


def edges_kernel(geometry, chunk, *refs):
    n_lat, n_lon, levels, rows, cols = geometry
    tiles = cols // LANES
    field_rows = 5 * levels
    partners, turning = refs[:2]
    reply_box = refs[2 : 2 + n_lat]
    (
        lon_even,
        lon_odd,
        lat_even,
        lat_odd,
        block,
        row_box,
        rate_in,
        state_in,
        _,
        _,
        rate_out,
        state_out,
        rate_box,
        state_box,
        replies,
        halo,
        side,
        mixed,
        sems,
    ) = refs[2 + n_lat :]
    lat_here = lax.axis_index("lat")
    lon_here = lax.axis_index("lon")
    lat_len, lon_len = 2 * cols, 2 * rows
    run_lat, run_lon = lat_len // n_lat, lon_len // n_lat
    width = window_of(run_lat, cols)
    step_lat = math.pi / 2.0 / (rows * n_lat)
    step_lon = 1.5 * math.pi / (cols * n_lon)
    by_lat = 1.0 / (12.0 * step_lat)
    by_lon = 1.0 / (12.0 * step_lon)
    chunks = levels // chunk
    parts = edge_parts(rows, tiles)

    def out_copies(c):
        out = []
        for n, part in enumerate(parts):
            out += part_copies(
                (rate_box, state_box),
                (rate_out, state_out),
                part,
                pl.ds(c * chunk, chunk),
                sems.at[c, n],
            )
        return out

    lat_is_even = lax.rem(lat_here, 2) == 0
    lon_is_even = lax.rem(lon_here, 2) == 0
    for even, north, south in ((True, lat_odd, lat_even), (False, lat_even, lat_odd)):

        @pl.when(lat_is_even == even)
        def _(north=north, south=south):
            halo[0] = north[...]
            halo[1] = south[...]

    for even, west, east in ((True, lon_odd, lon_even), (False, lon_even, lon_odd)):

        @pl.when(lon_is_even == even)
        def _(west=west, east=east):
            side[0] = west[...]
            side[1] = east[...]

    @pl.when((lat_here == 0) | (lat_here == n_lat - 1) | (lon_here == 0) | (lon_here == n_lon - 1))
    def _():
        for d in range(n_lat):
            replies[d] = reply_box[d][...]

    lane8 = lax.broadcasted_iota(jnp.int32, (SUB, LANES), 1)
    sub8 = lax.broadcasted_iota(jnp.int32, (SUB, LANES), 0)

    for which, slot0 in ((0, 0), (1, lat_len)):

        @pl.when(lat_here == (0 if which == 0 else n_lat - 1))
        def _(which=which, slot0=slot0):
            sources = [
                jnp.bitwise_xor(partners[0, 0, 0, slot0 + r * run_lat], lat_here) for r in range(n_lat)
            ]
            for layer in range(2):
                for t in range(tiles):
                    lane = lax.broadcasted_iota(jnp.int32, (field_rows, LANES), 1) + t * LANES
                    value = None
                    for r in range(n_lat):
                        first = r * run_lat - layer * cols
                        if first < 0 or first >= cols:
                            continue
                        if first >= (t + 1) * LANES or first + run_lat <= t * LANES:
                            continue
                        base = min(first // LANES, tiles - width)
                        here = (t - base) * LANES
                        piece = replies[sources[r], 0:field_rows, here : here + LANES]
                        value = piece if value is None else jnp.where(lane >= first, piece, value)
                    spot = slot0 + layer * cols + t * LANES
                    cosine = turning[0, 0, 0, 0:1, spot : spot + LANES]
                    sine = turning[0, 0, 0, 1:2, spot : spot + LANES]
                    parts = [value[f * levels : (f + 1) * levels] for f in range(5)]
                    parts[2], parts[3] = (
                        cosine * parts[2] + sine * parts[3],
                        cosine * parts[3] - sine * parts[2],
                    )
                    for f in range(5):
                        halo[which, layer, f, t] = parts[f]

    turn_lon = jnp.concatenate(
        [turning[0, 0, 0, :, 2 * lat_len :], jnp.zeros((SUB - 2, 2 * lon_len), jnp.float32)], axis=0
    ).T

    for which, slot0 in ((0, 2 * lat_len), (1, 2 * lat_len + lon_len)):
        @pl.when(lon_here == (0 if which == 0 else n_lon - 1))
        def _(which=which, slot0=slot0):
            lane = lax.broadcasted_iota(jnp.int32, (run_lon, LANES), 1)
            is_lat = (lane >= 2 * levels) & (lane < 3 * levels)
            is_lon = (lane >= 3 * levels) & (lane < 4 * levels)
            for r in range(n_lat):
                source = jnp.bitwise_xor(partners[0, 0, 0, slot0 + r * run_lon], lat_here)
                layer, first = r * run_lon // rows, r * run_lon % rows
                value = replies[source, field_rows : field_rows + run_lon, 0:LANES]
                slots = slice(which * lon_len + r * run_lon, which * lon_len + (r + 1) * run_lon)
                cosine = jnp.broadcast_to(turn_lon[slots, 0:1], (run_lon, LANES))
                sine = jnp.broadcast_to(turn_lon[slots, 1:2], (run_lon, LANES))
                later = pltpu.roll(value, LANES - levels, 1)
                earlier = pltpu.roll(value, levels, 1)
                value = jnp.where(
                    is_lat,
                    cosine * value + sine * later,
                    jnp.where(is_lon, cosine * value - sine * earlier, value),
                )
                side[which, layer, first : first + run_lon] = value

    lane_all = lax.broadcasted_iota(jnp.int32, (rows, LANES), 1)
    columns = [side[1, 0], side[1, 1], side[0, 0], side[0, 1]]
    columns = [columns[0]] + [pltpu.roll(columns[j], j, 1) for j in range(1, 4)]
    for q in range(4):
        pick = jnp.bitwise_and(lane_all - q, 3)
        value = columns[0]
        for j in range(1, 4):
            value = jnp.where(pick == j, columns[j], value)
        for row in range(q, field_rows, 4):
            mixed[row // levels, row % levels] = pltpu.roll(value, LANES - 2 - row, 1)

    def one_level(k):
        radius = jnp.broadcast_to(1.0 / step_lat + k.astype(jnp.float32), (SUB, LANES))
        inv_radius = 1.0 / radius
        for top in range(0, rows, SUB):
            for t in range(tiles):
                if top in (0, rows - SUB) or t in (0, tiles - 1):
                    one_tile(k, inv_radius, top, t)

    def one_tile(k, inv_radius, top, t):
        strip, lanes = slice(top, top + SUB), slice(t * LANES, (t + 1) * LANES)
        inv_arc = inv_radius * row_box[0, strip]
        lat_scale, lon_scale = inv_radius * by_lat, inv_arc * by_lon
        curve_lat = (VISCOSITY / (12.0 * step_lat * step_lat)) * inv_radius * inv_radius
        curve_lon = (VISCOSITY / (12.0 * step_lon * step_lon)) * inv_arc * inv_arc
        slope_extra = (VISCOSITY * by_lat) * inv_radius * (row_box[1, strip] * inv_radius)
        rho, _, wind_lat, wind_lon, heat = (
            block[f, t, k, SUB + top : 2 * SUB + top] for f in range(5)
        )
        go_lat, go_lon = lat_scale * wind_lat, lon_scale * wind_lon
        ratio = heat / rho

        def add(total, value):
            return value if total is None else total + value

        lat_d, lat_b, lon_d, lon_b = ([None] * 5 for _ in range(4))
        for f in range(5):
            if top == 0:
                far = jnp.broadcast_to(halo[0, 0, f, t, pl.ds(k, 1), :], (SUB, LANES))
                near = jnp.broadcast_to(halo[0, 1, f, t, pl.ds(k, 1), :], (SUB, LANES))
                second = jnp.where(sub8 == 0, far, jnp.where(sub8 == 1, near, 0.0))
                near = 8.0 * jnp.where(sub8 == 0, near, 0.0)
                lat_d[f] = add(lat_d[f], second - near)
                lat_b[f] = add(lat_b[f], 2.0 * near - second)
            if top == rows - SUB:
                near = jnp.broadcast_to(halo[1, 0, f, t, pl.ds(k, 1), :], (SUB, LANES))
                far = jnp.broadcast_to(halo[1, 1, f, t, pl.ds(k, 1), :], (SUB, LANES))
                second = jnp.where(sub8 == SUB - 1, far, jnp.where(sub8 == SUB - 2, near, 0.0))
                near = 8.0 * jnp.where(sub8 == SUB - 1, near, 0.0)
                lat_d[f] = add(lat_d[f], near - second)
                lat_b[f] = add(lat_b[f], 2.0 * near - second)
            ghost = mixed[f, k, strip]
            if t == 0:
                second = jnp.where(lane8 < 2, ghost, 0.0)
                near = 8.0 * jnp.where(lane8 == 0, pltpu.roll(ghost, LANES - 1, 1), 0.0)
                lon_d[f] = add(lon_d[f], second - near)
                lon_b[f] = add(lon_b[f], 2.0 * near - second)
            if t == tiles - 1:
                second = jnp.where(lane8 >= LANES - 2, ghost, 0.0)
                near = 8.0 * jnp.where(lane8 == LANES - 1, pltpu.roll(ghost, 1, 1), 0.0)
                lon_d[f] = add(lon_d[f], near - second)
                lon_b[f] = add(lon_b[f], 2.0 * near - second)

        rates = [None] * 5
        diverge = None
        if lat_d[0] is not None:
            diverge = add(diverge, lat_scale * lat_d[2])
            rates[0] = add(rates[0], -go_lat * lat_d[0])
            for f in range(1, 5):
                rates[f] = add(
                    rates[f], curve_lat * lat_b[f] + (slope_extra - go_lat) * lat_d[f]
                )
            rates[2] -= lat_scale * (ratio * lat_d[0] + lat_d[4])
        if lon_d[0] is not None:
            diverge = add(diverge, lon_scale * lon_d[3])
            rates[0] = add(rates[0], -go_lon * lon_d[0])
            for f in range(1, 5):
                rates[f] = add(rates[f], curve_lon * lon_b[f] - go_lon * lon_d[f])
            rates[3] -= lon_scale * (ratio * lon_d[0] + lon_d[4])
        rates[0] -= rho * diverge
        rates[4] -= (GAMMA - 1.0) * (heat * diverge)
        for f in range(5):
            rate_box[f, k, strip, lanes] = rate_in[f, k, strip, lanes] + rates[f]
            state_box[f, k, strip, lanes] = (
                state_in[f, k, strip, lanes] + (0.25 * TIME_STEP) * rates[f]
            )

    for c in range(chunks):

        @pl.loop(c * chunk, (c + 1) * chunk)
        def _(k):
            one_level(k)

        for copy in out_copies(c):
            copy.start()
    for c in range(chunks):
        for copy in out_copies(c):
            copy.wait()


def edges(partners, turning, replies, sides, halos, block, row_box, inner):
    rate_out, state_out, rate_box, state_box = inner
    levels, rows, cols = rate_box.shape[1:]
    n_lat, n_lon = lax.axis_size("lat"), lax.axis_size("lon")
    chunk = 4
    out = jax.ShapeDtypeStruct(rate_out.shape, jnp.float32)
    box = pltpu.VMEM(rate_box.shape, jnp.float32)
    n_in = n_lat + 10
    return pl.pallas_call(
        functools.partial(edges_kernel, (n_lat, n_lon, levels, rows, cols), chunk),
        out_shape=(out, out),
        in_specs=[SMEM] + [VMEM] * (n_in - 1) + [ANY] * 2,
        out_specs=(ANY, ANY),
        input_output_aliases={n_in: 0, n_in + 1: 1},
        scratch_shapes=[
            box,
            box,
            pltpu.VMEM((n_lat,) + replies[0].shape, jnp.float32),
            pltpu.VMEM((2,) + halos[0].shape, jnp.float32),
            pltpu.VMEM((2, 2, rows, LANES), jnp.float32),
            pltpu.VMEM((5, levels, rows, LANES), jnp.float32),
            pltpu.SemaphoreType.DMA((levels // chunk, 4, 2)),
        ],
        compiler_params=pltpu.CompilerParams(vmem_limit_bytes=20 * MIB),
        cost_estimate=pl.CostEstimate(
            flops=40 * levels * rows * cols,
            bytes_accessed=40 * levels * rows * cols,
            transcendentals=0,
        ),
        name="edges",
    )(
        partners,
        turning,
        *replies,
        *sides,
        *halos,
        block,
        row_box,
        rate_box,
        state_box,
        rate_out,
        state_out,
    )


def shards(rho, flow, heat, outset, opposite_block, donor_lower_corner, blend, turning):
    levels, rows, cols = rho.shape[1:]
    n_lat = lax.axis_size("lat")
    request = ask(opposite_block, donor_lower_corner, blend, rows, cols)
    requests = [swap_panels(request, d) for d in range(n_lat)]
    cells, block, even_rows, odd_rows, even_cols, odd_cols, row_box, spin_box = prepare(
        rho, flow, heat
    )
    *requests, even_rows, odd_rows, even_cols, odd_cols = lax.optimization_barrier(
        (*requests, even_rows, odd_rows, even_cols, odd_cols)
    )
    sides = (swap_pairs(even_cols, "lon", False), swap_pairs(odd_cols, "lon", True))
    halos = (swap_pairs(even_rows, "lat", False), swap_pairs(odd_rows, "lat", True))
    replies = donate(requests, cells, rows, cols, 5 * levels)
    *replies, spin_box = lax.optimization_barrier((*replies, spin_box))
    replies = [swap_panels(reply, d) for d, reply in enumerate(replies)]
    inner = stencil(block, row_box, spin_box, outset)
    return edges(opposite_block, turning, replies, sides, halos, block, row_box, inner)


def solution(mesh):
    in_specs = (
        P("panel", None, "lat", "lon"),
        P("panel", None, None, "lat", "lon"),
        P("panel", None, "lat", "lon"),
        P("panel", None, None, "lat", "lon"),
        P("panel", "lat", "lon", None),
        P("panel", "lat", "lon", None),
        P("panel", "lat", "lon", None, None),
        P("panel", "lat", "lon", None, None),
    )
    out_specs = (P("panel", None, None, "lat", "lon"), P("panel", None, None, "lat", "lon"))
    return jax.shard_map(shards, mesh=mesh, in_specs=in_specs, out_specs=out_specs, check_vma=False)
```

```python
import functools
import math

import jax
import jax.numpy as jnp
from jax import lax
from jax.experimental import pallas as pl
from jax.experimental.pallas import tpu as pltpu
from jax.sharding import PartitionSpec as P

OMEGA = 0.5
GRAVITY = 1.0
VISCOSITY = 0.2
DIFFUSIVITY = 0.2
GAMMA = 1.4
TIME_STEP = 0.05
LANES = 128
SUB = 8
MIB = 1024 * 1024
ANY = pl.BlockSpec(memory_space=pl.ANY)
HBM = pl.BlockSpec(memory_space=pltpu.HBM)
VMEM = pl.BlockSpec(memory_space=pltpu.VMEM)
SMEM = pl.BlockSpec(memory_space=pltpu.SMEM)


def in_hbm(value):
    return pltpu.with_memory_space_constraint(value, pltpu.HBM)


def pair_partner(i, count, odd, wrap):
    partner = i ^ 1 if not odd else (i + 1 if i % 2 else i - 1)
    if 0 <= partner < count:
        return partner
    return partner % count if wrap else i


def swap_pairs(value, axis, odd):
    count = lax.axis_size(axis)
    return lax.ppermute(value, axis, [(i, pair_partner(i, count, odd, axis == "lat")) for i in range(count)])


def swap_panels(value, distance):
    n_lat = lax.axis_size("lat")
    pairs = [
        (p * n_lat + a, (1 - p) * n_lat + (a ^ distance)) for p in range(2) for a in range(n_lat)
    ]
    return lax.ppermute(value, ("panel", "lat"), pairs)


def window_of(run, cols):
    tiles = cols // LANES
    for width in range(1, tiles + 1):
        if all(
            start - min(start // LANES, tiles - width) * LANES + run <= width * LANES
            for start in range(0, cols, run)
        ):
            return width
    return tiles


def ask_kernel(partners, corners, blend, request, partners_box, corners_box, blend_box, sems):
    lat_len = corners.shape[-1] - request.shape[-1]
    copies = [
        pltpu.make_async_copy(partners, partners_box, sems.at[0]),
        pltpu.make_async_copy(corners, corners_box, sems.at[1]),
        pltpu.make_async_copy(blend, blend_box, sems.at[2]),
    ]
    for copy in copies:
        copy.start()
    for copy in copies:
        copy.wait()
    north = lax.axis_index("lat") == 0
    for row, source in ((0, partners_box), (1, corners_box)):
        values = source[0, 0].astype(jnp.float32)
        request[row : row + 1, 0:lat_len] = jnp.where(
            north, values[:, 0:lat_len], values[:, lat_len : 2 * lat_len]
        )
        request[row : row + 1, lat_len:] = values[:, 2 * lat_len :]
    weights = blend_box[0, 0, 0]
    request[2:6, 0:lat_len] = jnp.where(
        north, weights[:, 0:lat_len], weights[:, lat_len : 2 * lat_len]
    )
    request[2:6, lat_len:] = weights[:, 2 * lat_len :]


def ask(partners, corners, blend, rows, cols):
    return pl.pallas_call(
        ask_kernel,
        out_shape=jax.ShapeDtypeStruct((SUB, 2 * cols + 4 * rows), jnp.float32),
        in_specs=[HBM] * 3,
        out_specs=VMEM,
        scratch_shapes=[
            pltpu.VMEM(partners.shape, jnp.int32),
            pltpu.VMEM(corners.shape, jnp.int32),
            pltpu.VMEM(blend.shape, jnp.float32),
            pltpu.SemaphoreType.DMA((3,)),
        ],
        compiler_params=pltpu.CompilerParams(vmem_limit_bytes=MIB),
        name="ask",
    )(*(in_hbm(x) for x in (partners, corners, blend)))


def prepare_kernel(
    n_lat,
    n_lon,
    rho,
    flow,
    heat,
    cells,
    block,
    even_rows,
    odd_rows,
    even_cols,
    odd_cols,
    row_box,
    spin_box,
    staged,
    sems,
):
    levels, rows, cols = rho.shape[1:]
    tiles = cols // LANES
    strips = rows // SUB

    def load_copies(strip):
        here = pl.ds(strip * SUB, SUB)
        return (
            pltpu.make_async_copy(rho.at[0, :, here], staged.at[0, :, here], sems.at[strip, 0]),
            pltpu.make_async_copy(
                flow.at[0, :, :, here], staged.at[pl.ds(1, 3), :, here], sems.at[strip, 1]
            ),
            pltpu.make_async_copy(heat.at[0, :, here], staged.at[4, :, here], sems.at[strip, 2]),
        )

    for strip in range(strips):
        for copy in load_copies(strip):
            copy.start()

    pitch = rows + 2 * SUB
    flat = block.reshape(5, tiles, levels * pitch, LANES)

    def level_rows(field, tile, row):
        return flat[field, tile, pl.ds(SUB + row, levels, stride=pitch), :]

    zero = jnp.zeros((levels, SUB, LANES), jnp.float32)
    for field in range(5):
        for tile in range(tiles):
            block[field, tile, :, 0:SUB] = zero
            block[field, tile, :, rows + SUB :] = zero

    step_lat = math.pi / 2.0 / (rows * n_lat)
    step_lon = 1.5 * math.pi / (cols * n_lon)
    sub = lax.broadcasted_iota(jnp.int32, (rows, LANES), 0)
    row_global = (lax.axis_index("lat") * rows + sub).astype(jnp.float32)
    theta = math.pi / 4.0 + (row_global + 0.5) * step_lat
    sin_lat, cos_lat = jnp.sin(theta), jnp.cos(theta)
    row_box[0] = 1.0 / sin_lat
    row_box[1] = cos_lat / sin_lat
    yang = lax.axis_index("panel").astype(jnp.float32)
    yin = 1.0 - yang
    for tile in range(tiles):
        lane = lax.broadcasted_iota(jnp.int32, (SUB, LANES), 1) + tile * LANES
        col_global = (lax.axis_index("lon") * cols + lane).astype(jnp.float32)
        longitude = -0.75 * math.pi + (col_global + 0.5) * step_lon
        sin_lon, cos_lon = jnp.sin(longitude)[0:1], jnp.cos(longitude)[0:1]
        spin_box[0, tile] = 2.0 * OMEGA * (yin * cos_lat + yang * sin_lat * sin_lon)
        spin_box[1, tile] = 2.0 * OMEGA * (yang * cos_lat * sin_lon - yin * sin_lat)
        spin_box[2, tile] = jnp.broadcast_to(2.0 * OMEGA * yang * cos_lon, (rows, LANES))

    for strip in range(strips):
        for copy in load_copies(strip):
            copy.wait()
        here, there = strip * SUB, (strip + 1) * SUB
        for field in range(5):
            for tile in range(tiles):
                block[field, tile, :, there : there + SUB] = staged[
                    field, :, here:there, tile * LANES : (tile + 1) * LANES
                ]
        for row in range(here, there):
            for tile in range(tiles):
                stack = jnp.concatenate([level_rows(f, tile, row) for f in range(5)], axis=0)
                at = row * cols + tile * LANES
                cells[at : at + LANES, 0 : 5 * levels] = stack.T

    lat_even = lax.rem(lax.axis_index("lat"), 2) == 0
    for first, to_even in ((0, jnp.logical_not(lat_even)), (rows - 2, lat_even)):
        for keep, out in ((to_even, even_rows), (jnp.logical_not(to_even), odd_rows)):

            @pl.when(keep)
            def _(first=first, out=out):
                for layer in range(2):
                    for field in range(5):
                        for tile in range(tiles):
                            out[layer, field, tile] = level_rows(field, tile, first + layer)

    lon_even = lax.rem(lax.axis_index("lon"), 2) == 0
    for first, to_even in ((0, jnp.logical_not(lon_even)), (cols - 2, lon_even)):
        for keep, out in ((to_even, even_cols), (jnp.logical_not(to_even), odd_cols)):

            @pl.when(keep)
            def _(first=first, out=out):
                for layer in range(2):
                    for row in range(rows):
                        at = row * cols + first + layer
                        out[layer, row : row + 1, :] = cells[at : at + 1, :]


def prepare(rho, flow, heat):
    levels, rows, cols = rho.shape[1:]
    tiles = cols // LANES
    shapes = (
        (rows * cols, LANES),
        (5, tiles, levels, rows + 2 * SUB, LANES),
        (2, 5, tiles, levels, LANES),
        (2, 5, tiles, levels, LANES),
        (2, rows, LANES),
        (2, rows, LANES),
        (2, rows, LANES),
        (3, tiles, rows, LANES),
    )
    return pl.pallas_call(
        functools.partial(prepare_kernel, lax.axis_size("lat"), lax.axis_size("lon")),
        out_shape=tuple(jax.ShapeDtypeStruct(shape, jnp.float32) for shape in shapes),
        in_specs=[ANY] * 3,
        out_specs=(VMEM,) * len(shapes),
        scratch_shapes=[
            pltpu.VMEM((5, levels, rows, cols), jnp.float32),
            pltpu.SemaphoreType.DMA((rows // SUB, 3)),
        ],
        compiler_params=pltpu.CompilerParams(vmem_limit_bytes=16 * MIB),
        name="prepare",
    )(*(in_hbm(x) for x in (rho, flow, heat)))


def donate_kernel(n_lat, n_lon, rows, cols, field_rows, *refs):
    weights = refs[:n_lat]
    cells = refs[n_lat]
    replies = refs[n_lat + 1 : 2 * n_lat + 1]
    corners, turned, gathered, whole_box, requests, sems = refs[2 * n_lat + 1 :]
    slots = weights[0].shape[1]
    lat_len, lon_len = 2 * cols, 2 * rows
    for distance in range(n_lat):
        for row in range(2):
            for tile in range(slots // LANES):
                lanes = slice(tile * LANES, (tile + 1) * LANES)
                whole_box[distance, row, tile : tile + 1] = weights[distance][
                    row : row + 1, lanes
                ].astype(jnp.int32)
    copy = pltpu.make_async_copy(whole_box, requests, sems.at[0])
    copy.start()
    for distance in range(n_lat):
        for at in range(lat_len, slots, LANES):
            turned[distance, at : at + LANES, 0:SUB] = weights[distance][:, at : at + LANES].T
        asker = jnp.bitwise_xor(lax.axis_index("lat"), distance)

        @pl.when((asker == 0) | (asker == n_lat - 1))
        def _(distance=distance):
            for at in range(0, lat_len, LANES):
                turned[distance, at : at + LANES, 0:SUB] = weights[distance][:, at : at + LANES].T

    copy.wait()
    lat_len, lon_len = 2 * cols, 2 * rows
    run_lat, run_lon = lat_len // n_lat, lon_len // n_lat
    tiles = cols // LANES
    width = window_of(run_lat, cols)
    lat_here = lax.axis_index("lat")
    lon_here = lax.axis_index("lon")

    def word(request, row, slot):
        return requests[request, row, lax.shift_right_logical(slot, 7), jnp.bitwise_and(slot, 127)]

    def find_run(request, start, run):
        start = jnp.int32(start)
        found = jnp.int32(0)
        for r in range(1, n_lat):
            match = word(request, 0, start + r * run) == lat_here
            found = jnp.where(match, jnp.int32(r), found)
        return found

    def gather(request, first, count):
        def step(i, carry):
            for u in range(SUB):
                t = i * SUB + u
                cell = word(request, 1, first + t)
                for j, shift in enumerate((0, cols, 1, cols + 1)):
                    corners[j, pl.ds(t, 1), :] = cells[pl.ds(cell + shift, 1), :]
            return carry

        lax.fori_loop(0, count // SUB, step, 0)

    def blend(distance, first, count):
        rows_here = pl.ds(pl.multiple_of(first, SUB), count)
        total = None
        for j in range(4):
            weight = jnp.broadcast_to(turned[distance, rows_here, 2 + j : 3 + j], (count, LANES))
            part = weight * corners[j, 0:count, :]
            total = part if total is None else total + part
        return total

    for distance in range(n_lat):
        request, reply = distance, replies[distance]
        asker = jnp.bitwise_xor(lat_here, distance)

        @pl.when((asker == 0) | (asker == n_lat - 1))
        def _(distance=distance, request=request, reply=reply):
            run = find_run(request, 0, run_lat)
            start = lax.rem(run * run_lat, cols)
            base = jnp.minimum(lax.div(start, LANES), tiles - width)
            offset = pl.multiple_of(start - base * LANES, SUB)
            gather(request, run * run_lat, run_lat)
            gathered[pl.ds(offset, run_lat), :] = blend(distance, run * run_lat, run_lat)
            for tile in range(width):
                block = gathered[tile * LANES : (tile + 1) * LANES, :]
                reply[0:field_rows, tile * LANES : (tile + 1) * LANES] = block.T[0:field_rows]

        @pl.when((lon_here == 0) | (lon_here == n_lon - 1))
        def _(distance=distance, request=request, reply=reply):
            first = lat_len + jnp.where(lon_here == 0, 0, lon_len)
            run = find_run(request, first, run_lon)
            gather(request, first + run * run_lon, run_lon)
            reply[field_rows : field_rows + run_lon, 0:LANES] = blend(
                distance, first + run * run_lon, run_lon
            )


def donate(requests, cells, rows, cols, field_rows):
    n_lat, n_lon = lax.axis_size("lat"), lax.axis_size("lon")
    run_lat = 2 * cols // n_lat
    width = window_of(run_lat, cols)
    slots = requests[0].shape[1]
    words = (pl.cdiv(slots, SUB * LANES) * SUB, LANES)
    reply = jax.ShapeDtypeStruct((field_rows + 2 * rows // n_lat, width * LANES), jnp.float32)
    return pl.pallas_call(
        functools.partial(donate_kernel, n_lat, n_lon, rows, cols, field_rows),
        out_shape=(reply,) * n_lat,
        in_specs=[VMEM] * (n_lat + 1),
        out_specs=(VMEM,) * n_lat,
        scratch_shapes=[
            pltpu.VMEM((4, max(run_lat, 2 * rows // n_lat), LANES), jnp.float32),
            pltpu.VMEM((n_lat, slots, LANES), jnp.float32),
            pltpu.VMEM((width * LANES, LANES), jnp.float32),
            pltpu.VMEM((n_lat, 2) + words, jnp.int32),
            pltpu.SMEM((n_lat, 2) + words, jnp.int32),
            pltpu.SemaphoreType.DMA((1,)),
        ],
        compiler_params=pltpu.CompilerParams(vmem_limit_bytes=9 * MIB),
        name="donate",
    )(*requests, cells)


def core_parts(rows, tiles):
    return (SUB, rows - 2 * SUB, LANES, (tiles - 2) * LANES)


def edge_parts(rows, tiles):
    cols = tiles * LANES
    return (
        (0, SUB, 0, cols),
        (rows - SUB, SUB, 0, cols),
        (SUB, rows - 2 * SUB, 0, LANES),
        (SUB, rows - 2 * SUB, cols - LANES, LANES),
    )


def part_copies(boxes, outs, part, span, sems):
    first, count, lane, lanes = part
    at = (span, pl.ds(first, count), pl.ds(lane, lanes))
    return [
        pltpu.make_async_copy(box.at[(slice(None),) + at], out.at[(0, slice(None)) + at], sems.at[n])
        for n, (box, out) in enumerate(zip(boxes, outs))
    ]


def stencil_kernel(
    geometry, chunk, block, row_box, spin_box, outset, rate_out, state_out, rate_box, state_box, sems
):
    n_lat, n_lon, levels, rows, cols = geometry
    tiles = cols // LANES
    step_lat = math.pi / 2.0 / (rows * n_lat)
    step_lon = 1.5 * math.pi / (cols * n_lon)
    chunks = levels // chunk
    by_lat = 1.0 / (12.0 * step_lat)
    by_lon = 1.0 / (12.0 * step_lon)
    lane8 = lax.broadcasted_iota(jnp.int32, (SUB, LANES), 1)

    def out_copies(c):
        return part_copies(
            (rate_box, state_box),
            (rate_out, state_out),
            core_parts(rows, tiles),
            pl.ds(c * chunk, chunk),
            sems.at[c],
        )

    def one_level(k):
        below = jnp.maximum(k - 1, 0)
        above = jnp.minimum(k + 1, levels - 1)
        radius = jnp.broadcast_to(1.0 / step_lat + k.astype(jnp.float32), (SUB, LANES))
        inv_radius = 1.0 / radius
        for top in range(0, rows, SUB):
            one_strip(k, below, above, inv_radius, inv_radius * by_lat, top)

    def one_strip(k, below, above, inv_radius, lat_scale, top):
        strip = slice(top, top + SUB)
        inv_sin, cot = row_box[0, strip], row_box[1, strip]
        inv_arc = inv_radius * inv_sin
        lon_scale = inv_arc * by_lon
        cot_r = cot * inv_radius
        two_r = 2.0 * inv_radius
        curve_lat = (VISCOSITY / (12.0 * step_lat * step_lat)) * inv_radius * inv_radius
        curve_lon = (VISCOSITY / (12.0 * step_lon * step_lon)) * inv_arc * inv_arc
        slope_extra = (VISCOSITY * by_lat) * inv_radius * cot_r
        radial_extra = VISCOSITY * inv_radius
        center_weight = 2.0 * VISCOSITY + 30.0 * (curve_lat + curve_lon)

        def derive(f, full):
            here = [block[f, t, k, SUB + top : 2 * SUB + top] for t in range(tiles)]
            w1s = [pltpu.roll(x, 1, 1) for x in here]
            w2s = [pltpu.roll(x, 2, 1) for x in here]
            e1s = [pltpu.roll(x, LANES - 1, 1) for x in here]
            e2s = [pltpu.roll(x, LANES - 2, 1) for x in here]
            out = []
            for t in range(tiles):
                at = SUB + top
                n1, n2 = block[f, t, k, at - 1 : at + 7], block[f, t, k, at - 2 : at + 6]
                s1, s2 = block[f, t, k, at + 1 : at + 9], block[f, t, k, at + 2 : at + 10]
                w1 = jnp.where(lane8 == 0, w1s[t - 1] if t else 0.0, w1s[t])
                w2 = jnp.where(lane8 < 2, w2s[t - 1] if t else 0.0, w2s[t])
                last = t == tiles - 1
                e1 = jnp.where(lane8 == LANES - 1, 0.0 if last else e1s[t + 1], e1s[t])
                e2 = jnp.where(lane8 >= LANES - 2, 0.0 if last else e2s[t + 1], e2s[t])
                low = block[f, t, below, SUB + top : 2 * SUB + top]
                high = block[f, t, above, SUB + top : 2 * SUB + top]
                rad = high - low
                lat = 8.0 * (s1 - n1) - (s2 - n2)
                lon = 8.0 * (e1 - w1) - (e2 - w2)
                bend = None
                if full:
                    bend = (
                        VISCOSITY * (high + low)
                        + curve_lat * (16.0 * (s1 + n1) - (s2 + n2))
                        + curve_lon * (16.0 * (e1 + w1) - (e2 + w2))
                        - center_weight * here[t]
                    )
                out.append((rad, lat, lon, bend))
            return here, out

        wind_rad = [block[1, t, k, SUB + top : 2 * SUB + top] for t in range(tiles)]
        wind_lat = [block[2, t, k, SUB + top : 2 * SUB + top] for t in range(tiles)]
        wind_lon = [block[3, t, k, SUB + top : 2 * SUB + top] for t in range(tiles)]
        go_rad = [0.5 * x for x in wind_rad]
        go_lat = [lat_scale * x for x in wind_lat]
        go_lon = [lon_scale * x for x in wind_lon]

        def put(f, t, center, rate):
            lanes = slice(t * LANES, (t + 1) * LANES)
            rate_box[f, k, strip, lanes] = rate
            state_box[f, k, strip, lanes] = (
                0.75 * outset[0, f, k, strip, lanes] + 0.25 * center
            ) + (0.25 * TIME_STEP) * rate

        rho_here, rho_d = derive(0, False)
        heat_here, heat_d = derive(4, True)
        ratio = [heat_here[t] / rho_here[t] for t in range(tiles)]
        press, rho_rate, heat_rate = [], [], []
        for t in range(tiles):
            (a, b, c, _), (d, e, g, bend) = rho_d[t], heat_d[t]
            press.append(
                (
                    0.5 * (ratio[t] * a + d),
                    lat_scale * (ratio[t] * b + e),
                    lon_scale * (ratio[t] * c + g),
                )
            )
            rho_rate.append(go_rad[t] * a + go_lat[t] * b + go_lon[t] * c)
            heat_rate.append(
                bend
                + (radial_extra - go_rad[t]) * d
                + (slope_extra - go_lat[t]) * e
                - go_lon[t] * g
            )
        diverge = [two_r * wind_rad[t] + cot_r * wind_lat[t] for t in range(tiles)]
        for f in (1, 2, 3):
            here, d_all = derive(f, True)
            for t in range(tiles):
                d, e, g, bend = d_all[t]
                spin_rad, spin_lat = spin_box[0, t, strip], spin_box[1, t, strip]
                spin_lon = spin_box[2, t, strip]
                rate = (
                    bend
                    + (radial_extra - go_rad[t]) * d
                    + (slope_extra - go_lat[t]) * e
                    - go_lon[t] * g
                    - press[t][f - 1]
                )
                if f == 1:
                    diverge[t] += 0.5 * d
                    rate += inv_radius * (wind_lat[t] * wind_lat[t] + wind_lon[t] * wind_lon[t])
                    rate += spin_lon * wind_lat[t] - spin_lat * wind_lon[t] - GRAVITY
                elif f == 2:
                    diverge[t] += lat_scale * e
                    rate += cot_r * (wind_lon[t] * wind_lon[t])
                    rate -= inv_radius * (wind_rad[t] * wind_lat[t])
                    rate += spin_rad * wind_lon[t] - spin_lon * wind_rad[t]
                else:
                    diverge[t] += lon_scale * g
                    rate -= (inv_radius * wind_rad[t] + cot_r * wind_lat[t]) * wind_lon[t]
                    rate += spin_lat * wind_rad[t] - spin_rad * wind_lat[t]
                put(f, t, here[t], rate)
        for t in range(tiles):
            put(0, t, rho_here[t], -rho_rate[t] - rho_here[t] * diverge[t])
            put(
                4,
                t,
                heat_here[t],
                heat_rate[t] - (GAMMA - 1.0) * (heat_here[t] * diverge[t]),
            )

    for c in range(chunks):

        @pl.loop(c * chunk, (c + 1) * chunk)
        def _(k):
            one_level(k)

        for copy in out_copies(c):
            copy.start()
    for c in range(chunks):
        for copy in out_copies(c):
            copy.wait()


def stencil(block, row_box, spin_box, outset):
    levels, rows, cols = outset.shape[2:]
    n_lat, n_lon = lax.axis_size("lat"), lax.axis_size("lon")
    chunk = 4
    out = jax.ShapeDtypeStruct(outset.shape, jnp.float32)
    box = jax.ShapeDtypeStruct(outset.shape[1:], jnp.float32)
    return pl.pallas_call(
        functools.partial(stencil_kernel, (n_lat, n_lon, levels, rows, cols), chunk),
        out_shape=(out, out, box, box),
        in_specs=[VMEM] * 4,
        out_specs=(ANY, ANY, VMEM, VMEM),
        scratch_shapes=[pltpu.SemaphoreType.DMA((levels // chunk, 2))],
        compiler_params=pltpu.CompilerParams(vmem_limit_bytes=20 * MIB),
        cost_estimate=pl.CostEstimate(
            flops=250 * levels * rows * cols,
            bytes_accessed=80 * levels * rows * cols,
            transcendentals=0,
        ),
        name="stencil",
    )(block, row_box, spin_box, outset)


def edges_kernel(geometry, chunk, *refs):
    n_lat, n_lon, levels, rows, cols = geometry
    tiles = cols // LANES
    field_rows = 5 * levels
    partners, turning = refs[:2]
    reply_box = refs[2 : 2 + n_lat]
    (
        lon_even,
        lon_odd,
        lat_even,
        lat_odd,
        block,
        row_box,
        rate_in,
        state_in,
        _,
        _,
        rate_out,
        state_out,
        rate_box,
        state_box,
        replies,
        halo,
        side,
        mixed,
        sems,
    ) = refs[2 + n_lat :]
    lat_here = lax.axis_index("lat")
    lon_here = lax.axis_index("lon")
    lat_len, lon_len = 2 * cols, 2 * rows
    run_lat, run_lon = lat_len // n_lat, lon_len // n_lat
    width = window_of(run_lat, cols)
    step_lat = math.pi / 2.0 / (rows * n_lat)
    step_lon = 1.5 * math.pi / (cols * n_lon)
    by_lat = 1.0 / (12.0 * step_lat)
    by_lon = 1.0 / (12.0 * step_lon)
    chunks = levels // chunk
    parts = edge_parts(rows, tiles)

    def out_copies(c):
        out = []
        for n, part in enumerate(parts):
            out += part_copies(
                (rate_box, state_box),
                (rate_out, state_out),
                part,
                pl.ds(c * chunk, chunk),
                sems.at[c, n],
            )
        return out

    lat_is_even = lax.rem(lat_here, 2) == 0
    lon_is_even = lax.rem(lon_here, 2) == 0
    for even, north, south in ((True, lat_odd, lat_even), (False, lat_even, lat_odd)):

        @pl.when(lat_is_even == even)
        def _(north=north, south=south):
            halo[0] = north[...]
            halo[1] = south[...]

    for even, west, east in ((True, lon_odd, lon_even), (False, lon_even, lon_odd)):

        @pl.when(lon_is_even == even)
        def _(west=west, east=east):
            side[0] = west[...]
            side[1] = east[...]

    @pl.when((lat_here == 0) | (lat_here == n_lat - 1) | (lon_here == 0) | (lon_here == n_lon - 1))
    def _():
        for d in range(n_lat):
            replies[d] = reply_box[d][...]

    lane8 = lax.broadcasted_iota(jnp.int32, (SUB, LANES), 1)
    sub8 = lax.broadcasted_iota(jnp.int32, (SUB, LANES), 0)

    for which, slot0 in ((0, 0), (1, lat_len)):

        @pl.when(lat_here == (0 if which == 0 else n_lat - 1))
        def _(which=which, slot0=slot0):
            sources = [
                jnp.bitwise_xor(partners[0, 0, 0, slot0 + r * run_lat], lat_here) for r in range(n_lat)
            ]
            for layer in range(2):
                for t in range(tiles):
                    lane = lax.broadcasted_iota(jnp.int32, (field_rows, LANES), 1) + t * LANES
                    value = None
                    for r in range(n_lat):
                        first = r * run_lat - layer * cols
                        if first < 0 or first >= cols:
                            continue
                        if first >= (t + 1) * LANES or first + run_lat <= t * LANES:
                            continue
                        base = min(first // LANES, tiles - width)
                        here = (t - base) * LANES
                        piece = replies[sources[r], 0:field_rows, here : here + LANES]
                        value = piece if value is None else jnp.where(lane >= first, piece, value)
                    spot = slot0 + layer * cols + t * LANES
                    cosine = turning[0, 0, 0, 0:1, spot : spot + LANES]
                    sine = turning[0, 0, 0, 1:2, spot : spot + LANES]
                    parts = [value[f * levels : (f + 1) * levels] for f in range(5)]
                    parts[2], parts[3] = (
                        cosine * parts[2] + sine * parts[3],
                        cosine * parts[3] - sine * parts[2],
                    )
                    for f in range(5):
                        halo[which, layer, f, t] = parts[f]

    turn_lon = jnp.concatenate(
        [turning[0, 0, 0, :, 2 * lat_len :], jnp.zeros((SUB - 2, 2 * lon_len), jnp.float32)], axis=0
    ).T

    for which, slot0 in ((0, 2 * lat_len), (1, 2 * lat_len + lon_len)):
        @pl.when(lon_here == (0 if which == 0 else n_lon - 1))
        def _(which=which, slot0=slot0):
            lane = lax.broadcasted_iota(jnp.int32, (run_lon, LANES), 1)
            is_lat = (lane >= 2 * levels) & (lane < 3 * levels)
            is_lon = (lane >= 3 * levels) & (lane < 4 * levels)
            for r in range(n_lat):
                source = jnp.bitwise_xor(partners[0, 0, 0, slot0 + r * run_lon], lat_here)
                layer, first = r * run_lon // rows, r * run_lon % rows
                value = replies[source, field_rows : field_rows + run_lon, 0:LANES]
                slots = slice(which * lon_len + r * run_lon, which * lon_len + (r + 1) * run_lon)
                cosine = jnp.broadcast_to(turn_lon[slots, 0:1], (run_lon, LANES))
                sine = jnp.broadcast_to(turn_lon[slots, 1:2], (run_lon, LANES))
                later = pltpu.roll(value, LANES - levels, 1)
                earlier = pltpu.roll(value, levels, 1)
                value = jnp.where(
                    is_lat,
                    cosine * value + sine * later,
                    jnp.where(is_lon, cosine * value - sine * earlier, value),
                )
                side[which, layer, first : first + run_lon] = value

    lane_all = lax.broadcasted_iota(jnp.int32, (rows, LANES), 1)
    columns = [side[1, 0], side[1, 1], side[0, 0], side[0, 1]]
    columns = [columns[0]] + [pltpu.roll(columns[j], j, 1) for j in range(1, 4)]
    for q in range(4):
        pick = jnp.bitwise_and(lane_all - q, 3)
        value = columns[0]
        for j in range(1, 4):
            value = jnp.where(pick == j, columns[j], value)
        for row in range(q, field_rows, 4):
            mixed[row // levels, row % levels] = pltpu.roll(value, LANES - 2 - row, 1)

    def one_level(k):
        radius = jnp.broadcast_to(1.0 / step_lat + k.astype(jnp.float32), (SUB, LANES))
        inv_radius = 1.0 / radius
        for top in range(0, rows, SUB):
            for t in range(tiles):
                if top in (0, rows - SUB) or t in (0, tiles - 1):
                    one_tile(k, inv_radius, top, t)

    def one_tile(k, inv_radius, top, t):
        strip, lanes = slice(top, top + SUB), slice(t * LANES, (t + 1) * LANES)
        inv_arc = inv_radius * row_box[0, strip]
        lat_scale, lon_scale = inv_radius * by_lat, inv_arc * by_lon
        curve_lat = (VISCOSITY / (12.0 * step_lat * step_lat)) * inv_radius * inv_radius
        curve_lon = (VISCOSITY / (12.0 * step_lon * step_lon)) * inv_arc * inv_arc
        slope_extra = (VISCOSITY * by_lat) * inv_radius * (row_box[1, strip] * inv_radius)
        rho, _, wind_lat, wind_lon, heat = (
            block[f, t, k, SUB + top : 2 * SUB + top] for f in range(5)
        )
        go_lat, go_lon = lat_scale * wind_lat, lon_scale * wind_lon
        ratio = heat / rho

        def add(total, value):
            return value if total is None else total + value

        lat_d, lat_b, lon_d, lon_b = ([None] * 5 for _ in range(4))
        for f in range(5):
            if top == 0:
                far = jnp.broadcast_to(halo[0, 0, f, t, pl.ds(k, 1), :], (SUB, LANES))
                near = jnp.broadcast_to(halo[0, 1, f, t, pl.ds(k, 1), :], (SUB, LANES))
                second = jnp.where(sub8 == 0, far, jnp.where(sub8 == 1, near, 0.0))
                near = 8.0 * jnp.where(sub8 == 0, near, 0.0)
                lat_d[f] = add(lat_d[f], second - near)
                lat_b[f] = add(lat_b[f], 2.0 * near - second)
            if top == rows - SUB:
                near = jnp.broadcast_to(halo[1, 0, f, t, pl.ds(k, 1), :], (SUB, LANES))
                far = jnp.broadcast_to(halo[1, 1, f, t, pl.ds(k, 1), :], (SUB, LANES))
                second = jnp.where(sub8 == SUB - 1, far, jnp.where(sub8 == SUB - 2, near, 0.0))
                near = 8.0 * jnp.where(sub8 == SUB - 1, near, 0.0)
                lat_d[f] = add(lat_d[f], near - second)
                lat_b[f] = add(lat_b[f], 2.0 * near - second)
            ghost = mixed[f, k, strip]
            if t == 0:
                second = jnp.where(lane8 < 2, ghost, 0.0)
                near = 8.0 * jnp.where(lane8 == 0, pltpu.roll(ghost, LANES - 1, 1), 0.0)
                lon_d[f] = add(lon_d[f], second - near)
                lon_b[f] = add(lon_b[f], 2.0 * near - second)
            if t == tiles - 1:
                second = jnp.where(lane8 >= LANES - 2, ghost, 0.0)
                near = 8.0 * jnp.where(lane8 == LANES - 1, pltpu.roll(ghost, 1, 1), 0.0)
                lon_d[f] = add(lon_d[f], near - second)
                lon_b[f] = add(lon_b[f], 2.0 * near - second)

        rates = [None] * 5
        diverge = None
        if lat_d[0] is not None:
            diverge = add(diverge, lat_scale * lat_d[2])
            rates[0] = add(rates[0], -go_lat * lat_d[0])
            for f in range(1, 5):
                rates[f] = add(
                    rates[f], curve_lat * lat_b[f] + (slope_extra - go_lat) * lat_d[f]
                )
            rates[2] -= lat_scale * (ratio * lat_d[0] + lat_d[4])
        if lon_d[0] is not None:
            diverge = add(diverge, lon_scale * lon_d[3])
            rates[0] = add(rates[0], -go_lon * lon_d[0])
            for f in range(1, 5):
                rates[f] = add(rates[f], curve_lon * lon_b[f] - go_lon * lon_d[f])
            rates[3] -= lon_scale * (ratio * lon_d[0] + lon_d[4])
        rates[0] -= rho * diverge
        rates[4] -= (GAMMA - 1.0) * (heat * diverge)
        for f in range(5):
            rate_box[f, k, strip, lanes] = rate_in[f, k, strip, lanes] + rates[f]
            state_box[f, k, strip, lanes] = (
                state_in[f, k, strip, lanes] + (0.25 * TIME_STEP) * rates[f]
            )

    for c in range(chunks):

        @pl.loop(c * chunk, (c + 1) * chunk)
        def _(k):
            one_level(k)

        for copy in out_copies(c):
            copy.start()
    for c in range(chunks):
        for copy in out_copies(c):
            copy.wait()


def edges(partners, turning, replies, sides, halos, block, row_box, inner):
    rate_out, state_out, rate_box, state_box = inner
    levels, rows, cols = rate_box.shape[1:]
    n_lat, n_lon = lax.axis_size("lat"), lax.axis_size("lon")
    chunk = 2
    out = jax.ShapeDtypeStruct(rate_out.shape, jnp.float32)
    box = pltpu.VMEM(rate_box.shape, jnp.float32)
    n_in = n_lat + 10
    return pl.pallas_call(
        functools.partial(edges_kernel, (n_lat, n_lon, levels, rows, cols), chunk),
        out_shape=(out, out),
        in_specs=[SMEM] + [VMEM] * (n_in - 1) + [ANY] * 2,
        out_specs=(ANY, ANY),
        input_output_aliases={n_in: 0, n_in + 1: 1},
        scratch_shapes=[
            box,
            box,
            pltpu.VMEM((n_lat,) + replies[0].shape, jnp.float32),
            pltpu.VMEM((2,) + halos[0].shape, jnp.float32),
            pltpu.VMEM((2, 2, rows, LANES), jnp.float32),
            pltpu.VMEM((5, levels, rows, LANES), jnp.float32),
            pltpu.SemaphoreType.DMA((levels // chunk, 4, 2)),
        ],
        compiler_params=pltpu.CompilerParams(vmem_limit_bytes=20 * MIB),
        cost_estimate=pl.CostEstimate(
            flops=40 * levels * rows * cols,
            bytes_accessed=40 * levels * rows * cols,
            transcendentals=0,
        ),
        name="edges",
    )(
        partners,
        turning,
        *replies,
        *sides,
        *halos,
        block,
        row_box,
        rate_box,
        state_box,
        rate_out,
        state_out,
    )


def shards(rho, flow, heat, outset, opposite_block, donor_lower_corner, blend, turning):
    levels, rows, cols = rho.shape[1:]
    n_lat = lax.axis_size("lat")
    request = ask(opposite_block, donor_lower_corner, blend, rows, cols)
    requests = [swap_panels(request, d) for d in range(n_lat)]
    cells, block, even_rows, odd_rows, even_cols, odd_cols, row_box, spin_box = prepare(
        rho, flow, heat
    )
    *requests, even_rows, odd_rows, even_cols, odd_cols = lax.optimization_barrier(
        (*requests, even_rows, odd_rows, even_cols, odd_cols)
    )
    sides = (swap_pairs(even_cols, "lon", False), swap_pairs(odd_cols, "lon", True))
    halos = (swap_pairs(even_rows, "lat", False), swap_pairs(odd_rows, "lat", True))
    replies = donate(requests, cells, rows, cols, 5 * levels)
    *replies, spin_box = lax.optimization_barrier((*replies, spin_box))
    *sides, spin_box = lax.optimization_barrier((*sides, spin_box))
    replies = [swap_panels(reply, d) for d, reply in enumerate(replies)]
    inner = stencil(block, row_box, spin_box, outset)
    return edges(opposite_block, turning, replies, sides, halos, block, row_box, inner)


def solution(mesh):
    in_specs = (
        P("panel", None, "lat", "lon"),
        P("panel", None, None, "lat", "lon"),
        P("panel", None, "lat", "lon"),
        P("panel", None, None, "lat", "lon"),
        P("panel", "lat", "lon", None),
        P("panel", "lat", "lon", None),
        P("panel", "lat", "lon", None, None),
        P("panel", "lat", "lon", None, None),
    )
    out_specs = (P("panel", None, None, "lat", "lon"), P("panel", None, None, "lat", "lon"))
    return jax.shard_map(shards, mesh=mesh, in_specs=in_specs, out_specs=out_specs, check_vma=False)
```

```python
import functools
import math

import jax
import jax.numpy as jnp
from jax import lax
from jax.experimental import pallas as pl
from jax.experimental.pallas import tpu as pltpu
from jax.sharding import PartitionSpec as P

OMEGA = 0.5
GRAVITY = 1.0
VISCOSITY = 0.2
DIFFUSIVITY = 0.2
GAMMA = 1.4
TIME_STEP = 0.05
LANES = 128
SUB = 8
MIB = 1024 * 1024
ANY = pl.BlockSpec(memory_space=pl.ANY)
HBM = pl.BlockSpec(memory_space=pltpu.HBM)
VMEM = pl.BlockSpec(memory_space=pltpu.VMEM)
SMEM = pl.BlockSpec(memory_space=pltpu.SMEM)


def in_hbm(value):
    return pltpu.with_memory_space_constraint(value, pltpu.HBM)


def pair_partner(i, count, odd, wrap):
    partner = i ^ 1 if not odd else (i + 1 if i % 2 else i - 1)
    if 0 <= partner < count:
        return partner
    return partner % count if wrap else i


def swap_pairs(value, axis, odd):
    count = lax.axis_size(axis)
    return lax.ppermute(value, axis, [(i, pair_partner(i, count, odd, axis == "lat")) for i in range(count)])


def swap_panels(value, distance):
    n_lat = lax.axis_size("lat")
    pairs = [
        (p * n_lat + a, (1 - p) * n_lat + (a ^ distance)) for p in range(2) for a in range(n_lat)
    ]
    return lax.ppermute(value, ("panel", "lat"), pairs)


def window_of(run, cols):
    tiles = cols // LANES
    for width in range(1, tiles + 1):
        if all(
            start - min(start // LANES, tiles - width) * LANES + run <= width * LANES
            for start in range(0, cols, run)
        ):
            return width
    return tiles


def ask_kernel(partners, corners, blend, request, partners_box, corners_box, blend_box, sems):
    lat_len = corners.shape[-1] - request.shape[-1]
    copies = [
        pltpu.make_async_copy(partners, partners_box, sems.at[0]),
        pltpu.make_async_copy(corners, corners_box, sems.at[1]),
        pltpu.make_async_copy(blend, blend_box, sems.at[2]),
    ]
    for copy in copies:
        copy.start()
    for copy in copies:
        copy.wait()
    north = lax.axis_index("lat") == 0
    for row, source in ((0, partners_box), (1, corners_box)):
        values = source[0, 0].astype(jnp.float32)
        request[row : row + 1, 0:lat_len] = jnp.where(
            north, values[:, 0:lat_len], values[:, lat_len : 2 * lat_len]
        )
        request[row : row + 1, lat_len:] = values[:, 2 * lat_len :]
    weights = blend_box[0, 0, 0]
    request[2:6, 0:lat_len] = jnp.where(
        north, weights[:, 0:lat_len], weights[:, lat_len : 2 * lat_len]
    )
    request[2:6, lat_len:] = weights[:, 2 * lat_len :]


def ask(partners, corners, blend, rows, cols):
    return pl.pallas_call(
        ask_kernel,
        out_shape=jax.ShapeDtypeStruct((SUB, 2 * cols + 4 * rows), jnp.float32),
        in_specs=[HBM] * 3,
        out_specs=VMEM,
        scratch_shapes=[
            pltpu.VMEM(partners.shape, jnp.int32),
            pltpu.VMEM(corners.shape, jnp.int32),
            pltpu.VMEM(blend.shape, jnp.float32),
            pltpu.SemaphoreType.DMA((3,)),
        ],
        compiler_params=pltpu.CompilerParams(vmem_limit_bytes=MIB),
        name="ask",
    )(*(in_hbm(x) for x in (partners, corners, blend)))


def prepare_kernel(
    n_lat,
    n_lon,
    rho,
    flow,
    heat,
    cells,
    block,
    even_rows,
    odd_rows,
    even_cols,
    odd_cols,
    row_box,
    spin_box,
    staged,
    sems,
):
    levels, rows, cols = rho.shape[1:]
    tiles = cols // LANES
    strips = rows // SUB

    def load_copies(strip):
        here = pl.ds(strip * SUB, SUB)
        return (
            pltpu.make_async_copy(rho.at[0, :, here], staged.at[0, :, here], sems.at[strip, 0]),
            pltpu.make_async_copy(
                flow.at[0, :, :, here], staged.at[pl.ds(1, 3), :, here], sems.at[strip, 1]
            ),
            pltpu.make_async_copy(heat.at[0, :, here], staged.at[4, :, here], sems.at[strip, 2]),
        )

    for strip in range(strips):
        for copy in load_copies(strip):
            copy.start()

    pitch = rows + 2 * SUB
    flat = block.reshape(5, tiles, levels * pitch, LANES)

    def level_rows(field, tile, row):
        return flat[field, tile, pl.ds(SUB + row, levels, stride=pitch), :]

    zero = jnp.zeros((levels, SUB, LANES), jnp.float32)
    for field in range(5):
        for tile in range(tiles):
            block[field, tile, :, 0:SUB] = zero
            block[field, tile, :, rows + SUB :] = zero

    step_lat = math.pi / 2.0 / (rows * n_lat)
    step_lon = 1.5 * math.pi / (cols * n_lon)
    sub = lax.broadcasted_iota(jnp.int32, (rows, LANES), 0)
    row_global = (lax.axis_index("lat") * rows + sub).astype(jnp.float32)
    theta = math.pi / 4.0 + (row_global + 0.5) * step_lat
    sin_lat, cos_lat = jnp.sin(theta), jnp.cos(theta)
    row_box[0] = 1.0 / sin_lat
    row_box[1] = cos_lat / sin_lat
    yang = lax.axis_index("panel").astype(jnp.float32)
    yin = 1.0 - yang
    for tile in range(tiles):
        lane = lax.broadcasted_iota(jnp.int32, (SUB, LANES), 1) + tile * LANES
        col_global = (lax.axis_index("lon") * cols + lane).astype(jnp.float32)
        longitude = -0.75 * math.pi + (col_global + 0.5) * step_lon
        sin_lon, cos_lon = jnp.sin(longitude)[0:1], jnp.cos(longitude)[0:1]
        spin_box[0, tile] = 2.0 * OMEGA * (yin * cos_lat + yang * sin_lat * sin_lon)
        spin_box[1, tile] = 2.0 * OMEGA * (yang * cos_lat * sin_lon - yin * sin_lat)
        spin_box[2, tile] = jnp.broadcast_to(2.0 * OMEGA * yang * cos_lon, (rows, LANES))

    for strip in range(strips):
        for copy in load_copies(strip):
            copy.wait()
        here, there = strip * SUB, (strip + 1) * SUB
        for field in range(5):
            for tile in range(tiles):
                block[field, tile, :, there : there + SUB] = staged[
                    field, :, here:there, tile * LANES : (tile + 1) * LANES
                ]
        for row in range(here, there):
            for tile in range(tiles):
                stack = jnp.concatenate([level_rows(f, tile, row) for f in range(5)], axis=0)
                at = row * cols + tile * LANES
                cells[at : at + LANES, 0 : 5 * levels] = stack.T

    lat_even = lax.rem(lax.axis_index("lat"), 2) == 0
    for first, to_even in ((0, jnp.logical_not(lat_even)), (rows - 2, lat_even)):
        for keep, out in ((to_even, even_rows), (jnp.logical_not(to_even), odd_rows)):

            @pl.when(keep)
            def _(first=first, out=out):
                for layer in range(2):
                    for field in range(5):
                        for tile in range(tiles):
                            out[layer, field, tile] = level_rows(field, tile, first + layer)

    lon_even = lax.rem(lax.axis_index("lon"), 2) == 0
    for first, to_even in ((0, jnp.logical_not(lon_even)), (cols - 2, lon_even)):
        for keep, out in ((to_even, even_cols), (jnp.logical_not(to_even), odd_cols)):

            @pl.when(keep)
            def _(first=first, out=out):
                for layer in range(2):
                    for row in range(rows):
                        at = row * cols + first + layer
                        out[layer, row : row + 1, :] = cells[at : at + 1, :]


def prepare(rho, flow, heat):
    levels, rows, cols = rho.shape[1:]
    tiles = cols // LANES
    shapes = (
        (rows * cols, LANES),
        (5, tiles, levels, rows + 2 * SUB, LANES),
        (2, 5, tiles, levels, LANES),
        (2, 5, tiles, levels, LANES),
        (2, rows, LANES),
        (2, rows, LANES),
        (2, rows, LANES),
        (3, tiles, rows, LANES),
    )
    return pl.pallas_call(
        functools.partial(prepare_kernel, lax.axis_size("lat"), lax.axis_size("lon")),
        out_shape=tuple(jax.ShapeDtypeStruct(shape, jnp.float32) for shape in shapes),
        in_specs=[ANY] * 3,
        out_specs=(VMEM,) * len(shapes),
        scratch_shapes=[
            pltpu.VMEM((5, levels, rows, cols), jnp.float32),
            pltpu.SemaphoreType.DMA((rows // SUB, 3)),
        ],
        compiler_params=pltpu.CompilerParams(vmem_limit_bytes=16 * MIB),
        name="prepare",
    )(*(in_hbm(x) for x in (rho, flow, heat)))


def donate_kernel(n_lat, n_lon, rows, cols, field_rows, *refs):
    weights = refs[:n_lat]
    cells = refs[n_lat]
    replies = refs[n_lat + 1 : 2 * n_lat + 1]
    corners, turned, gathered, whole_box, requests, sems = refs[2 * n_lat + 1 :]
    slots = weights[0].shape[1]
    lat_len, lon_len = 2 * cols, 2 * rows
    for distance in range(n_lat):
        for row in range(2):
            for tile in range(slots // LANES):
                lanes = slice(tile * LANES, (tile + 1) * LANES)
                whole_box[distance, row, tile : tile + 1] = weights[distance][
                    row : row + 1, lanes
                ].astype(jnp.int32)
    copy = pltpu.make_async_copy(whole_box, requests, sems.at[0])
    copy.start()
    for distance in range(n_lat):
        for at in range(lat_len, slots, LANES):
            turned[distance, at : at + LANES, 0:SUB] = weights[distance][:, at : at + LANES].T
        asker = jnp.bitwise_xor(lax.axis_index("lat"), distance)

        @pl.when((asker == 0) | (asker == n_lat - 1))
        def _(distance=distance):
            for at in range(0, lat_len, LANES):
                turned[distance, at : at + LANES, 0:SUB] = weights[distance][:, at : at + LANES].T

    copy.wait()
    lat_len, lon_len = 2 * cols, 2 * rows
    run_lat, run_lon = lat_len // n_lat, lon_len // n_lat
    tiles = cols // LANES
    width = window_of(run_lat, cols)
    lat_here = lax.axis_index("lat")
    lon_here = lax.axis_index("lon")

    def word(request, row, slot):
        return requests[request, row, lax.shift_right_logical(slot, 7), jnp.bitwise_and(slot, 127)]

    def find_run(request, start, run):
        start = jnp.int32(start)
        found = jnp.int32(0)
        for r in range(1, n_lat):
            match = word(request, 0, start + r * run) == lat_here
            found = jnp.where(match, jnp.int32(r), found)
        return found

    def gather(request, first, count):
        def step(i, carry):
            for u in range(SUB):
                t = i * SUB + u
                cell = word(request, 1, first + t)
                for j, shift in enumerate((0, cols, 1, cols + 1)):
                    corners[j, pl.ds(t, 1), :] = cells[pl.ds(cell + shift, 1), :]
            return carry

        lax.fori_loop(0, count // SUB, step, 0)

    def blend(distance, first, count):
        rows_here = pl.ds(pl.multiple_of(first, SUB), count)
        total = None
        for j in range(4):
            weight = jnp.broadcast_to(turned[distance, rows_here, 2 + j : 3 + j], (count, LANES))
            part = weight * corners[j, 0:count, :]
            total = part if total is None else total + part
        return total

    for distance in range(n_lat):
        request, reply = distance, replies[distance]
        asker = jnp.bitwise_xor(lat_here, distance)

        @pl.when((asker == 0) | (asker == n_lat - 1))
        def _(distance=distance, request=request, reply=reply):
            run = find_run(request, 0, run_lat)
            start = lax.rem(run * run_lat, cols)
            base = jnp.minimum(lax.div(start, LANES), tiles - width)
            offset = pl.multiple_of(start - base * LANES, SUB)
            gather(request, run * run_lat, run_lat)
            gathered[pl.ds(offset, run_lat), :] = blend(distance, run * run_lat, run_lat)
            for tile in range(width):
                block = gathered[tile * LANES : (tile + 1) * LANES, :]
                reply[0:field_rows, tile * LANES : (tile + 1) * LANES] = block.T[0:field_rows]

        @pl.when((lon_here == 0) | (lon_here == n_lon - 1))
        def _(distance=distance, request=request, reply=reply):
            first = lat_len + jnp.where(lon_here == 0, 0, lon_len)
            run = find_run(request, first, run_lon)
            gather(request, first + run * run_lon, run_lon)
            reply[field_rows : field_rows + run_lon, 0:LANES] = blend(
                distance, first + run * run_lon, run_lon
            )


def donate(requests, cells, rows, cols, field_rows):
    n_lat, n_lon = lax.axis_size("lat"), lax.axis_size("lon")
    run_lat = 2 * cols // n_lat
    width = window_of(run_lat, cols)
    slots = requests[0].shape[1]
    words = (pl.cdiv(slots, SUB * LANES) * SUB, LANES)
    reply = jax.ShapeDtypeStruct((field_rows + 2 * rows // n_lat, width * LANES), jnp.float32)
    return pl.pallas_call(
        functools.partial(donate_kernel, n_lat, n_lon, rows, cols, field_rows),
        out_shape=(reply,) * n_lat,
        in_specs=[VMEM] * (n_lat + 1),
        out_specs=(VMEM,) * n_lat,
        scratch_shapes=[
            pltpu.VMEM((4, max(run_lat, 2 * rows // n_lat), LANES), jnp.float32),
            pltpu.VMEM((n_lat, slots, LANES), jnp.float32),
            pltpu.VMEM((width * LANES, LANES), jnp.float32),
            pltpu.VMEM((n_lat, 2) + words, jnp.int32),
            pltpu.SMEM((n_lat, 2) + words, jnp.int32),
            pltpu.SemaphoreType.DMA((1,)),
        ],
        compiler_params=pltpu.CompilerParams(vmem_limit_bytes=9 * MIB),
        name="donate",
    )(*requests, cells)


def core_parts(rows, tiles):
    return (SUB, rows - 2 * SUB, LANES, (tiles - 2) * LANES)


def edge_parts(rows, tiles):
    cols = tiles * LANES
    return (
        (0, SUB, 0, cols),
        (rows - SUB, SUB, 0, cols),
        (SUB, rows - 2 * SUB, 0, LANES),
        (SUB, rows - 2 * SUB, cols - LANES, LANES),
    )


def part_copies(boxes, outs, part, span, sems):
    first, count, lane, lanes = part
    at = (span, pl.ds(first, count), pl.ds(lane, lanes))
    return [
        pltpu.make_async_copy(box.at[(slice(None),) + at], out.at[(0, slice(None)) + at], sems.at[n])
        for n, (box, out) in enumerate(zip(boxes, outs))
    ]


def stencil_kernel(
    geometry, chunk, block, row_box, spin_box, outset, rate_out, state_out, rate_box, state_box, sems
):
    n_lat, n_lon, levels, rows, cols = geometry
    tiles = cols // LANES
    step_lat = math.pi / 2.0 / (rows * n_lat)
    step_lon = 1.5 * math.pi / (cols * n_lon)
    chunks = levels // chunk
    by_lat = 1.0 / (12.0 * step_lat)
    by_lon = 1.0 / (12.0 * step_lon)
    lane8 = lax.broadcasted_iota(jnp.int32, (SUB, LANES), 1)

    def out_copies(c):
        return part_copies(
            (rate_box, state_box),
            (rate_out, state_out),
            core_parts(rows, tiles),
            pl.ds(c * chunk, chunk),
            sems.at[c],
        )

    def one_level(k):
        below = jnp.maximum(k - 1, 0)
        above = jnp.minimum(k + 1, levels - 1)
        radius = jnp.broadcast_to(1.0 / step_lat + k.astype(jnp.float32), (SUB, LANES))
        inv_radius = 1.0 / radius
        for top in range(SUB, rows - SUB, SUB):
            one_strip(k, below, above, inv_radius, inv_radius * by_lat, top)

    def one_strip(k, below, above, inv_radius, lat_scale, top):
        strip = slice(top, top + SUB)
        inv_sin, cot = row_box[0, strip], row_box[1, strip]
        inv_arc = inv_radius * inv_sin
        lon_scale = inv_arc * by_lon
        cot_r = cot * inv_radius
        two_r = 2.0 * inv_radius
        curve_lat = (VISCOSITY / (12.0 * step_lat * step_lat)) * inv_radius * inv_radius
        curve_lon = (VISCOSITY / (12.0 * step_lon * step_lon)) * inv_arc * inv_arc
        slope_extra = (VISCOSITY * by_lat) * inv_radius * cot_r
        radial_extra = VISCOSITY * inv_radius
        center_weight = 2.0 * VISCOSITY + 30.0 * (curve_lat + curve_lon)

        def derive(f, full):
            here = [block[f, t, k, SUB + top : 2 * SUB + top] for t in range(tiles)]
            w1s = [pltpu.roll(x, 1, 1) for x in here]
            w2s = [pltpu.roll(x, 2, 1) for x in here]
            e1s = [pltpu.roll(x, LANES - 1, 1) for x in here]
            e2s = [pltpu.roll(x, LANES - 2, 1) for x in here]
            out = []
            for t in range(tiles):
                at = SUB + top
                n1, n2 = block[f, t, k, at - 1 : at + 7], block[f, t, k, at - 2 : at + 6]
                s1, s2 = block[f, t, k, at + 1 : at + 9], block[f, t, k, at + 2 : at + 10]
                w1 = jnp.where(lane8 == 0, w1s[t - 1] if t else 0.0, w1s[t])
                w2 = jnp.where(lane8 < 2, w2s[t - 1] if t else 0.0, w2s[t])
                last = t == tiles - 1
                e1 = jnp.where(lane8 == LANES - 1, 0.0 if last else e1s[t + 1], e1s[t])
                e2 = jnp.where(lane8 >= LANES - 2, 0.0 if last else e2s[t + 1], e2s[t])
                low = block[f, t, below, SUB + top : 2 * SUB + top]
                high = block[f, t, above, SUB + top : 2 * SUB + top]
                rad = high - low
                lat = 8.0 * (s1 - n1) - (s2 - n2)
                lon = 8.0 * (e1 - w1) - (e2 - w2)
                bend = None
                if full:
                    bend = (
                        VISCOSITY * (high + low)
                        + curve_lat * (16.0 * (s1 + n1) - (s2 + n2))
                        + curve_lon * (16.0 * (e1 + w1) - (e2 + w2))
                        - center_weight * here[t]
                    )
                out.append((rad, lat, lon, bend))
            return here, out

        wind_rad = [block[1, t, k, SUB + top : 2 * SUB + top] for t in range(tiles)]
        wind_lat = [block[2, t, k, SUB + top : 2 * SUB + top] for t in range(tiles)]
        wind_lon = [block[3, t, k, SUB + top : 2 * SUB + top] for t in range(tiles)]
        go_rad = [0.5 * x for x in wind_rad]
        go_lat = [lat_scale * x for x in wind_lat]
        go_lon = [lon_scale * x for x in wind_lon]

        def put(f, t, center, rate):
            lanes = slice(t * LANES, (t + 1) * LANES)
            rate_box[f, k, strip, lanes] = rate
            state_box[f, k, strip, lanes] = (
                0.75 * outset[0, f, k, strip, lanes] + 0.25 * center
            ) + (0.25 * TIME_STEP) * rate

        rho_here, rho_d = derive(0, False)
        heat_here, heat_d = derive(4, True)
        ratio = [heat_here[t] / rho_here[t] for t in range(tiles)]
        press, rho_rate, heat_rate = [], [], []
        for t in range(tiles):
            (a, b, c, _), (d, e, g, bend) = rho_d[t], heat_d[t]
            press.append(
                (
                    0.5 * (ratio[t] * a + d),
                    lat_scale * (ratio[t] * b + e),
                    lon_scale * (ratio[t] * c + g),
                )
            )
            rho_rate.append(go_rad[t] * a + go_lat[t] * b + go_lon[t] * c)
            heat_rate.append(
                bend
                + (radial_extra - go_rad[t]) * d
                + (slope_extra - go_lat[t]) * e
                - go_lon[t] * g
            )
        diverge = [two_r * wind_rad[t] + cot_r * wind_lat[t] for t in range(tiles)]
        for f in (1, 2, 3):
            here, d_all = derive(f, True)
            for t in range(tiles):
                d, e, g, bend = d_all[t]
                spin_rad, spin_lat = spin_box[0, t, strip], spin_box[1, t, strip]
                spin_lon = spin_box[2, t, strip]
                rate = (
                    bend
                    + (radial_extra - go_rad[t]) * d
                    + (slope_extra - go_lat[t]) * e
                    - go_lon[t] * g
                    - press[t][f - 1]
                )
                if f == 1:
                    diverge[t] += 0.5 * d
                    rate += inv_radius * (wind_lat[t] * wind_lat[t] + wind_lon[t] * wind_lon[t])
                    rate += spin_lon * wind_lat[t] - spin_lat * wind_lon[t] - GRAVITY
                elif f == 2:
                    diverge[t] += lat_scale * e
                    rate += cot_r * (wind_lon[t] * wind_lon[t])
                    rate -= inv_radius * (wind_rad[t] * wind_lat[t])
                    rate += spin_rad * wind_lon[t] - spin_lon * wind_rad[t]
                else:
                    diverge[t] += lon_scale * g
                    rate -= (inv_radius * wind_rad[t] + cot_r * wind_lat[t]) * wind_lon[t]
                    rate += spin_lat * wind_rad[t] - spin_rad * wind_lat[t]
                put(f, t, here[t], rate)
        for t in range(tiles):
            put(0, t, rho_here[t], -rho_rate[t] - rho_here[t] * diverge[t])
            put(
                4,
                t,
                heat_here[t],
                heat_rate[t] - (GAMMA - 1.0) * (heat_here[t] * diverge[t]),
            )

    for c in range(chunks):

        @pl.loop(c * chunk, (c + 1) * chunk)
        def _(k):
            one_level(k)

        for copy in out_copies(c):
            copy.start()
    for c in range(chunks):
        for copy in out_copies(c):
            copy.wait()


def stencil(block, row_box, spin_box, outset):
    levels, rows, cols = outset.shape[2:]
    n_lat, n_lon = lax.axis_size("lat"), lax.axis_size("lon")
    chunk = 4
    out = jax.ShapeDtypeStruct(outset.shape, jnp.float32)
    box = jax.ShapeDtypeStruct(outset.shape[1:], jnp.float32)
    return pl.pallas_call(
        functools.partial(stencil_kernel, (n_lat, n_lon, levels, rows, cols), chunk),
        out_shape=(out, out, box, box),
        in_specs=[VMEM] * 4,
        out_specs=(ANY, ANY, VMEM, VMEM),
        scratch_shapes=[pltpu.SemaphoreType.DMA((levels // chunk, 2))],
        compiler_params=pltpu.CompilerParams(vmem_limit_bytes=20 * MIB),
        cost_estimate=pl.CostEstimate(
            flops=125 * levels * rows * cols,
            bytes_accessed=80 * levels * rows * cols,
            transcendentals=0,
        ),
        name="stencil",
    )(block, row_box, spin_box, outset)


def edges_kernel(geometry, chunk, *refs):
    n_lat, n_lon, levels, rows, cols = geometry
    tiles = cols // LANES
    field_rows = 5 * levels
    partners, turning = refs[:2]
    reply_box = refs[2 : 2 + n_lat]
    (
        lon_even,
        lon_odd,
        lat_even,
        lat_odd,
        block,
        row_box,
        spin_box,
        outset,
        rate_in,
        state_in,
        _,
        _,
        rate_out,
        state_out,
        rate_box,
        state_box,
        replies,
        halo,
        side,
        mixed,
        sems,
    ) = refs[2 + n_lat :]
    lat_here = lax.axis_index("lat")
    lon_here = lax.axis_index("lon")
    lat_len, lon_len = 2 * cols, 2 * rows
    run_lat, run_lon = lat_len // n_lat, lon_len // n_lat
    width = window_of(run_lat, cols)
    step_lat = math.pi / 2.0 / (rows * n_lat)
    step_lon = 1.5 * math.pi / (cols * n_lon)
    by_lat = 1.0 / (12.0 * step_lat)
    by_lon = 1.0 / (12.0 * step_lon)
    chunks = levels // chunk
    parts = edge_parts(rows, tiles)

    def out_copies(c):
        out = []
        for n, part in enumerate(parts):
            out += part_copies(
                (rate_box, state_box),
                (rate_out, state_out),
                part,
                pl.ds(c * chunk, chunk),
                sems.at[c, n],
            )
        return out

    lat_is_even = lax.rem(lat_here, 2) == 0
    lon_is_even = lax.rem(lon_here, 2) == 0
    for even, north, south in ((True, lat_odd, lat_even), (False, lat_even, lat_odd)):

        @pl.when(lat_is_even == even)
        def _(north=north, south=south):
            halo[0] = north[...]
            halo[1] = south[...]

    for even, west, east in ((True, lon_odd, lon_even), (False, lon_even, lon_odd)):

        @pl.when(lon_is_even == even)
        def _(west=west, east=east):
            side[0] = west[...]
            side[1] = east[...]

    @pl.when((lat_here == 0) | (lat_here == n_lat - 1) | (lon_here == 0) | (lon_here == n_lon - 1))
    def _():
        for d in range(n_lat):
            replies[d] = reply_box[d][...]

    lane8 = lax.broadcasted_iota(jnp.int32, (SUB, LANES), 1)
    sub8 = lax.broadcasted_iota(jnp.int32, (SUB, LANES), 0)

    for which, slot0 in ((0, 0), (1, lat_len)):

        @pl.when(lat_here == (0 if which == 0 else n_lat - 1))
        def _(which=which, slot0=slot0):
            sources = [
                jnp.bitwise_xor(partners[0, 0, 0, slot0 + r * run_lat], lat_here) for r in range(n_lat)
            ]
            for layer in range(2):
                for t in range(tiles):
                    lane = lax.broadcasted_iota(jnp.int32, (field_rows, LANES), 1) + t * LANES
                    value = None
                    for r in range(n_lat):
                        first = r * run_lat - layer * cols
                        if first < 0 or first >= cols:
                            continue
                        if first >= (t + 1) * LANES or first + run_lat <= t * LANES:
                            continue
                        base = min(first // LANES, tiles - width)
                        here = (t - base) * LANES
                        piece = replies[sources[r], 0:field_rows, here : here + LANES]
                        value = piece if value is None else jnp.where(lane >= first, piece, value)
                    spot = slot0 + layer * cols + t * LANES
                    cosine = turning[0, 0, 0, 0:1, spot : spot + LANES]
                    sine = turning[0, 0, 0, 1:2, spot : spot + LANES]
                    parts = [value[f * levels : (f + 1) * levels] for f in range(5)]
                    parts[2], parts[3] = (
                        cosine * parts[2] + sine * parts[3],
                        cosine * parts[3] - sine * parts[2],
                    )
                    for f in range(5):
                        halo[which, layer, f, t] = parts[f]

    turn_lon = jnp.concatenate(
        [turning[0, 0, 0, :, 2 * lat_len :], jnp.zeros((SUB - 2, 2 * lon_len), jnp.float32)], axis=0
    ).T

    for which, slot0 in ((0, 2 * lat_len), (1, 2 * lat_len + lon_len)):
        @pl.when(lon_here == (0 if which == 0 else n_lon - 1))
        def _(which=which, slot0=slot0):
            lane = lax.broadcasted_iota(jnp.int32, (run_lon, LANES), 1)
            is_lat = (lane >= 2 * levels) & (lane < 3 * levels)
            is_lon = (lane >= 3 * levels) & (lane < 4 * levels)
            for r in range(n_lat):
                source = jnp.bitwise_xor(partners[0, 0, 0, slot0 + r * run_lon], lat_here)
                layer, first = r * run_lon // rows, r * run_lon % rows
                value = replies[source, field_rows : field_rows + run_lon, 0:LANES]
                slots = slice(which * lon_len + r * run_lon, which * lon_len + (r + 1) * run_lon)
                cosine = jnp.broadcast_to(turn_lon[slots, 0:1], (run_lon, LANES))
                sine = jnp.broadcast_to(turn_lon[slots, 1:2], (run_lon, LANES))
                later = pltpu.roll(value, LANES - levels, 1)
                earlier = pltpu.roll(value, levels, 1)
                value = jnp.where(
                    is_lat,
                    cosine * value + sine * later,
                    jnp.where(is_lon, cosine * value - sine * earlier, value),
                )
                side[which, layer, first : first + run_lon] = value

    lane_all = lax.broadcasted_iota(jnp.int32, (rows, LANES), 1)
    columns = [side[1, 0], side[1, 1], side[0, 0], side[0, 1]]
    columns = [columns[0]] + [pltpu.roll(columns[j], j, 1) for j in range(1, 4)]
    for q in range(4):
        pick = jnp.bitwise_and(lane_all - q, 3)
        value = columns[0]
        for j in range(1, 4):
            value = jnp.where(pick == j, columns[j], value)
        for row in range(q, field_rows, 4):
            mixed[row // levels, row % levels] = pltpu.roll(value, LANES - 2 - row, 1)

    def one_level(k):
        below = jnp.maximum(k - 1, 0)
        above = jnp.minimum(k + 1, levels - 1)
        radius = jnp.broadcast_to(1.0 / step_lat + k.astype(jnp.float32), (SUB, LANES))
        inv_radius = 1.0 / radius
        for top in range(0, rows, SUB):
            if top in (0, rows - SUB):
                one_strip(k, below, above, inv_radius, inv_radius * by_lat, top)
            else:
                for t in (0, tiles - 1):
                    one_tile(k, inv_radius, top, t)

    def one_strip(k, below, above, inv_radius, lat_scale, top):
        strip = slice(top, top + SUB)
        inv_sin, cot = row_box[0, strip], row_box[1, strip]
        inv_arc = inv_radius * inv_sin
        lon_scale = inv_arc * by_lon
        cot_r = cot * inv_radius
        two_r = 2.0 * inv_radius
        curve_lat = (VISCOSITY / (12.0 * step_lat * step_lat)) * inv_radius * inv_radius
        curve_lon = (VISCOSITY / (12.0 * step_lon * step_lon)) * inv_arc * inv_arc
        slope_extra = (VISCOSITY * by_lat) * inv_radius * cot_r
        radial_extra = VISCOSITY * inv_radius
        center_weight = 2.0 * VISCOSITY + 30.0 * (curve_lat + curve_lon)
        north, south = top == 0, top == rows - SUB

        def derive(f, full):
            here = [block[f, t, k, SUB + top : 2 * SUB + top] for t in range(tiles)]
            ghost = mixed[f, k, strip]
            ghost_w, ghost_e = pltpu.roll(ghost, LANES - 1, 1), pltpu.roll(ghost, 1, 1)
            w1s = [pltpu.roll(x, 1, 1) for x in here]
            w2s = [pltpu.roll(x, 2, 1) for x in here]
            e1s = [pltpu.roll(x, LANES - 1, 1) for x in here]
            e2s = [pltpu.roll(x, LANES - 2, 1) for x in here]
            out = []
            for t in range(tiles):
                at = SUB + top
                n1, n2 = block[f, t, k, at - 1 : at + 7], block[f, t, k, at - 2 : at + 6]
                s1, s2 = block[f, t, k, at + 1 : at + 9], block[f, t, k, at + 2 : at + 10]
                if north:
                    g2 = jnp.broadcast_to(halo[0, 0, f, t, pl.ds(k, 1), :], (SUB, LANES))
                    g1 = jnp.broadcast_to(halo[0, 1, f, t, pl.ds(k, 1), :], (SUB, LANES))
                    n1 = jnp.where(sub8 == 0, g1, n1)
                    n2 = jnp.where(sub8 == 0, g2, jnp.where(sub8 == 1, g1, n2))
                if south:
                    g1 = jnp.broadcast_to(halo[1, 0, f, t, pl.ds(k, 1), :], (SUB, LANES))
                    g2 = jnp.broadcast_to(halo[1, 1, f, t, pl.ds(k, 1), :], (SUB, LANES))
                    s1 = jnp.where(sub8 == SUB - 1, g1, s1)
                    s2 = jnp.where(sub8 == SUB - 1, g2, jnp.where(sub8 == SUB - 2, g1, s2))
                w1 = jnp.where(lane8 == 0, w1s[t - 1] if t else ghost_w, w1s[t])
                w2 = jnp.where(lane8 < 2, w2s[t - 1] if t else ghost, w2s[t])
                last = t == tiles - 1
                e1 = jnp.where(lane8 == LANES - 1, ghost_e if last else e1s[t + 1], e1s[t])
                e2 = jnp.where(lane8 >= LANES - 2, ghost if last else e2s[t + 1], e2s[t])
                low = block[f, t, below, SUB + top : 2 * SUB + top]
                high = block[f, t, above, SUB + top : 2 * SUB + top]
                rad = high - low
                lat = 8.0 * (s1 - n1) - (s2 - n2)
                lon = 8.0 * (e1 - w1) - (e2 - w2)
                bend = None
                if full:
                    bend = (
                        VISCOSITY * (high + low)
                        + curve_lat * (16.0 * (s1 + n1) - (s2 + n2))
                        + curve_lon * (16.0 * (e1 + w1) - (e2 + w2))
                        - center_weight * here[t]
                    )
                out.append((rad, lat, lon, bend))
            return here, out

        wind_rad = [block[1, t, k, SUB + top : 2 * SUB + top] for t in range(tiles)]
        wind_lat = [block[2, t, k, SUB + top : 2 * SUB + top] for t in range(tiles)]
        wind_lon = [block[3, t, k, SUB + top : 2 * SUB + top] for t in range(tiles)]
        go_rad = [0.5 * x for x in wind_rad]
        go_lat = [lat_scale * x for x in wind_lat]
        go_lon = [lon_scale * x for x in wind_lon]

        def put(f, t, center, rate):
            lanes = slice(t * LANES, (t + 1) * LANES)
            rate_box[f, k, strip, lanes] = rate
            state_box[f, k, strip, lanes] = (
                0.75 * outset[0, f, k, strip, lanes] + 0.25 * center
            ) + (0.25 * TIME_STEP) * rate

        rho_here, rho_d = derive(0, False)
        heat_here, heat_d = derive(4, True)
        ratio = [heat_here[t] / rho_here[t] for t in range(tiles)]
        press, rho_rate, heat_rate = [], [], []
        for t in range(tiles):
            (a, b, c, _), (d, e, g, bend) = rho_d[t], heat_d[t]
            press.append(
                (
                    0.5 * (ratio[t] * a + d),
                    lat_scale * (ratio[t] * b + e),
                    lon_scale * (ratio[t] * c + g),
                )
            )
            rho_rate.append(go_rad[t] * a + go_lat[t] * b + go_lon[t] * c)
            heat_rate.append(
                bend
                + (radial_extra - go_rad[t]) * d
                + (slope_extra - go_lat[t]) * e
                - go_lon[t] * g
            )
        diverge = [two_r * wind_rad[t] + cot_r * wind_lat[t] for t in range(tiles)]
        for f in (1, 2, 3):
            here, d_all = derive(f, True)
            for t in range(tiles):
                d, e, g, bend = d_all[t]
                spin_rad, spin_lat = spin_box[0, t, strip], spin_box[1, t, strip]
                spin_lon = spin_box[2, t, strip]
                rate = (
                    bend
                    + (radial_extra - go_rad[t]) * d
                    + (slope_extra - go_lat[t]) * e
                    - go_lon[t] * g
                    - press[t][f - 1]
                )
                if f == 1:
                    diverge[t] += 0.5 * d
                    rate += inv_radius * (wind_lat[t] * wind_lat[t] + wind_lon[t] * wind_lon[t])
                    rate += spin_lon * wind_lat[t] - spin_lat * wind_lon[t] - GRAVITY
                elif f == 2:
                    diverge[t] += lat_scale * e
                    rate += cot_r * (wind_lon[t] * wind_lon[t])
                    rate -= inv_radius * (wind_rad[t] * wind_lat[t])
                    rate += spin_rad * wind_lon[t] - spin_lon * wind_rad[t]
                else:
                    diverge[t] += lon_scale * g
                    rate -= (inv_radius * wind_rad[t] + cot_r * wind_lat[t]) * wind_lon[t]
                    rate += spin_lat * wind_rad[t] - spin_rad * wind_lat[t]
                put(f, t, here[t], rate)
        for t in range(tiles):
            put(0, t, rho_here[t], -rho_rate[t] - rho_here[t] * diverge[t])
            put(
                4,
                t,
                heat_here[t],
                heat_rate[t] - (GAMMA - 1.0) * (heat_here[t] * diverge[t]),
            )

    def one_tile(k, inv_radius, top, t):
        strip, lanes = slice(top, top + SUB), slice(t * LANES, (t + 1) * LANES)
        inv_arc = inv_radius * row_box[0, strip]
        lon_scale = inv_arc * by_lon
        curve_lon = (VISCOSITY / (12.0 * step_lon * step_lon)) * inv_arc * inv_arc
        rho, _, _, wind_lon, heat = (
            block[f, t, k, SUB + top : 2 * SUB + top] for f in range(5)
        )
        go_lon = lon_scale * wind_lon
        ratio = heat / rho

        def add(total, value):
            return value if total is None else total + value

        lon_d, lon_b = ([None] * 5 for _ in range(2))
        for f in range(5):
            ghost = mixed[f, k, strip]
            if t == 0:
                second = jnp.where(lane8 < 2, ghost, 0.0)
                near = 8.0 * jnp.where(lane8 == 0, pltpu.roll(ghost, LANES - 1, 1), 0.0)
                lon_d[f] = add(lon_d[f], second - near)
                lon_b[f] = add(lon_b[f], 2.0 * near - second)
            if t == tiles - 1:
                second = jnp.where(lane8 >= LANES - 2, ghost, 0.0)
                near = 8.0 * jnp.where(lane8 == LANES - 1, pltpu.roll(ghost, 1, 1), 0.0)
                lon_d[f] = add(lon_d[f], near - second)
                lon_b[f] = add(lon_b[f], 2.0 * near - second)

        rates = [None] * 5
        diverge = None
        if lon_d[0] is not None:
            diverge = add(diverge, lon_scale * lon_d[3])
            rates[0] = add(rates[0], -go_lon * lon_d[0])
            for f in range(1, 5):
                rates[f] = add(rates[f], curve_lon * lon_b[f] - go_lon * lon_d[f])
            rates[3] -= lon_scale * (ratio * lon_d[0] + lon_d[4])
        rates[0] -= rho * diverge
        rates[4] -= (GAMMA - 1.0) * (heat * diverge)
        for f in range(5):
            rate_box[f, k, strip, lanes] = rate_in[f, k, strip, lanes] + rates[f]
            state_box[f, k, strip, lanes] = (
                state_in[f, k, strip, lanes] + (0.25 * TIME_STEP) * rates[f]
            )

    for c in range(chunks):

        @pl.loop(c * chunk, (c + 1) * chunk)
        def _(k):
            one_level(k)

        for copy in out_copies(c):
            copy.start()
    for c in range(chunks):
        for copy in out_copies(c):
            copy.wait()


def edges(
    partners, turning, replies, sides, halos, block, row_box, spin_box, outset, inner
):
    rate_out, state_out, rate_box, state_box = inner
    levels, rows, cols = rate_box.shape[1:]
    n_lat, n_lon = lax.axis_size("lat"), lax.axis_size("lon")
    chunk = 4
    out = jax.ShapeDtypeStruct(rate_out.shape, jnp.float32)
    box = pltpu.VMEM(rate_box.shape, jnp.float32)
    n_in = n_lat + 12
    return pl.pallas_call(
        functools.partial(edges_kernel, (n_lat, n_lon, levels, rows, cols), chunk),
        out_shape=(out, out),
        in_specs=[SMEM] + [VMEM] * (n_in - 1) + [ANY] * 2,
        out_specs=(ANY, ANY),
        input_output_aliases={n_in: 0, n_in + 1: 1},
        scratch_shapes=[
            box,
            box,
            pltpu.VMEM((n_lat,) + replies[0].shape, jnp.float32),
            pltpu.VMEM((2,) + halos[0].shape, jnp.float32),
            pltpu.VMEM((2, 2, rows, LANES), jnp.float32),
            pltpu.VMEM((5, levels, rows, LANES), jnp.float32),
            pltpu.SemaphoreType.DMA((levels // chunk, 4, 2)),
        ],
        compiler_params=pltpu.CompilerParams(vmem_limit_bytes=20 * MIB),
        cost_estimate=pl.CostEstimate(
            flops=150 * levels * rows * cols,
            bytes_accessed=40 * levels * rows * cols,
            transcendentals=0,
        ),
        name="edges",
    )(
        partners,
        turning,
        *replies,
        *sides,
        *halos,
        block,
        row_box,
        spin_box,
        outset,
        rate_box,
        state_box,
        rate_out,
        state_out,
    )


def shards(rho, flow, heat, outset, opposite_block, donor_lower_corner, blend, turning):
    levels, rows, cols = rho.shape[1:]
    n_lat = lax.axis_size("lat")
    request = ask(opposite_block, donor_lower_corner, blend, rows, cols)
    requests = [swap_panels(request, d) for d in range(n_lat)]
    cells, block, even_rows, odd_rows, even_cols, odd_cols, row_box, spin_box = prepare(
        rho, flow, heat
    )
    *requests, even_rows, odd_rows, even_cols, odd_cols = lax.optimization_barrier(
        (*requests, even_rows, odd_rows, even_cols, odd_cols)
    )
    sides = (swap_pairs(even_cols, "lon", False), swap_pairs(odd_cols, "lon", True))
    halos = (swap_pairs(even_rows, "lat", False), swap_pairs(odd_rows, "lat", True))
    replies = donate(requests, cells, rows, cols, 5 * levels)
    *replies, spin_box = lax.optimization_barrier((*replies, spin_box))
    *sides, spin_box = lax.optimization_barrier((*sides, spin_box))
    replies = [swap_panels(reply, d) for d, reply in enumerate(replies)]
    inner = stencil(block, row_box, spin_box, outset)
    return edges(opposite_block, turning, replies, sides, halos, block, row_box, spin_box, outset, inner)


def solution(mesh):
    in_specs = (
        P("panel", None, "lat", "lon"),
        P("panel", None, None, "lat", "lon"),
        P("panel", None, "lat", "lon"),
        P("panel", None, None, "lat", "lon"),
        P("panel", "lat", "lon", None),
        P("panel", "lat", "lon", None),
        P("panel", "lat", "lon", None, None),
        P("panel", "lat", "lon", None, None),
    )
    out_specs = (P("panel", None, None, "lat", "lon"), P("panel", None, None, "lat", "lon"))
    return jax.shard_map(shards, mesh=mesh, in_specs=in_specs, out_specs=out_specs, check_vma=False)
```

```python
import functools
import math

import jax
import jax.numpy as jnp
from jax import lax
from jax.experimental import pallas as pl
from jax.experimental.pallas import tpu as pltpu
from jax.sharding import PartitionSpec as P

OMEGA = 0.5
GRAVITY = 1.0
VISCOSITY = 0.2
DIFFUSIVITY = 0.2
GAMMA = 1.4
TIME_STEP = 0.05
LANES = 128
SUB = 8
MIB = 1024 * 1024
ANY = pl.BlockSpec(memory_space=pl.ANY)
HBM = pl.BlockSpec(memory_space=pltpu.HBM)
VMEM = pl.BlockSpec(memory_space=pltpu.VMEM)
SMEM = pl.BlockSpec(memory_space=pltpu.SMEM)


def in_hbm(value):
    return pltpu.with_memory_space_constraint(value, pltpu.HBM)


def pair_partner(i, count, odd, wrap):
    partner = i ^ 1 if not odd else (i + 1 if i % 2 else i - 1)
    if 0 <= partner < count:
        return partner
    return partner % count if wrap else i


def swap_pairs(value, axis, odd):
    count = lax.axis_size(axis)
    return lax.ppermute(value, axis, [(i, pair_partner(i, count, odd, axis == "lat")) for i in range(count)])


def swap_panels(value, distance):
    n_lat = lax.axis_size("lat")
    pairs = [
        (p * n_lat + a, (1 - p) * n_lat + (a ^ distance)) for p in range(2) for a in range(n_lat)
    ]
    return lax.ppermute(value, ("panel", "lat"), pairs)


def window_of(run, cols):
    tiles = cols // LANES
    for width in range(1, tiles + 1):
        if all(
            start - min(start // LANES, tiles - width) * LANES + run <= width * LANES
            for start in range(0, cols, run)
        ):
            return width
    return tiles


def ask_kernel(partners, corners, blend, request, partners_box, corners_box, blend_box, sems):
    lat_len = corners.shape[-1] - request.shape[-1]
    copies = [
        pltpu.make_async_copy(partners, partners_box, sems.at[0]),
        pltpu.make_async_copy(corners, corners_box, sems.at[1]),
        pltpu.make_async_copy(blend, blend_box, sems.at[2]),
    ]
    for copy in copies:
        copy.start()
    for copy in copies:
        copy.wait()
    north = lax.axis_index("lat") == 0
    for row, source in ((0, partners_box), (1, corners_box)):
        values = source[0, 0].astype(jnp.float32)
        request[row : row + 1, 0:lat_len] = jnp.where(
            north, values[:, 0:lat_len], values[:, lat_len : 2 * lat_len]
        )
        request[row : row + 1, lat_len:] = values[:, 2 * lat_len :]
    weights = blend_box[0, 0, 0]
    request[2:6, 0:lat_len] = jnp.where(
        north, weights[:, 0:lat_len], weights[:, lat_len : 2 * lat_len]
    )
    request[2:6, lat_len:] = weights[:, 2 * lat_len :]


def ask(partners, corners, blend, rows, cols):
    return pl.pallas_call(
        ask_kernel,
        out_shape=jax.ShapeDtypeStruct((SUB, 2 * cols + 4 * rows), jnp.float32),
        in_specs=[HBM] * 3,
        out_specs=VMEM,
        scratch_shapes=[
            pltpu.VMEM(partners.shape, jnp.int32),
            pltpu.VMEM(corners.shape, jnp.int32),
            pltpu.VMEM(blend.shape, jnp.float32),
            pltpu.SemaphoreType.DMA((3,)),
        ],
        compiler_params=pltpu.CompilerParams(vmem_limit_bytes=MIB),
        name="ask",
    )(*(in_hbm(x) for x in (partners, corners, blend)))


def prepare_kernel(
    n_lat,
    n_lon,
    rho,
    flow,
    heat,
    cells,
    block,
    even_rows,
    odd_rows,
    even_cols,
    odd_cols,
    row_box,
    spin_box,
    staged,
    sems,
):
    levels, rows, cols = rho.shape[1:]
    tiles = cols // LANES
    strips = rows // SUB

    def load_copies(strip):
        here = pl.ds(strip * SUB, SUB)
        return (
            pltpu.make_async_copy(rho.at[0, :, here], staged.at[0, :, here], sems.at[strip, 0]),
            pltpu.make_async_copy(
                flow.at[0, :, :, here], staged.at[pl.ds(1, 3), :, here], sems.at[strip, 1]
            ),
            pltpu.make_async_copy(heat.at[0, :, here], staged.at[4, :, here], sems.at[strip, 2]),
        )

    for strip in range(strips):
        for copy in load_copies(strip):
            copy.start()

    pitch = rows + 2 * SUB
    flat = block.reshape(5, tiles, levels * pitch, LANES)

    def level_rows(field, tile, row):
        return flat[field, tile, pl.ds(SUB + row, levels, stride=pitch), :]

    step_lat = math.pi / 2.0 / (rows * n_lat)
    step_lon = 1.5 * math.pi / (cols * n_lon)
    sub = lax.broadcasted_iota(jnp.int32, (rows, LANES), 0)
    row_global = (lax.axis_index("lat") * rows + sub).astype(jnp.float32)
    theta = math.pi / 4.0 + (row_global + 0.5) * step_lat
    sin_lat, cos_lat = jnp.sin(theta), jnp.cos(theta)
    row_box[0] = 1.0 / sin_lat
    row_box[1] = cos_lat / sin_lat
    yang = lax.axis_index("panel").astype(jnp.float32)
    yin = 1.0 - yang
    for tile in range(tiles):
        lane = lax.broadcasted_iota(jnp.int32, (SUB, LANES), 1) + tile * LANES
        col_global = (lax.axis_index("lon") * cols + lane).astype(jnp.float32)
        longitude = -0.75 * math.pi + (col_global + 0.5) * step_lon
        sin_lon, cos_lon = jnp.sin(longitude)[0:1], jnp.cos(longitude)[0:1]
        spin_box[0, tile] = 2.0 * OMEGA * (yin * cos_lat + yang * sin_lat * sin_lon)
        spin_box[1, tile] = 2.0 * OMEGA * (yang * cos_lat * sin_lon - yin * sin_lat)
        spin_box[2, tile] = jnp.broadcast_to(2.0 * OMEGA * yang * cos_lon, (rows, LANES))

    for strip in range(strips):
        for copy in load_copies(strip):
            copy.wait()
        here, there = strip * SUB, (strip + 1) * SUB
        for field in range(5):
            for tile in range(tiles):
                block[field, tile, :, there : there + SUB] = staged[
                    field, :, here:there, tile * LANES : (tile + 1) * LANES
                ]
        for row in range(here, there):
            for tile in range(tiles):
                stack = jnp.concatenate([level_rows(f, tile, row) for f in range(5)], axis=0)
                at = row * cols + tile * LANES
                cells[at : at + LANES, 0 : 5 * levels] = stack.T

    lat_even = lax.rem(lax.axis_index("lat"), 2) == 0
    for first, to_even in ((0, jnp.logical_not(lat_even)), (rows - 2, lat_even)):
        for keep, out in ((to_even, even_rows), (jnp.logical_not(to_even), odd_rows)):

            @pl.when(keep)
            def _(first=first, out=out):
                for layer in range(2):
                    for field in range(5):
                        for tile in range(tiles):
                            out[layer, field, tile] = level_rows(field, tile, first + layer)

    lon_even = lax.rem(lax.axis_index("lon"), 2) == 0
    for first, to_even in ((0, jnp.logical_not(lon_even)), (cols - 2, lon_even)):
        for keep, out in ((to_even, even_cols), (jnp.logical_not(to_even), odd_cols)):

            @pl.when(keep)
            def _(first=first, out=out):
                for layer in range(2):
                    for row in range(rows):
                        at = row * cols + first + layer
                        out[layer, row : row + 1, :] = cells[at : at + 1, :]


def prepare(rho, flow, heat):
    levels, rows, cols = rho.shape[1:]
    tiles = cols // LANES
    shapes = (
        (rows * cols, LANES),
        (5, tiles, levels, rows + 2 * SUB, LANES),
        (2, 5, tiles, levels, LANES),
        (2, 5, tiles, levels, LANES),
        (2, rows, LANES),
        (2, rows, LANES),
        (2, rows, LANES),
        (3, tiles, rows, LANES),
    )
    return pl.pallas_call(
        functools.partial(prepare_kernel, lax.axis_size("lat"), lax.axis_size("lon")),
        out_shape=tuple(jax.ShapeDtypeStruct(shape, jnp.float32) for shape in shapes),
        in_specs=[ANY] * 3,
        out_specs=(VMEM,) * len(shapes),
        scratch_shapes=[
            pltpu.VMEM((5, levels, rows, cols), jnp.float32),
            pltpu.SemaphoreType.DMA((rows // SUB, 3)),
        ],
        compiler_params=pltpu.CompilerParams(vmem_limit_bytes=16 * MIB),
        name="prepare",
    )(*(in_hbm(x) for x in (rho, flow, heat)))


def donate_kernel(n_lat, n_lon, rows, cols, field_rows, *refs):
    weights = refs[:n_lat]
    cells = refs[n_lat]
    replies = refs[n_lat + 1 : 2 * n_lat + 1]
    corners, turned, gathered, whole_box, requests, sems = refs[2 * n_lat + 1 :]
    slots = weights[0].shape[1]
    lat_len, lon_len = 2 * cols, 2 * rows
    for distance in range(n_lat):
        for row in range(2):
            for tile in range(slots // LANES):
                lanes = slice(tile * LANES, (tile + 1) * LANES)
                whole_box[distance, row, tile : tile + 1] = weights[distance][
                    row : row + 1, lanes
                ].astype(jnp.int32)
    copy = pltpu.make_async_copy(whole_box, requests, sems.at[0])
    copy.start()
    for distance in range(n_lat):
        for at in range(lat_len, slots, LANES):
            turned[distance, at : at + LANES, 0:SUB] = weights[distance][:, at : at + LANES].T
        asker = jnp.bitwise_xor(lax.axis_index("lat"), distance)

        @pl.when((asker == 0) | (asker == n_lat - 1))
        def _(distance=distance):
            for at in range(0, lat_len, LANES):
                turned[distance, at : at + LANES, 0:SUB] = weights[distance][:, at : at + LANES].T

    copy.wait()
    lat_len, lon_len = 2 * cols, 2 * rows
    run_lat, run_lon = lat_len // n_lat, lon_len // n_lat
    tiles = cols // LANES
    width = window_of(run_lat, cols)
    lat_here = lax.axis_index("lat")
    lon_here = lax.axis_index("lon")

    def word(request, row, slot):
        return requests[request, row, lax.shift_right_logical(slot, 7), jnp.bitwise_and(slot, 127)]

    def find_run(request, start, run):
        start = jnp.int32(start)
        found = jnp.int32(0)
        for r in range(1, n_lat):
            match = word(request, 0, start + r * run) == lat_here
            found = jnp.where(match, jnp.int32(r), found)
        return found

    def gather(request, first, count):
        def step(i, carry):
            for u in range(SUB):
                t = i * SUB + u
                cell = word(request, 1, first + t)
                for j, shift in enumerate((0, cols, 1, cols + 1)):
                    corners[j, pl.ds(t, 1), :] = cells[pl.ds(cell + shift, 1), :]
            return carry

        lax.fori_loop(0, count // SUB, step, 0)

    def blend(distance, first, count):
        rows_here = pl.ds(pl.multiple_of(first, SUB), count)
        total = None
        for j in range(4):
            weight = jnp.broadcast_to(turned[distance, rows_here, 2 + j : 3 + j], (count, LANES))
            part = weight * corners[j, 0:count, :]
            total = part if total is None else total + part
        return total

    for distance in range(n_lat):
        request, reply = distance, replies[distance]
        asker = jnp.bitwise_xor(lat_here, distance)

        @pl.when((asker == 0) | (asker == n_lat - 1))
        def _(distance=distance, request=request, reply=reply):
            run = find_run(request, 0, run_lat)
            start = lax.rem(run * run_lat, cols)
            base = jnp.minimum(lax.div(start, LANES), tiles - width)
            offset = pl.multiple_of(start - base * LANES, SUB)
            gather(request, run * run_lat, run_lat)
            gathered[pl.ds(offset, run_lat), :] = blend(distance, run * run_lat, run_lat)
            for tile in range(width):
                block = gathered[tile * LANES : (tile + 1) * LANES, :]
                reply[0:field_rows, tile * LANES : (tile + 1) * LANES] = block.T[0:field_rows]

        @pl.when((lon_here == 0) | (lon_here == n_lon - 1))
        def _(distance=distance, request=request, reply=reply):
            first = lat_len + jnp.where(lon_here == 0, 0, lon_len)
            run = find_run(request, first, run_lon)
            gather(request, first + run * run_lon, run_lon)
            reply[field_rows : field_rows + run_lon, 0:LANES] = blend(
                distance, first + run * run_lon, run_lon
            )


def donate(requests, cells, rows, cols, field_rows):
    n_lat, n_lon = lax.axis_size("lat"), lax.axis_size("lon")
    run_lat = 2 * cols // n_lat
    width = window_of(run_lat, cols)
    slots = requests[0].shape[1]
    words = (pl.cdiv(slots, SUB * LANES) * SUB, LANES)
    reply = jax.ShapeDtypeStruct((field_rows + 2 * rows // n_lat, width * LANES), jnp.float32)
    return pl.pallas_call(
        functools.partial(donate_kernel, n_lat, n_lon, rows, cols, field_rows),
        out_shape=(reply,) * n_lat,
        in_specs=[VMEM] * (n_lat + 1),
        out_specs=(VMEM,) * n_lat,
        scratch_shapes=[
            pltpu.VMEM((4, max(run_lat, 2 * rows // n_lat), LANES), jnp.float32),
            pltpu.VMEM((n_lat, slots, LANES), jnp.float32),
            pltpu.VMEM((width * LANES, LANES), jnp.float32),
            pltpu.VMEM((n_lat, 2) + words, jnp.int32),
            pltpu.SMEM((n_lat, 2) + words, jnp.int32),
            pltpu.SemaphoreType.DMA((1,)),
        ],
        compiler_params=pltpu.CompilerParams(vmem_limit_bytes=9 * MIB),
        name="donate",
    )(*requests, cells)


def core_parts(rows, tiles):
    return (SUB, rows - 2 * SUB, LANES, (tiles - 2) * LANES)


def edge_parts(rows, tiles):
    cols = tiles * LANES
    return (
        (0, SUB, 0, cols),
        (rows - SUB, SUB, 0, cols),
        (SUB, rows - 2 * SUB, 0, LANES),
        (SUB, rows - 2 * SUB, cols - LANES, LANES),
    )


def part_copies(boxes, outs, part, span, sems):
    first, count, lane, lanes = part
    at = (span, pl.ds(first, count), pl.ds(lane, lanes))
    return [
        pltpu.make_async_copy(box.at[(slice(None),) + at], out.at[(0, slice(None)) + at], sems.at[n])
        for n, (box, out) in enumerate(zip(boxes, outs))
    ]


def stencil_kernel(
    geometry, chunk, block, row_box, spin_box, outset, rate_out, state_out, rate_box, state_box, sems
):
    n_lat, n_lon, levels, rows, cols = geometry
    tiles = cols // LANES
    step_lat = math.pi / 2.0 / (rows * n_lat)
    step_lon = 1.5 * math.pi / (cols * n_lon)
    chunks = levels // chunk
    by_lat = 1.0 / (12.0 * step_lat)
    by_lon = 1.0 / (12.0 * step_lon)
    lane8 = lax.broadcasted_iota(jnp.int32, (SUB, LANES), 1)

    def out_copies(c):
        return part_copies(
            (rate_box, state_box),
            (rate_out, state_out),
            core_parts(rows, tiles),
            pl.ds(c * chunk, chunk),
            sems.at[c],
        )

    def one_level(k):
        below = jnp.maximum(k - 1, 0)
        above = jnp.minimum(k + 1, levels - 1)
        radius = jnp.broadcast_to(1.0 / step_lat + k.astype(jnp.float32), (SUB, LANES))
        inv_radius = 1.0 / radius
        for top in range(SUB, rows - SUB, SUB):
            one_strip(k, below, above, inv_radius, inv_radius * by_lat, top)

    def one_strip(k, below, above, inv_radius, lat_scale, top):
        strip = slice(top, top + SUB)
        inv_sin, cot = row_box[0, strip], row_box[1, strip]
        inv_arc = inv_radius * inv_sin
        lon_scale = inv_arc * by_lon
        cot_r = cot * inv_radius
        two_r = 2.0 * inv_radius
        curve_lat = (VISCOSITY / (12.0 * step_lat * step_lat)) * inv_radius * inv_radius
        curve_lon = (VISCOSITY / (12.0 * step_lon * step_lon)) * inv_arc * inv_arc
        slope_extra = (VISCOSITY * by_lat) * inv_radius * cot_r
        radial_extra = VISCOSITY * inv_radius
        center_weight = 2.0 * VISCOSITY + 30.0 * (curve_lat + curve_lon)

        def derive(f, full):
            here = [block[f, t, k, SUB + top : 2 * SUB + top] for t in range(tiles)]
            w1s = [pltpu.roll(x, 1, 1) for x in here]
            w2s = [pltpu.roll(x, 2, 1) for x in here]
            e1s = [pltpu.roll(x, LANES - 1, 1) for x in here]
            e2s = [pltpu.roll(x, LANES - 2, 1) for x in here]
            out = []
            for t in range(tiles):
                at = SUB + top
                n1, n2 = block[f, t, k, at - 1 : at + 7], block[f, t, k, at - 2 : at + 6]
                s1, s2 = block[f, t, k, at + 1 : at + 9], block[f, t, k, at + 2 : at + 10]
                w1 = jnp.where(lane8 == 0, w1s[t - 1] if t else 0.0, w1s[t])
                w2 = jnp.where(lane8 < 2, w2s[t - 1] if t else 0.0, w2s[t])
                last = t == tiles - 1
                e1 = jnp.where(lane8 == LANES - 1, 0.0 if last else e1s[t + 1], e1s[t])
                e2 = jnp.where(lane8 >= LANES - 2, 0.0 if last else e2s[t + 1], e2s[t])
                low = block[f, t, below, SUB + top : 2 * SUB + top]
                high = block[f, t, above, SUB + top : 2 * SUB + top]
                rad = high - low
                lat = 8.0 * (s1 - n1) - (s2 - n2)
                lon = 8.0 * (e1 - w1) - (e2 - w2)
                bend = None
                if full:
                    bend = (
                        VISCOSITY * (high + low)
                        + curve_lat * (16.0 * (s1 + n1) - (s2 + n2))
                        + curve_lon * (16.0 * (e1 + w1) - (e2 + w2))
                        - center_weight * here[t]
                    )
                out.append((rad, lat, lon, bend))
            return here, out

        wind_rad = [block[1, t, k, SUB + top : 2 * SUB + top] for t in range(tiles)]
        wind_lat = [block[2, t, k, SUB + top : 2 * SUB + top] for t in range(tiles)]
        wind_lon = [block[3, t, k, SUB + top : 2 * SUB + top] for t in range(tiles)]
        go_rad = [0.5 * x for x in wind_rad]
        go_lat = [lat_scale * x for x in wind_lat]
        go_lon = [lon_scale * x for x in wind_lon]

        def put(f, t, center, rate):
            lanes = slice(t * LANES, (t + 1) * LANES)
            rate_box[f, k, strip, lanes] = rate
            state_box[f, k, strip, lanes] = (
                0.75 * outset[0, f, k, strip, lanes] + 0.25 * center
            ) + (0.25 * TIME_STEP) * rate

        rho_here, rho_d = derive(0, False)
        heat_here, heat_d = derive(4, True)
        ratio = [heat_here[t] / rho_here[t] for t in range(tiles)]
        press, rho_rate, heat_rate = [], [], []
        for t in range(tiles):
            (a, b, c, _), (d, e, g, bend) = rho_d[t], heat_d[t]
            press.append(
                (
                    0.5 * (ratio[t] * a + d),
                    lat_scale * (ratio[t] * b + e),
                    lon_scale * (ratio[t] * c + g),
                )
            )
            rho_rate.append(go_rad[t] * a + go_lat[t] * b + go_lon[t] * c)
            heat_rate.append(
                bend
                + (radial_extra - go_rad[t]) * d
                + (slope_extra - go_lat[t]) * e
                - go_lon[t] * g
            )
        diverge = [two_r * wind_rad[t] + cot_r * wind_lat[t] for t in range(tiles)]
        for f in (1, 2, 3):
            here, d_all = derive(f, True)
            for t in range(tiles):
                d, e, g, bend = d_all[t]
                spin_rad, spin_lat = spin_box[0, t, strip], spin_box[1, t, strip]
                spin_lon = spin_box[2, t, strip]
                rate = (
                    bend
                    + (radial_extra - go_rad[t]) * d
                    + (slope_extra - go_lat[t]) * e
                    - go_lon[t] * g
                    - press[t][f - 1]
                )
                if f == 1:
                    diverge[t] += 0.5 * d
                    rate += inv_radius * (wind_lat[t] * wind_lat[t] + wind_lon[t] * wind_lon[t])
                    rate += spin_lon * wind_lat[t] - spin_lat * wind_lon[t] - GRAVITY
                elif f == 2:
                    diverge[t] += lat_scale * e
                    rate += cot_r * (wind_lon[t] * wind_lon[t])
                    rate -= inv_radius * (wind_rad[t] * wind_lat[t])
                    rate += spin_rad * wind_lon[t] - spin_lon * wind_rad[t]
                else:
                    diverge[t] += lon_scale * g
                    rate -= (inv_radius * wind_rad[t] + cot_r * wind_lat[t]) * wind_lon[t]
                    rate += spin_lat * wind_rad[t] - spin_rad * wind_lat[t]
                put(f, t, here[t], rate)
        for t in range(tiles):
            put(0, t, rho_here[t], -rho_rate[t] - rho_here[t] * diverge[t])
            put(
                4,
                t,
                heat_here[t],
                heat_rate[t] - (GAMMA - 1.0) * (heat_here[t] * diverge[t]),
            )

    for c in range(chunks):

        @pl.loop(c * chunk, (c + 1) * chunk)
        def _(k):
            one_level(k)

        for copy in out_copies(c):
            copy.start()
    for c in range(chunks):
        for copy in out_copies(c):
            copy.wait()


def stencil(block, row_box, spin_box, outset):
    levels, rows, cols = outset.shape[2:]
    n_lat, n_lon = lax.axis_size("lat"), lax.axis_size("lon")
    chunk = 8
    out = jax.ShapeDtypeStruct(outset.shape, jnp.float32)
    box = jax.ShapeDtypeStruct(outset.shape[1:], jnp.float32)
    return pl.pallas_call(
        functools.partial(stencil_kernel, (n_lat, n_lon, levels, rows, cols), chunk),
        out_shape=(out, out, box, box),
        in_specs=[VMEM] * 4,
        out_specs=(ANY, ANY, VMEM, VMEM),
        scratch_shapes=[pltpu.SemaphoreType.DMA((levels // chunk, 2))],
        compiler_params=pltpu.CompilerParams(vmem_limit_bytes=20 * MIB),
        cost_estimate=pl.CostEstimate(
            flops=125 * levels * rows * cols,
            bytes_accessed=80 * levels * rows * cols,
            transcendentals=0,
        ),
        name="stencil",
    )(block, row_box, spin_box, outset)


def edges_kernel(geometry, chunk, *refs):
    n_lat, n_lon, levels, rows, cols = geometry
    tiles = cols // LANES
    field_rows = 5 * levels
    partners, turning = refs[:2]
    reply_box = refs[2 : 2 + n_lat]
    (
        lon_even,
        lon_odd,
        lat_even,
        lat_odd,
        block,
        row_box,
        spin_box,
        outset,
        rate_in,
        state_in,
        _,
        _,
        rate_out,
        state_out,
        rate_box,
        state_box,
        replies,
        halo,
        side,
        mixed,
        sems,
    ) = refs[2 + n_lat :]
    lat_here = lax.axis_index("lat")
    lon_here = lax.axis_index("lon")
    lat_len, lon_len = 2 * cols, 2 * rows
    run_lat, run_lon = lat_len // n_lat, lon_len // n_lat
    width = window_of(run_lat, cols)
    step_lat = math.pi / 2.0 / (rows * n_lat)
    step_lon = 1.5 * math.pi / (cols * n_lon)
    by_lat = 1.0 / (12.0 * step_lat)
    by_lon = 1.0 / (12.0 * step_lon)
    chunks = levels // chunk
    parts = edge_parts(rows, tiles)

    def out_copies(c):
        out = []
        for n, part in enumerate(parts):
            out += part_copies(
                (rate_box, state_box),
                (rate_out, state_out),
                part,
                pl.ds(c * chunk, chunk),
                sems.at[c, n],
            )
        return out

    lat_is_even = lax.rem(lat_here, 2) == 0
    lon_is_even = lax.rem(lon_here, 2) == 0
    for even, north, south in ((True, lat_odd, lat_even), (False, lat_even, lat_odd)):

        @pl.when(lat_is_even == even)
        def _(north=north, south=south):
            halo[0] = north[...]
            halo[1] = south[...]

    for even, west, east in ((True, lon_odd, lon_even), (False, lon_even, lon_odd)):

        @pl.when(lon_is_even == even)
        def _(west=west, east=east):
            side[0] = west[...]
            side[1] = east[...]

    @pl.when((lat_here == 0) | (lat_here == n_lat - 1) | (lon_here == 0) | (lon_here == n_lon - 1))
    def _():
        for d in range(n_lat):
            replies[d] = reply_box[d][...]

    lane8 = lax.broadcasted_iota(jnp.int32, (SUB, LANES), 1)
    sub8 = lax.broadcasted_iota(jnp.int32, (SUB, LANES), 0)

    for which, slot0 in ((0, 0), (1, lat_len)):

        @pl.when(lat_here == (0 if which == 0 else n_lat - 1))
        def _(which=which, slot0=slot0):
            sources = [
                jnp.bitwise_xor(partners[0, 0, 0, slot0 + r * run_lat], lat_here) for r in range(n_lat)
            ]
            for layer in range(2):
                for t in range(tiles):
                    lane = lax.broadcasted_iota(jnp.int32, (field_rows, LANES), 1) + t * LANES
                    value = None
                    for r in range(n_lat):
                        first = r * run_lat - layer * cols
                        if first < 0 or first >= cols:
                            continue
                        if first >= (t + 1) * LANES or first + run_lat <= t * LANES:
                            continue
                        base = min(first // LANES, tiles - width)
                        here = (t - base) * LANES
                        piece = replies[sources[r], 0:field_rows, here : here + LANES]
                        value = piece if value is None else jnp.where(lane >= first, piece, value)
                    spot = slot0 + layer * cols + t * LANES
                    cosine = turning[0, 0, 0, 0:1, spot : spot + LANES]
                    sine = turning[0, 0, 0, 1:2, spot : spot + LANES]
                    parts = [value[f * levels : (f + 1) * levels] for f in range(5)]
                    parts[2], parts[3] = (
                        cosine * parts[2] + sine * parts[3],
                        cosine * parts[3] - sine * parts[2],
                    )
                    for f in range(5):
                        halo[which, layer, f, t] = parts[f]

    turn_lon = jnp.concatenate(
        [turning[0, 0, 0, :, 2 * lat_len :], jnp.zeros((SUB - 2, 2 * lon_len), jnp.float32)], axis=0
    ).T

    for which, slot0 in ((0, 2 * lat_len), (1, 2 * lat_len + lon_len)):
        @pl.when(lon_here == (0 if which == 0 else n_lon - 1))
        def _(which=which, slot0=slot0):
            lane = lax.broadcasted_iota(jnp.int32, (run_lon, LANES), 1)
            is_lat = (lane >= 2 * levels) & (lane < 3 * levels)
            is_lon = (lane >= 3 * levels) & (lane < 4 * levels)
            for r in range(n_lat):
                source = jnp.bitwise_xor(partners[0, 0, 0, slot0 + r * run_lon], lat_here)
                layer, first = r * run_lon // rows, r * run_lon % rows
                value = replies[source, field_rows : field_rows + run_lon, 0:LANES]
                slots = slice(which * lon_len + r * run_lon, which * lon_len + (r + 1) * run_lon)
                cosine = jnp.broadcast_to(turn_lon[slots, 0:1], (run_lon, LANES))
                sine = jnp.broadcast_to(turn_lon[slots, 1:2], (run_lon, LANES))
                later = pltpu.roll(value, LANES - levels, 1)
                earlier = pltpu.roll(value, levels, 1)
                value = jnp.where(
                    is_lat,
                    cosine * value + sine * later,
                    jnp.where(is_lon, cosine * value - sine * earlier, value),
                )
                side[which, layer, first : first + run_lon] = value

    lane_all = lax.broadcasted_iota(jnp.int32, (rows, LANES), 1)
    columns = [side[1, 0], side[1, 1], side[0, 0], side[0, 1]]
    columns = [columns[0]] + [pltpu.roll(columns[j], j, 1) for j in range(1, 4)]
    for q in range(4):
        pick = jnp.bitwise_and(lane_all - q, 3)
        value = columns[0]
        for j in range(1, 4):
            value = jnp.where(pick == j, columns[j], value)
        for row in range(q, field_rows, 4):
            mixed[row // levels, row % levels] = pltpu.roll(value, LANES - 2 - row, 1)

    def one_level(k):
        below = jnp.maximum(k - 1, 0)
        above = jnp.minimum(k + 1, levels - 1)
        radius = jnp.broadcast_to(1.0 / step_lat + k.astype(jnp.float32), (SUB, LANES))
        inv_radius = 1.0 / radius
        for top in range(0, rows, SUB):
            if top in (0, rows - SUB):
                one_strip(k, below, above, inv_radius, inv_radius * by_lat, top)
            else:
                for t in (0, tiles - 1):
                    one_tile(k, inv_radius, top, t)

    def one_strip(k, below, above, inv_radius, lat_scale, top):
        strip = slice(top, top + SUB)
        inv_sin, cot = row_box[0, strip], row_box[1, strip]
        inv_arc = inv_radius * inv_sin
        lon_scale = inv_arc * by_lon
        cot_r = cot * inv_radius
        two_r = 2.0 * inv_radius
        curve_lat = (VISCOSITY / (12.0 * step_lat * step_lat)) * inv_radius * inv_radius
        curve_lon = (VISCOSITY / (12.0 * step_lon * step_lon)) * inv_arc * inv_arc
        slope_extra = (VISCOSITY * by_lat) * inv_radius * cot_r
        radial_extra = VISCOSITY * inv_radius
        center_weight = 2.0 * VISCOSITY + 30.0 * (curve_lat + curve_lon)
        north, south = top == 0, top == rows - SUB

        def derive(f, full):
            here = [block[f, t, k, SUB + top : 2 * SUB + top] for t in range(tiles)]
            ghost = mixed[f, k, strip]
            ghost_w, ghost_e = pltpu.roll(ghost, LANES - 1, 1), pltpu.roll(ghost, 1, 1)
            w1s = [pltpu.roll(x, 1, 1) for x in here]
            w2s = [pltpu.roll(x, 2, 1) for x in here]
            e1s = [pltpu.roll(x, LANES - 1, 1) for x in here]
            e2s = [pltpu.roll(x, LANES - 2, 1) for x in here]
            out = []
            for t in range(tiles):
                at = SUB + top
                n1, n2 = block[f, t, k, at - 1 : at + 7], block[f, t, k, at - 2 : at + 6]
                s1, s2 = block[f, t, k, at + 1 : at + 9], block[f, t, k, at + 2 : at + 10]
                if north:
                    g2 = jnp.broadcast_to(halo[0, 0, f, t, pl.ds(k, 1), :], (SUB, LANES))
                    g1 = jnp.broadcast_to(halo[0, 1, f, t, pl.ds(k, 1), :], (SUB, LANES))
                    n1 = jnp.where(sub8 == 0, g1, n1)
                    n2 = jnp.where(sub8 == 0, g2, jnp.where(sub8 == 1, g1, n2))
                if south:
                    g1 = jnp.broadcast_to(halo[1, 0, f, t, pl.ds(k, 1), :], (SUB, LANES))
                    g2 = jnp.broadcast_to(halo[1, 1, f, t, pl.ds(k, 1), :], (SUB, LANES))
                    s1 = jnp.where(sub8 == SUB - 1, g1, s1)
                    s2 = jnp.where(sub8 == SUB - 1, g2, jnp.where(sub8 == SUB - 2, g1, s2))
                w1 = jnp.where(lane8 == 0, w1s[t - 1] if t else ghost_w, w1s[t])
                w2 = jnp.where(lane8 < 2, w2s[t - 1] if t else ghost, w2s[t])
                last = t == tiles - 1
                e1 = jnp.where(lane8 == LANES - 1, ghost_e if last else e1s[t + 1], e1s[t])
                e2 = jnp.where(lane8 >= LANES - 2, ghost if last else e2s[t + 1], e2s[t])
                low = block[f, t, below, SUB + top : 2 * SUB + top]
                high = block[f, t, above, SUB + top : 2 * SUB + top]
                rad = high - low
                lat = 8.0 * (s1 - n1) - (s2 - n2)
                lon = 8.0 * (e1 - w1) - (e2 - w2)
                bend = None
                if full:
                    bend = (
                        VISCOSITY * (high + low)
                        + curve_lat * (16.0 * (s1 + n1) - (s2 + n2))
                        + curve_lon * (16.0 * (e1 + w1) - (e2 + w2))
                        - center_weight * here[t]
                    )
                out.append((rad, lat, lon, bend))
            return here, out

        wind_rad = [block[1, t, k, SUB + top : 2 * SUB + top] for t in range(tiles)]
        wind_lat = [block[2, t, k, SUB + top : 2 * SUB + top] for t in range(tiles)]
        wind_lon = [block[3, t, k, SUB + top : 2 * SUB + top] for t in range(tiles)]
        go_rad = [0.5 * x for x in wind_rad]
        go_lat = [lat_scale * x for x in wind_lat]
        go_lon = [lon_scale * x for x in wind_lon]

        def put(f, t, center, rate):
            lanes = slice(t * LANES, (t + 1) * LANES)
            rate_box[f, k, strip, lanes] = rate
            state_box[f, k, strip, lanes] = (
                0.75 * outset[0, f, k, strip, lanes] + 0.25 * center
            ) + (0.25 * TIME_STEP) * rate

        rho_here, rho_d = derive(0, False)
        heat_here, heat_d = derive(4, True)
        ratio = [heat_here[t] / rho_here[t] for t in range(tiles)]
        press, rho_rate, heat_rate = [], [], []
        for t in range(tiles):
            (a, b, c, _), (d, e, g, bend) = rho_d[t], heat_d[t]
            press.append(
                (
                    0.5 * (ratio[t] * a + d),
                    lat_scale * (ratio[t] * b + e),
                    lon_scale * (ratio[t] * c + g),
                )
            )
            rho_rate.append(go_rad[t] * a + go_lat[t] * b + go_lon[t] * c)
            heat_rate.append(
                bend
                + (radial_extra - go_rad[t]) * d
                + (slope_extra - go_lat[t]) * e
                - go_lon[t] * g
            )
        diverge = [two_r * wind_rad[t] + cot_r * wind_lat[t] for t in range(tiles)]
        for f in (1, 2, 3):
            here, d_all = derive(f, True)
            for t in range(tiles):
                d, e, g, bend = d_all[t]
                spin_rad, spin_lat = spin_box[0, t, strip], spin_box[1, t, strip]
                spin_lon = spin_box[2, t, strip]
                rate = (
                    bend
                    + (radial_extra - go_rad[t]) * d
                    + (slope_extra - go_lat[t]) * e
                    - go_lon[t] * g
                    - press[t][f - 1]
                )
                if f == 1:
                    diverge[t] += 0.5 * d
                    rate += inv_radius * (wind_lat[t] * wind_lat[t] + wind_lon[t] * wind_lon[t])
                    rate += spin_lon * wind_lat[t] - spin_lat * wind_lon[t] - GRAVITY
                elif f == 2:
                    diverge[t] += lat_scale * e
                    rate += cot_r * (wind_lon[t] * wind_lon[t])
                    rate -= inv_radius * (wind_rad[t] * wind_lat[t])
                    rate += spin_rad * wind_lon[t] - spin_lon * wind_rad[t]
                else:
                    diverge[t] += lon_scale * g
                    rate -= (inv_radius * wind_rad[t] + cot_r * wind_lat[t]) * wind_lon[t]
                    rate += spin_lat * wind_rad[t] - spin_rad * wind_lat[t]
                put(f, t, here[t], rate)
        for t in range(tiles):
            put(0, t, rho_here[t], -rho_rate[t] - rho_here[t] * diverge[t])
            put(
                4,
                t,
                heat_here[t],
                heat_rate[t] - (GAMMA - 1.0) * (heat_here[t] * diverge[t]),
            )

    def one_tile(k, inv_radius, top, t):
        strip, lanes = slice(top, top + SUB), slice(t * LANES, (t + 1) * LANES)
        inv_arc = inv_radius * row_box[0, strip]
        lon_scale = inv_arc * by_lon
        curve_lon = (VISCOSITY / (12.0 * step_lon * step_lon)) * inv_arc * inv_arc
        rho, _, _, wind_lon, heat = (
            block[f, t, k, SUB + top : 2 * SUB + top] for f in range(5)
        )
        go_lon = lon_scale * wind_lon
        ratio = heat / rho

        def add(total, value):
            return value if total is None else total + value

        lon_d, lon_b = ([None] * 5 for _ in range(2))
        for f in range(5):
            ghost = mixed[f, k, strip]
            if t == 0:
                second = jnp.where(lane8 < 2, ghost, 0.0)
                near = 8.0 * jnp.where(lane8 == 0, pltpu.roll(ghost, LANES - 1, 1), 0.0)
                lon_d[f] = add(lon_d[f], second - near)
                lon_b[f] = add(lon_b[f], 2.0 * near - second)
            if t == tiles - 1:
                second = jnp.where(lane8 >= LANES - 2, ghost, 0.0)
                near = 8.0 * jnp.where(lane8 == LANES - 1, pltpu.roll(ghost, 1, 1), 0.0)
                lon_d[f] = add(lon_d[f], near - second)
                lon_b[f] = add(lon_b[f], 2.0 * near - second)

        rates = [None] * 5
        diverge = None
        if lon_d[0] is not None:
            diverge = add(diverge, lon_scale * lon_d[3])
            rates[0] = add(rates[0], -go_lon * lon_d[0])
            for f in range(1, 5):
                rates[f] = add(rates[f], curve_lon * lon_b[f] - go_lon * lon_d[f])
            rates[3] -= lon_scale * (ratio * lon_d[0] + lon_d[4])
        rates[0] -= rho * diverge
        rates[4] -= (GAMMA - 1.0) * (heat * diverge)
        for f in range(5):
            rate_box[f, k, strip, lanes] = rate_in[f, k, strip, lanes] + rates[f]
            state_box[f, k, strip, lanes] = (
                state_in[f, k, strip, lanes] + (0.25 * TIME_STEP) * rates[f]
            )

    for c in range(chunks):

        @pl.loop(c * chunk, (c + 1) * chunk)
        def _(k):
            one_level(k)

        for copy in out_copies(c):
            copy.start()
    for c in range(chunks):
        for copy in out_copies(c):
            copy.wait()


def edges(
    partners, turning, replies, sides, halos, block, row_box, spin_box, outset, inner
):
    rate_out, state_out, rate_box, state_box = inner
    levels, rows, cols = rate_box.shape[1:]
    n_lat, n_lon = lax.axis_size("lat"), lax.axis_size("lon")
    chunk = 4
    out = jax.ShapeDtypeStruct(rate_out.shape, jnp.float32)
    box = pltpu.VMEM(rate_box.shape, jnp.float32)
    n_in = n_lat + 12
    return pl.pallas_call(
        functools.partial(edges_kernel, (n_lat, n_lon, levels, rows, cols), chunk),
        out_shape=(out, out),
        in_specs=[SMEM] + [VMEM] * (n_in - 1) + [ANY] * 2,
        out_specs=(ANY, ANY),
        input_output_aliases={n_in: 0, n_in + 1: 1},
        scratch_shapes=[
            box,
            box,
            pltpu.VMEM((n_lat,) + replies[0].shape, jnp.float32),
            pltpu.VMEM((2,) + halos[0].shape, jnp.float32),
            pltpu.VMEM((2, 2, rows, LANES), jnp.float32),
            pltpu.VMEM((5, levels, rows, LANES), jnp.float32),
            pltpu.SemaphoreType.DMA((levels // chunk, 4, 2)),
        ],
        compiler_params=pltpu.CompilerParams(vmem_limit_bytes=20 * MIB),
        cost_estimate=pl.CostEstimate(
            flops=150 * levels * rows * cols,
            bytes_accessed=40 * levels * rows * cols,
            transcendentals=0,
        ),
        name="edges",
    )(
        partners,
        turning,
        *replies,
        *sides,
        *halos,
        block,
        row_box,
        spin_box,
        outset,
        rate_box,
        state_box,
        rate_out,
        state_out,
    )


def shards(rho, flow, heat, outset, opposite_block, donor_lower_corner, blend, turning):
    levels, rows, cols = rho.shape[1:]
    n_lat = lax.axis_size("lat")
    request = ask(opposite_block, donor_lower_corner, blend, rows, cols)
    requests = [swap_panels(request, d) for d in range(n_lat)]
    cells, block, even_rows, odd_rows, even_cols, odd_cols, row_box, spin_box = prepare(
        rho, flow, heat
    )
    *requests, even_rows, odd_rows, even_cols, odd_cols = lax.optimization_barrier(
        (*requests, even_rows, odd_rows, even_cols, odd_cols)
    )
    sides = (swap_pairs(even_cols, "lon", False), swap_pairs(odd_cols, "lon", True))
    halos = (swap_pairs(even_rows, "lat", False), swap_pairs(odd_rows, "lat", True))
    replies = donate(requests, cells, rows, cols, 5 * levels)
    *replies, spin_box = lax.optimization_barrier((*replies, spin_box))
    *sides, spin_box = lax.optimization_barrier((*sides, spin_box))
    replies = [swap_panels(reply, d) for d, reply in enumerate(replies)]
    inner = stencil(block, row_box, spin_box, outset)
    return edges(opposite_block, turning, replies, sides, halos, block, row_box, spin_box, outset, inner)


def solution(mesh):
    in_specs = (
        P("panel", None, "lat", "lon"),
        P("panel", None, None, "lat", "lon"),
        P("panel", None, "lat", "lon"),
        P("panel", None, None, "lat", "lon"),
        P("panel", "lat", "lon", None),
        P("panel", "lat", "lon", None),
        P("panel", "lat", "lon", None, None),
        P("panel", "lat", "lon", None, None),
    )
    out_specs = (P("panel", None, None, "lat", "lon"), P("panel", None, None, "lat", "lon"))
    return jax.shard_map(shards, mesh=mesh, in_specs=in_specs, out_specs=out_specs, check_vma=False)
```
